32 devices in a mesh: groups: 2 (over x), head: 4 (over y, core), req: 4 (over z).
Axes of the slice: x: 2, y: 2, z: 4, core: 2. Of those that a mesh axis runs over, the one named last changes fastest.
Arguments:
- ssm_input: bfloat16 [16, 64, 4096], P(None, ('groups', 'req'), 'head'), parts along dimension 1, may hold values from -6 to 6
- write_vec: bfloat16 [16, 64, 128], P('head', ('groups', 'req')), parts along dimension 1, may hold values from -6 to 6
- read_vec: bfloat16 [16, 64, 128], P('head', ('groups', 'req')), parts along dimension 1, may hold values from -0.5 to 0.5
- step_raw: float32 [16, 64, 64], P(None, ('groups', 'req'), 'head'), parts along dimension 1, may hold values from -4 to 4
- step_bias: float32 [64], P('head'), may hold values from -3 to -0.5
- decay_rate: float32 [64], P('head'), may hold values from 1 to 16
- skip_gain: float32 [64], P('head'), may hold values from 0.5 to 1.5
- cache_state: bfloat16 [64, 64, 64, 128], P(('groups', 'req'), 'head'), parts along dimension 0, may hold values from -6 to 6
- parents: int32 [64, 16], P(('groups', 'req')), parts along dimension 0, may hold values from -1 to 14, as said below
- out_proj: bfloat16 [4096, 4096], P('head'), may hold values from -0.09375 to 0.09375
- residual: bfloat16 [16, 64, 4096], P('head', ('groups', 'req')), parts along dimension 1, may hold values from -6 to 6
- norm_gain: float32 [4096], replicated, may hold values from 0.1 to 1.9
- router: bfloat16 [4096, 64], replicated, may hold values from -0.09375 to 0.09375
- expert_ids: int32 [16, 64, 10], P('head', ('groups', 'req')), parts along dimension 1, may hold values from 0 to 63, as said below
- gate_proj: bfloat16 [128, 4096, 384], P(('head', 'req')), may hold values from -0.09375 to 0.09375
- up_proj: bfloat16 [128, 4096, 384], P(('head', 'req')), may hold values from -0.09375 to 0.09375
- down_proj: bfloat16 [128, 384, 4096], P(('head', 'req')), may hold values from -0.21875 to 0.21875
Outputs:
- layer_out: bfloat16 [16, 64, 4096], P('head', ('groups', 'req')), parts along dimension 1
The draws below stay inside these ranges and needn't reach their ends.
There are 2 independent parts, one for each index of `groups`. The reference program is written for one: setup_inputs(seed, part) draws one part's arguments, and reference() takes and returns one part's arrays. A program takes and returns all parts, laid end to end along the dimension named above; an argument that names none is the same for every part. Nothing has to cross between parts.
Inputs may be any that keep to these rules, and one draw needn't show every extreme that they name: parents[r, 0] = -1 (the root); for j >= 1, parents[r, j] lies in 0 to j - 1; the last node's parent is node 14. `expert_ids`: each row names 10 different experts. Within the rows of one device (an aligned block of the 4 node index or indices and 8 requests held there) every expert is named by 4 or by 8 rows, 16 experts by 8; one expert is named by 8 rows in every such block.
All inputs are finite; a program needn't handle non-finite values.
Results may differ from the reference program's by a relative error of at most 0.0058.
Values may be sent and summed in bfloat16 or wider, within the bound.
No kernel may reach another device: no remote copies, remote signals or barrier semaphores. Data moves between devices by JAX's collectives and lax.ppermute only.
A program may use at most 192 MiB of HBM per device.

```python
import math
import jax
import jax.numpy as jnp
from jax import lax

D = 4096
NH = 64
P_SIZE = 64
N = 128
NODES = 16
TOPK = 10
EXPERTS = 64
FFE = 768
REQ_DEV = 8
REQS = 32
HALF = 384
NPD = 4
CAP = 8
N_HEAD = 4
N_REQ = 4


def draw_parents(key, part):
    labels = jnp.arange(NODES, dtype=jnp.int32)
    ceiling = jnp.maximum(labels, 1)
    drawn = jax.random.randint(jax.random.fold_in(key, 7), (REQS, NODES), 0, ceiling[None, :])
    chosen = jnp.where(labels[None, :] == 0, -1, drawn)
    chosen = jnp.where(labels[None, :] == NODES - 1, NODES - 2, chosen)
    return chosen.astype(jnp.int32)


def draw_expert_ids(key, part):
    spare = EXPERTS // 4
    cycle_length = EXPERTS + spare
    node_blocks = NODES // NPD
    req_blocks = REQS // REQ_DEV
    blocks = node_blocks * req_blocks
    per_block = NPD * REQ_DEV * TOPK
    labels = jnp.arange(EXPERTS, dtype=jnp.int32)
    scores = jax.random.randint(jax.random.fold_in(key, 21), (blocks, EXPERTS), 0, 1 << 20) * EXPERTS + labels[None, :]
    orders = jnp.argsort(scores, axis=1).astype(jnp.int32)
    favored = jax.random.randint(jax.random.fold_in(key, 22), (), 0, EXPERTS).astype(jnp.int32)
    leading = orders[:, :1]
    swapped = jnp.where(orders == favored, leading, orders)
    orders = jnp.where(labels[None, :] == 0, favored, swapped)
    cycle_list = jnp.concatenate([orders, orders[:, :spare]], axis=1)
    shifts = jax.random.randint(jax.random.fold_in(key, 23), (blocks, 1), 0, cycle_length)
    positions = jnp.arange(per_block, dtype=jnp.int32)
    picks = jnp.take_along_axis(cycle_list, (positions[None, :] + shifts) % cycle_length, axis=1)
    picks = picks.reshape(node_blocks, req_blocks, NPD, REQ_DEV, TOPK).transpose(0, 2, 1, 3, 4)
    return picks.reshape(NODES, REQS, TOPK).astype(jnp.int32)


def block_scale(own_key, extent, split, smallest, high):
    def one(axis_at, shards_of):
        steps = jax.random.uniform(jax.random.fold_in(jax.random.fold_in(own_key, 6), axis_at), (shards_of,), jnp.float32, smallest / len(split), high / len(split))
        return jnp.repeat(jnp.exp(steps), extent[axis_at] // shards_of).reshape((-1,) + (1,) * (len(extent) - axis_at - 1))

    gain = one(*split[0])
    for cut in split[1:]:
        gain = gain * one(*cut)
    return gain


def gaussian(rng, dims, scale, most, cuts=(), kind=jnp.bfloat16):
    values = jax.random.normal(rng, dims, jnp.float32) * scale
    if len(cuts) > 0:
        values = block_scale(rng, dims, cuts, -0.22, 0.18) * values
    return jnp.clip(values, min=-most, max=most).astype(kind)


def setup_inputs(seed: int = 0, part: int = 0) -> dict:
    keys = jax.random.split(jax.random.key(seed), 18)
    own_keys = jax.random.split(jax.random.fold_in(keys[17], part), 18)
    ssm_input = gaussian(own_keys[0], (NODES, REQS, NH * P_SIZE), 1.0, 6.0, ((1, 4), (2, 4)))
    write_vec = gaussian(own_keys[1], (NODES, REQS, N), 1.0, 6.0, ((0, 4), (1, 4)))
    read_vec = gaussian(own_keys[2], (NODES, REQS, N), N ** -0.5, 0.5, ((0, 4), (1, 4)))
    step_raw = gaussian(own_keys[3], (NODES, REQS, NH), 1.0, 4.0, ((1, 4), (2, 4)), jnp.float32)
    step_bias = jnp.clip(-3.0 + 2.5 * jax.random.uniform(keys[4], (NH,), jnp.float32) ** block_scale(keys[4], (NH,), ((0, 4),), -0.2, 0.2), -3.0, -0.5)
    decay_rate = jnp.clip(jnp.exp(math.log(16.0) - 2.7725887 * jax.random.uniform(keys[5], (NH,), jnp.float32) ** block_scale(keys[5], (NH,), ((0, 4),), -0.2, 0.2)), 1.0, 16.0)
    skip_gain = jnp.clip(0.5 + 1.0 * jax.random.uniform(keys[6], (NH,), jnp.float32) ** block_scale(keys[6], (NH,), ((0, 4),), -0.2, 0.2), 0.5, 1.5)
    cache_state = gaussian(own_keys[7], (REQS, NH, P_SIZE, N), 1.0, 6.0, ((0, 4), (1, 4)))
    parents = draw_parents(jax.random.fold_in(jax.random.fold_in(keys[17], part), 71), part)
    out_proj = gaussian(keys[9], (NH * P_SIZE, D), (NH * P_SIZE) ** -0.5, 0.09375, ((0, 4),))
    residual = gaussian(own_keys[10], (NODES, REQS, D), 1.0, 6.0, ((0, 4), (1, 4)))
    norm_gain = jnp.clip(1.0 + 0.18 * jax.random.normal(keys[11], (D,), jnp.float32), 0.1, 1.9)
    router = gaussian(keys[12], (D, EXPERTS), D ** -0.5, 0.09375)
    expert_ids = draw_expert_ids(jax.random.fold_in(jax.random.fold_in(keys[17], part), 71), part)
    gate_proj = gaussian(keys[14], (2 * EXPERTS, D, HALF), D ** -0.5, 0.09375, ((0, 16),))
    up_proj = gaussian(keys[15], (2 * EXPERTS, D, HALF), D ** -0.5, 0.09375, ((0, 16),))
    down_proj = gaussian(keys[16], (2 * EXPERTS, HALF, D), FFE ** -0.5, 0.21875, ((0, 16),))
    return dict(ssm_input=ssm_input, write_vec=write_vec, read_vec=read_vec, step_raw=step_raw, step_bias=step_bias, decay_rate=decay_rate, skip_gain=skip_gain, cache_state=cache_state, parents=parents, out_proj=out_proj, residual=residual, norm_gain=norm_gain, router=router, expert_ids=expert_ids, gate_proj=gate_proj, up_proj=up_proj, down_proj=down_proj)


def ancestry(parents):
    nodes = parents.shape[1]
    labels = jnp.arange(nodes, dtype=jnp.int32)
    parent_hot = (parents[:, :, None] == labels[None, None, :]).astype(jnp.float32)
    identity = jnp.broadcast_to(jnp.eye(nodes, dtype=jnp.float32), parent_hot.shape)

    def extend(turn, reach):
        return identity + jnp.einsum('rjk,rki->rji', parent_hot, reach, precision=lax.Precision.HIGHEST)
    return lax.fori_loop(0, nodes, extend, identity)

def reference(ssm_input, write_vec, read_vec, step_raw, step_bias, decay_rate, skip_gain, cache_state, parents, out_proj, residual, norm_gain, router, expert_ids, gate_proj, up_proj, down_proj):
    nodes, requests, columns = ssm_input.shape
    heads = step_raw.shape[2]
    head_size = columns // heads
    inputs4 = ssm_input.reshape(nodes, requests, heads, head_size)
    step = jax.nn.softplus(step_raw + step_bias)
    rates = -step * decay_rate
    reach = ancestry(parents)
    depth = jnp.einsum('rji,irh->jrh', reach, rates, precision=lax.Precision.HIGHEST)
    affinity = jnp.einsum('jrn,irn->rji', read_vec.astype(jnp.float32), write_vec.astype(jnp.float32), precision=lax.Precision.HIGHEST)
    by_request = depth.transpose(1, 0, 2)
    spread = by_request[:, :, None, :] - by_request[:, None, :, :]
    linked = reach[:, :, :, None] > 0
    factor = jnp.where(linked, jnp.exp(jnp.where(linked, spread, 0.0)), 0.0)
    weights = (factor * affinity[:, :, :, None] * step.transpose(1, 0, 2)[:, None, :, :]).astype(jnp.bfloat16)
    tree_part = jnp.einsum('rjih,irhp->jrhp', weights.astype(jnp.float32), inputs4.astype(jnp.float32), precision=lax.Precision.HIGHEST)
    cache_part = jnp.einsum('jrn,rhpn->jrhp', read_vec.astype(jnp.float32), cache_state.astype(jnp.float32), precision=lax.Precision.HIGHEST)
    cache_part = cache_part * jnp.exp(depth)[:, :, :, None]
    ssm_out = (tree_part + cache_part + skip_gain[:, None] * inputs4.astype(jnp.float32)).astype(jnp.bfloat16)
    ssm_out = ssm_out.reshape(nodes * requests, columns)
    mixed = jnp.dot(ssm_out, out_proj, preferred_element_type=jnp.float32)
    width = out_proj.shape[1]
    after_mixer = (residual.reshape(nodes * requests, width).astype(jnp.float32) + mixed).astype(jnp.bfloat16)
    widened = after_mixer.astype(jnp.float32)
    meansq = lax.optimization_barrier(jnp.mean(widened * widened, axis=-1, keepdims=True))
    normed = (widened * lax.rsqrt(meansq + 1e-05) * norm_gain).astype(jnp.bfloat16)
    choices_flat = expert_ids.reshape(nodes * requests, TOPK)
    logits = jnp.dot(normed, router, preferred_element_type=jnp.float32)
    picked_logits = jnp.take_along_axis(logits, choices_flat, axis=1)
    powered = jnp.exp(picked_logits)
    gate = (powered / lax.optimization_barrier(jnp.sum(powered, axis=1, keepdims=True))).astype(jnp.bfloat16)
    gate_wide = gate.astype(jnp.float32)
    limit = N_HEAD * N_REQ * CAP
    token_count = nodes * requests

    def visit(total, expert):
        chosen = choices_flat == expert
        present = jnp.any(chosen, axis=1)
        share = lax.optimization_barrier(jnp.sum(jnp.where(chosen, gate_wide, 0.0), axis=1))
        order = jnp.cumsum(present.astype(jnp.int32)) - 1
        target = jnp.where(present, order, limit).astype(jnp.int32)
        owner = jnp.zeros((limit,), jnp.int32).at[target].set(jnp.arange(token_count, dtype=jnp.int32), mode='drop')
        filled = jnp.zeros((limit,), jnp.float32).at[target].set(1.0, mode='drop')
        rows = jnp.where(filled[:, None] > 0, normed[owner], jnp.zeros((), jnp.bfloat16))
        halves = []
        for side in range(2):
            index = (side * EXPERTS + expert).astype(jnp.int32)
            gate_rows = lax.dynamic_index_in_dim(gate_proj, index, 0, keepdims=False)
            up_rows = lax.dynamic_index_in_dim(up_proj, index, 0, keepdims=False)
            down_rows = lax.dynamic_index_in_dim(down_proj, index, 0, keepdims=False)
            gated = jnp.dot(rows, gate_rows, preferred_element_type=jnp.float32)
            lifted = jnp.dot(rows, up_rows, preferred_element_type=jnp.float32)
            act = (jax.nn.silu(gated) * lifted).astype(jnp.bfloat16)
            halves.append(jnp.dot(act, down_rows, preferred_element_type=jnp.float32).astype(jnp.bfloat16))
        result = (halves[0].astype(jnp.float32) + halves[1].astype(jnp.float32)).astype(jnp.bfloat16)
        fetched = result[jnp.where(present, order, 0).astype(jnp.int32)].astype(jnp.float32)
        return (total + share[:, None] * fetched, None)
    moe, _ = lax.scan(visit, jnp.zeros((token_count, width), jnp.float32), jnp.arange(EXPERTS, dtype=jnp.int32))
    layer_out = (after_mixer.astype(jnp.float32) + moe).astype(jnp.bfloat16)
    return layer_out.reshape(nodes, requests, width)
```

```python
import functools
import jax
import jax.numpy as jnp
from jax import lax
from jax.experimental import pallas as pl
from jax.experimental.pallas import tpu as pltpu
from jax.sharding import PartitionSpec as P


BF = jnp.bfloat16
F32 = jnp.float32
AXES = ("head", "req")
LANES = 128
AG_CHUNKS = 2
RS_CHUNKS = 2


def ancestry(parents):
    nodes = parents.shape[1]
    labels = jnp.arange(nodes, dtype=jnp.int32)
    power = (parents[:, :, None] == labels[None, None, :]).astype(BF)
    identity = jnp.broadcast_to(jnp.eye(nodes, dtype=F32), power.shape)
    reach = identity + power.astype(F32)
    span = 2
    while span < nodes:
        power = jnp.einsum("rjk,rki->rji", power, power, preferred_element_type=F32).astype(BF)
        reach = reach + jnp.einsum(
            "rjk,rki->rji", reach.astype(BF), power, preferred_element_type=F32
        )
        span *= 2
    return reach


class Ring:
    def __init__(self, heads, reqs):
        self.heads, self.reqs = heads, reqs
        self.cores = 2 if heads % 2 == 0 else 1
        self.ys = heads // self.cores

    def pairs(self, dy, dc, dz):
        found = []
        for y in range(self.ys):
            for c in range(self.cores):
                for z in range(self.reqs):
                    there = ((y + dy) % self.ys) * self.cores + (c + dc) % self.cores
                    found.append(
                        (
                            (y * self.cores + c) * self.reqs + z,
                            there * self.reqs + (z + dz) % self.reqs,
                        )
                    )
        return found

    def shift(self, x, dy=0, dc=0, dz=0):
        return lax.ppermute(x, AXES, self.pairs(dy, dc, dz))

    def gather_core(self, x):
        return jnp.stack([x] + [self.shift(x, dc=s) for s in range(1, self.cores)])

    def gather_y(self, x):
        return jnp.stack([x] + [self.shift(x, dy=s) for s in range(1, self.ys)])

    def gather_z(self, x):
        return jnp.stack([x] + [self.shift(x, dz=s) for s in range(1, self.reqs)])

    def scatter(self, parts, keep, axis):
        total = keep
        for s, part in enumerate(parts, 1):
            total = total + self.shift(part, **{axis: -s}).astype(F32)
        return total


def up_body(first, last, width, sel, x, wg, wu, *rest):
    rest = list(rest)
    if not first:
        gin, uin = rest.pop(0), rest.pop(0)
    if last:
        e0 = rest.pop(0)
    picked = jnp.dot(sel[0], x[...], preferred_element_type=F32)
    rows = picked[:, :width].astype(BF)
    gated = jnp.dot(rows, wg[0], preferred_element_type=F32)
    lifted = jnp.dot(rows, wu[0], preferred_element_type=F32)
    if not first:
        gated = gated + gin[0]
        lifted = lifted + uin[0]
    if not last:
        gout, uout = rest
        gout[0] = gated
        uout[0] = lifted
        return
    act_out, comb_out = rest
    extra = picked[:, width:]
    scale = extra[:, 0:1] + extra[:, 1:2] + extra[:, 2:3]
    gated = gated * scale
    lifted = lifted * scale
    act_out[0] = (gated / (1.0 + jnp.exp(-gated)) * lifted).astype(BF)
    column = lax.broadcasted_iota(jnp.int32, extra.shape, 1)
    wanted = e0[0] + pl.program_id(0) + 3
    share = jnp.sum(jnp.where(column == wanted, extra, 0.0), axis=1, keepdims=True)
    comb_out[0] = (sel[0].astype(F32) * share).astype(BF)


def expert_up(k, chunks, sel, x, gate_proj, up_proj, sums, e0):
    held, slots, tokens = sel.shape
    units = gate_proj.shape[2]
    width = gate_proj.shape[1] // chunks
    first, last = k == 0, k == chunks - 1
    per_expert = lambda *tail: pl.BlockSpec((1,) + tail, lambda q: (q, 0, 0))
    weight = pl.BlockSpec((1, width, units), lambda q: (q, k, 0))
    in_specs = [per_expert(slots, tokens), pl.BlockSpec(x.shape, lambda q: (0, 0)), weight, weight]
    args = [sel, x, gate_proj, up_proj]
    if not first:
        in_specs += [per_expert(slots, units)] * 2
        args += list(sums)
    if last:
        in_specs.append(pl.BlockSpec(memory_space=pltpu.SMEM))
        args.append(e0)
        out_shape = (
            jax.ShapeDtypeStruct((held, slots, units), BF),
            jax.ShapeDtypeStruct((held, slots, tokens), BF),
        )
        out_specs = (per_expert(slots, units), per_expert(slots, tokens))
    else:
        out_shape = (jax.ShapeDtypeStruct((held, slots, units), F32),) * 2
        out_specs = (per_expert(slots, units),) * 2
    flops = 2 * held * slots * width * (tokens + 2 * units)
    return pl.pallas_call(
        functools.partial(up_body, first, last, width),
        grid=(held,),
        in_specs=in_specs,
        out_specs=out_specs,
        out_shape=out_shape,
        compiler_params=pltpu.CompilerParams(vmem_limit_bytes=40 << 20),
        cost_estimate=pl.CostEstimate(
            flops=flops, transcendentals=0, bytes_accessed=4 * held * width * units
        ),
        name=f"expert_up_{k}",
    )(*args)


def down_body(act, comb, wd, keep, send, total):
    q = pl.program_id(0)
    half = jnp.dot(act[0], wd[0], preferred_element_type=F32).astype(BF)
    part = lax.dot_general(
        comb[0], half, (((0,), (0,)), ((), ())), preferred_element_type=F32
    )

    @pl.when(q == 0)
    def _():
        total[...] = part

    @pl.when(q > 0)
    def _():
        total[...] += part

    @pl.when(q == pl.num_programs(0) - 1)
    def _():
        rows = keep.shape[0]
        keep[...] = total[:rows]
        send[...] = total[rows:].astype(BF)


def expert_down(k, chunks, act, comb, down_proj, kept):
    held, slots, units = act.shape
    tokens = comb.shape[2]
    width = down_proj.shape[2] // chunks
    return pl.pallas_call(
        down_body,
        grid=(held,),
        in_specs=[
            pl.BlockSpec((1, slots, units), lambda q: (q, 0, 0)),
            pl.BlockSpec((1, slots, tokens), lambda q: (q, 0, 0)),
            pl.BlockSpec((1, units, width), lambda q: (q, 0, k)),
        ],
        out_specs=(
            pl.BlockSpec((kept, width), lambda q: (0, 0)),
            pl.BlockSpec((tokens - kept, width), lambda q: (0, 0)),
        ),
        out_shape=(
            jax.ShapeDtypeStruct((kept, width), F32),
            jax.ShapeDtypeStruct((tokens - kept, width), BF),
        ),
        scratch_shapes=[pltpu.VMEM((tokens, width), F32)],
        compiler_params=pltpu.CompilerParams(vmem_limit_bytes=40 << 20),
        cost_estimate=pl.CostEstimate(
            flops=2 * held * slots * width * (tokens + units),
            transcendentals=0,
            bytes_accessed=2 * held * width * units,
        ),
        name=f"expert_down_{k}",
    )(act, comb, down_proj)


def body(
    ssm_input,
    write_vec,
    read_vec,
    step_raw,
    step_bias,
    decay_rate,
    skip_gain,
    cache_state,
    parents,
    out_proj,
    residual,
    norm_gain,
    router,
    expert_ids,
    gate_proj,
    up_proj,
    down_proj,
):
    nodes, requests, columns = ssm_input.shape
    heads = step_raw.shape[2]
    head_size = columns // heads
    local_nodes, _, width = residual.shape
    tokens = local_nodes * requests
    topk = expert_ids.shape[2]
    experts = router.shape[1]
    held = gate_proj.shape[0]
    ring = Ring(lax.axis_size("head"), lax.axis_size("req"))
    cores, ys, reqs = ring.cores, ring.ys, ring.reqs
    head_at = lax.axis_index("head")
    y_at, c_at = head_at // cores, head_at % cores
    device = head_at * reqs + lax.axis_index("req")
    e0 = (device * held) % experts

    choices = expert_ids.reshape(tokens, topk)
    labels = jnp.arange(experts, dtype=jnp.int32)
    match = choices[:, :, None] == labels[None, None, :]
    named = jnp.any(match, axis=1).astype(BF)

    states = write_vec.shape[2]
    early = jnp.concatenate(
        [write_vec.reshape(tokens, states), read_vec.reshape(tokens, states), named], axis=1
    )
    early = ring.gather_y(ring.gather_core(early))
    named_all = ring.gather_z(early[..., 2 * states :])
    named_all = named_all.transpose(2, 1, 0, 3, 4).reshape(-1, experts)
    early = early.reshape(ys * cores, tokens, -1)
    absolute = jnp.arange(ys * cores, dtype=jnp.int32)
    slot_of = ((y_at - absolute // cores) % ys) * cores + (c_at - absolute % cores) % cores
    vectors = jnp.take(early[..., : 2 * states], slot_of, axis=0, mode="clip")
    vectors = vectors.reshape(nodes, requests, 2 * states)
    writes, reads = vectors[..., :states], vectors[..., states:]

    inputs4 = ssm_input.reshape(nodes, requests, heads, head_size)
    step = jax.nn.softplus(step_raw + step_bias)
    rates = -step * decay_rate
    reach = ancestry(parents)
    depth = jnp.einsum("rji,irh->jrh", reach, rates, precision=lax.Precision.HIGHEST)
    affinity = jnp.einsum("jrn,irn->rji", reads, writes, preferred_element_type=F32)
    by_request = depth.transpose(1, 0, 2)
    spread = by_request[:, :, None, :] - by_request[:, None, :, :]
    linked = reach[:, :, :, None] > 0
    factor = jnp.where(linked, jnp.exp(jnp.where(linked, spread, 0.0)), 0.0)
    weights = (factor * affinity[:, :, :, None] * step.transpose(1, 0, 2)[:, None, :, :]).astype(BF)
    tree_part = jnp.einsum("rjih,irhp->jrhp", weights, inputs4, preferred_element_type=F32)
    cache_part = jnp.einsum("jrn,rhpn->jrhp", reads, cache_state, preferred_element_type=F32)
    cache_part = cache_part * jnp.exp(depth)[:, :, :, None]
    ssm_out = (tree_part + cache_part + skip_gain[:, None] * inputs4.astype(F32)).astype(BF)
    ssm_out = ssm_out.reshape(ys * cores, tokens, columns)

    slots = jnp.arange(cores * ys, dtype=jnp.int32)
    goes_to = ((y_at - slots % ys) % ys) * cores + (c_at - slots // ys) % cores
    ssm_out = jnp.take(ssm_out, goes_to, axis=0, mode="clip")
    near = ssm_out[:ys].reshape(ys * tokens, columns)
    far = ssm_out[ys:].reshape((cores - 1) * ys * tokens, columns)

    all_tokens = named_all.shape[0]
    capacity = 2 * tokens * topk // (experts + experts // 4)
    room = capacity * (all_tokens // tokens)
    mine = lax.dynamic_slice_in_dim(named_all, e0, held, axis=1)
    order = jnp.arange(all_tokens, dtype=jnp.int32)
    before = (order[:, None] > order[None, :]).astype(BF)
    rank = jnp.dot(before, mine, preferred_element_type=F32)
    place = jnp.where(mine > 0, rank, -1.0).T
    spots = jnp.arange(room, dtype=jnp.int32).astype(F32)
    sel = (place[:, None, :] == spots[None, :, None]).astype(BF)

    rows_left = residual.reshape(tokens, width)
    span = width // AG_CHUNKS
    chunks = []
    squares = 0.0
    sums = None
    for k in range(AG_CHUNKS):
        cut = slice(k * span, (k + 1) * span)
        weight = out_proj[:, cut]
        mixed = jnp.dot(near, weight, preferred_element_type=F32)
        if cores > 1:
            away = jnp.dot(far, weight, preferred_element_type=F32).astype(BF)
            mixed = ring.scatter([away], mixed, "dc")
        mixed = mixed.reshape(ys, tokens, span)
        mixed = ring.scatter([mixed[s].astype(BF) for s in range(1, ys)], mixed[0], "dy")
        after = (rows_left[:, cut].astype(F32) + mixed).astype(BF)
        chunks.append(after)
        widened = after.astype(F32)
        squares = squares + jnp.sum(widened * widened, axis=-1, keepdims=True)
        payload = (widened * norm_gain[cut]).astype(BF)
        if k == AG_CHUNKS - 1:
            after_mixer = jnp.concatenate(chunks, axis=1)
            scale = lax.rsqrt(squares / width + 1e-05)
            normed = (after_mixer.astype(F32) * scale * norm_gain).astype(BF)
            logits = jnp.dot(normed, router, preferred_element_type=F32)
            picked_logits = jnp.sum(jnp.where(match, logits[:, None, :], 0.0), axis=2)
            powered = jnp.exp(picked_logits)
            gate = (powered / jnp.sum(powered, axis=1, keepdims=True)).astype(BF)
            dense = jnp.sum(jnp.where(match, gate.astype(F32)[:, :, None], 0.0), axis=1)
            top = scale.astype(BF)
            middle = (scale - top.astype(F32)).astype(BF)
            low = (scale - top.astype(F32) - middle.astype(F32)).astype(BF)
            extra = jnp.concatenate([top, middle, low, dense.astype(BF)], axis=1)
            tail = -(-extra.shape[1] // LANES) * LANES
            extra = jnp.pad(extra, ((0, 0), (0, tail - extra.shape[1])))
            payload = jnp.concatenate([payload, extra], axis=1)
        rows = ring.gather_core(ring.gather_y(ring.gather_z(payload)))
        rows = rows.reshape(all_tokens, -1)
        sums = expert_up(
            k, AG_CHUNKS, sel, rows, gate_proj, up_proj, sums, e0.reshape(1).astype(jnp.int32)
        )
    act, comb = sums

    pieces = []
    span = width // RS_CHUNKS
    for k in range(RS_CHUNKS):
        keep, send = expert_down(k, RS_CHUNKS, act, comb, down_proj, ys * reqs * tokens)
        total = ring.scatter([send], keep, "dc") if cores > 1 else keep
        total = total.reshape(ys, reqs * tokens, span)
        total = ring.scatter([total[s].astype(BF) for s in range(1, ys)], total[0], "dy")
        total = total.reshape(reqs, tokens, span)
        total = ring.scatter([total[s].astype(BF) for s in range(1, reqs)], total[0], "dz")
        cut = slice(k * span, (k + 1) * span)
        pieces.append((after_mixer[:, cut].astype(F32) + total).astype(BF))
    return jnp.concatenate(pieces, axis=1).reshape(local_nodes, requests, width)


def solution(mesh):
    in_specs = (
        P(None, ("groups", "req"), "head"),
        P("head", ("groups", "req"), None),
        P("head", ("groups", "req"), None),
        P(None, ("groups", "req"), "head"),
        P("head"),
        P("head"),
        P("head"),
        P(("groups", "req"), "head", None, None),
        P(("groups", "req"), None),
        P("head", None),
        P("head", ("groups", "req"), None),
        P(),
        P(),
        P("head", ("groups", "req"), None),
        P(("head", "req"), None, None),
        P(("head", "req"), None, None),
        P(("head", "req"), None, None),
    )
    out_specs = P("head", ("groups", "req"), None)
    return jax.shard_map(body, mesh=mesh, in_specs=in_specs, out_specs=out_specs, check_vma=False)
```

```python
import functools
import jax
import jax.numpy as jnp
from jax import lax
from jax.experimental import pallas as pl
from jax.experimental.pallas import tpu as pltpu
from jax.sharding import PartitionSpec as P


BF = jnp.bfloat16
F32 = jnp.float32
AXES = ("head", "req")
LANES = 128
MIX_CHUNKS = 2
AG_CHUNKS = 4
RS_CHUNKS = 4
DOWN_BLOCK = 256


class Ring:
    def __init__(self, heads, reqs):
        self.heads, self.reqs = heads, reqs
        self.cores = 2 if heads % 2 == 0 else 1
        self.ys = heads // self.cores

    def pairs(self, dy, dc, dz):
        found = []
        for y in range(self.ys):
            for c in range(self.cores):
                for z in range(self.reqs):
                    there = ((y + dy) % self.ys) * self.cores + (c + dc) % self.cores
                    found.append(
                        (
                            (y * self.cores + c) * self.reqs + z,
                            there * self.reqs + (z + dz) % self.reqs,
                        )
                    )
        return found

    def shift(self, x, dy=0, dc=0, dz=0):
        return lax.ppermute(x, AXES, self.pairs(dy, dc, dz))

    def gather_core(self, x):
        return jnp.stack([x] + [self.shift(x, dc=s) for s in range(1, self.cores)])

    def gather_y(self, x):
        return jnp.stack([x] + [self.shift(x, dy=s) for s in range(1, self.ys)])

    def gather_z(self, x):
        return jnp.stack([x] + [self.shift(x, dz=s) for s in range(1, self.reqs)])

    def scatter(self, parts, keep, axis):
        total = keep
        for s, part in enumerate(parts, 1):
            total = total + self.shift(part, **{axis: -s}).astype(F32)
        return total


def prep_body(heads, parents, step_raw, bias, decay, factor, grown):
    rows = parents.shape[0]
    reqs = step_raw.shape[1]
    lane = lax.broadcasted_iota(jnp.int32, (rows, rows), 1)
    row = lax.broadcasted_iota(jnp.int32, (rows, rows), 0)
    hop = parents[...]
    at = jnp.where(hop >= 0, hop * reqs + lax.broadcasted_iota(jnp.int32, hop.shape, 0) % reqs, -1)
    power = jnp.where(at == lane, 1.0, 0.0)
    reach = jnp.where(row == lane, 1.0, 0.0) + power
    power = power.astype(BF)
    span = 2
    while span * reqs < rows:
        power = jnp.dot(power, power, preferred_element_type=F32).astype(BF)
        reach = reach + jnp.dot(reach.astype(BF), power, preferred_element_type=F32)
        span *= 2
    raw = step_raw[...].reshape(rows, heads) + bias[...]
    step = jnp.maximum(raw, 0.0) + jnp.log1p(jnp.exp(-jnp.abs(raw)))
    rate = -step * decay[...]
    blank = jnp.zeros((rows, rows - heads), F32)
    wide_step = jnp.concatenate([step, blank], axis=1)
    wide_rate = jnp.concatenate([rate, blank], axis=1)
    depth = jnp.dot(
        reach, wide_rate, preferred_element_type=F32, precision=lax.Precision.HIGHEST
    )
    grown[...] = jnp.exp(depth[:, :heads])
    depth_t = depth.T
    step_t = wide_step.T
    linked = reach > 0
    for h in range(heads):
        spread = jnp.where(linked, depth[:, h : h + 1] - depth_t[h : h + 1, :], 0.0)
        factor[h] = jnp.where(linked, jnp.exp(spread) * step_t[h : h + 1, :], 0.0)


def prepare(parents, step_raw, step_bias, decay_rate):
    nodes, reqs, heads = step_raw.shape
    rows = nodes * reqs
    return pl.pallas_call(
        functools.partial(prep_body, heads),
        out_shape=(
            jax.ShapeDtypeStruct((heads, rows, rows), F32),
            jax.ShapeDtypeStruct((rows, heads), F32),
        ),
        compiler_params=pltpu.CompilerParams(vmem_limit_bytes=16 << 20),
        name="prepare",
    )(
        parents.T.reshape(rows, 1),
        step_raw,
        step_bias.reshape(1, heads),
        decay_rate.reshape(1, heads),
    )


def front_body(
    heads, near_rows, slot_of, goes_to, early, x, state, factor, grown, skip, weight,
    near, far, mixed_rows, read_rows, write_rows, cache, result,
):
    blocks, tokens = early.shape[0], early.shape[1]
    nodes, reqs, columns = x.shape
    rows = nodes * reqs
    size = columns // heads
    states = state.shape[2]

    @pl.when(pl.program_id(0) == 0)
    def _():
        for a in range(blocks):
            block = early[slot_of[a]].astype(F32)
            write_rows[a * tokens : (a + 1) * tokens] = block[:, :states]
            read_rows[a * tokens : (a + 1) * tokens] = block[:, states : 2 * states]
        writes = write_rows[...].astype(BF)
        reads = read_rows[...].astype(BF)
        affinity = lax.dot_general(
            reads, writes, (((1,), (1,)), ((), ())), preferred_element_type=F32
        )
        for r in range(reqs):
            mine = read_rows[pl.ds(r, nodes, stride=reqs), :].astype(BF)
            got = lax.dot_general(
                mine, state[r], (((1,), (1,)), ((), ())), preferred_element_type=F32
            )
            for i in range(columns // LANES):
                cache.at[i][pl.ds(r, nodes, stride=reqs), :] = got[:, i * LANES : (i + 1) * LANES]
        values = x[...].reshape(rows, columns)
        pair = 2 * size
        left = lax.broadcasted_iota(jnp.int32, (rows, pair), 1) < size
        for h in range(0, heads, 2):
            cut = slice(h * size, h * size + pair)
            own = values[:, cut]
            first = (factor[h] * affinity).astype(BF)
            second = (factor[h + 1] * affinity).astype(BF)
            zero = jnp.zeros_like(own)
            both = jnp.dot(
                jnp.concatenate([first, second], axis=1),
                jnp.concatenate([jnp.where(left, own, zero), jnp.where(left, zero, own)], axis=0),
                preferred_element_type=F32,
            )
            grow = jnp.where(left, grown[:, h : h + 1], grown[:, h + 1 : h + 2])
            gain = jnp.where(left, skip[:, h : h + 1], skip[:, h + 1 : h + 2])
            both = both + cache[h * size // LANES] * grow + gain * own.astype(F32)
            result[:, cut] = both.astype(BF).astype(F32)
        for s in range(blocks):
            start = pl.multiple_of(goes_to[s] * tokens, tokens)
            mixed_rows[s * tokens : (s + 1) * tokens] = result[pl.ds(start, tokens)].astype(BF)

    total = jnp.dot(mixed_rows[...], weight[...], preferred_element_type=F32)
    near[...] = total[:near_rows]
    far[...] = total[near_rows:].astype(BF)


def front(early, x, state, factor, grown, skip_gain, out_proj, slot_of, goes_to, near_rows, part, parts):
    nodes, reqs, columns = x.shape
    heads = skip_gain.shape[0]
    rows = nodes * reqs
    states = state.shape[3]
    span = out_proj.shape[1] // parts
    block = min(span, 512)
    steps = span // block
    whole = lambda a: pl.BlockSpec(a.shape, lambda j, *_: (0,) * len(a.shape))
    state = state.reshape(state.shape[0], columns, states)
    skip = skip_gain.reshape(1, heads)
    return pl.pallas_call(
        functools.partial(front_body, heads, near_rows),
        grid_spec=pltpu.PrefetchScalarGridSpec(
            num_scalar_prefetch=2,
            grid=(steps,),
            in_specs=[
                whole(early), whole(x), whole(state), whole(factor), whole(grown), whole(skip),
                pl.BlockSpec((columns, block), lambda j, *_: (0, part * steps + j)),
            ],
            out_specs=(
                pl.BlockSpec((near_rows, block), lambda j, *_: (0, j)),
                pl.BlockSpec((rows - near_rows, block), lambda j, *_: (0, j)),
                pl.BlockSpec((rows, columns), lambda j, *_: (0, 0)),
            ),
            scratch_shapes=[
                pltpu.VMEM((rows, states), F32),
                pltpu.VMEM((rows, states), F32),
                pltpu.VMEM((columns // LANES, rows, LANES), F32),
                pltpu.VMEM((rows, columns), F32),
            ],
        ),
        out_shape=(
            jax.ShapeDtypeStruct((near_rows, span), F32),
            jax.ShapeDtypeStruct((rows - near_rows, span), BF),
            jax.ShapeDtypeStruct((rows, columns), BF),
        ),
        compiler_params=pltpu.CompilerParams(vmem_limit_bytes=32 << 20),
        cost_estimate=pl.CostEstimate(
            flops=2 * rows * columns * span, transcendentals=0, bytes_accessed=2 * columns * span
        ),
        name="front",
    )(slot_of, goes_to, early, x, state, factor, grown, skip, out_proj)


def project_body(near_rows, rows, weight, near, far):
    total = jnp.dot(rows[...], weight[...], preferred_element_type=F32)
    near[...] = total[:near_rows]
    far[...] = total[near_rows:].astype(BF)


def project(rows, out_proj, near_rows, part, parts):
    count, columns = rows.shape
    span = out_proj.shape[1] // parts
    block = min(span, 512)
    steps = span // block
    return pl.pallas_call(
        functools.partial(project_body, near_rows),
        grid=(steps,),
        in_specs=[
            pl.BlockSpec((count, columns), lambda j: (0, 0)),
            pl.BlockSpec((columns, block), lambda j: (0, part * steps + j)),
        ],
        out_specs=(
            pl.BlockSpec((near_rows, block), lambda j: (0, j)),
            pl.BlockSpec((count - near_rows, block), lambda j: (0, j)),
        ),
        out_shape=(
            jax.ShapeDtypeStruct((near_rows, span), F32),
            jax.ShapeDtypeStruct((count - near_rows, span), BF),
        ),
        compiler_params=pltpu.CompilerParams(vmem_limit_bytes=16 << 20),
        cost_estimate=pl.CostEstimate(
            flops=2 * count * columns * span, transcendentals=0, bytes_accessed=2 * columns * span
        ),
        name="project",
    )(rows, out_proj)


def up_body(first, last, token_at, x, wg, wu, *rest):
    rest = list(rest)
    if not first:
        gin, uin = rest.pop(0), rest.pop(0)
    if last:
        extra, spot, share = rest.pop(0), rest.pop(0), rest.pop(0)
    if last:
        act_out, comb_out, spread, picked, scales = rest
    else:
        gout, uout, spread, picked = rest
    q = pl.program_id(0)
    tokens, width = x.shape
    tall = width // LANES
    slots = picked.shape[0] // tall

    @pl.when(q == 0)
    def _():
        for i in range(tall):
            spread[pl.ds(i, tokens, stride=tall), :] = x[:, i * LANES : (i + 1) * LANES].astype(F32)

    for c in range(slots):
        token = token_at[q * slots + c]
        picked[c * tall : (c + 1) * tall] = spread[pl.ds(pl.multiple_of(token * tall, tall), tall)]
        if last:
            scales[c : c + 1] = extra[pl.ds(token, 1)]
    rows = jnp.concatenate(
        [picked[pl.ds(i, slots, stride=tall), :].astype(BF) for i in range(tall)], axis=1
    )
    gated = jnp.dot(rows, wg[0], preferred_element_type=F32)
    lifted = jnp.dot(rows, wu[0], preferred_element_type=F32)
    if not first:
        gated = gated + gin[0]
        lifted = lifted + uin[0]
    if not last:
        gout[0] = gated
        uout[0] = lifted
        return
    scale = scales[:, 0:1] + scales[:, 1:2] + scales[:, 2:3]
    gated = gated * scale
    lifted = lifted * scale
    act_out[0] = (gated / (1.0 + jnp.exp(-gated)) * lifted).astype(BF)
    lane = lax.broadcasted_iota(jnp.int32, (tokens, slots), 1)
    column = lax.broadcasted_iota(jnp.int32, spot.shape, 1)
    own_spot = jnp.sum(jnp.where(column == q, spot[...], 0), axis=1, keepdims=True)
    own_share = jnp.sum(jnp.where(column == q, share[...], 0.0), axis=1, keepdims=True)
    comb_out[...] = jnp.where(lane == own_spot, own_share, 0.0).astype(BF)


def expert_up(k, chunks, token_at, x, gate_proj, up_proj, sums, extras):
    held = gate_proj.shape[0]
    tokens, width = x.shape
    slots = token_at.shape[0] // held
    units = gate_proj.shape[2]
    first, last = k == 0, k == chunks - 1
    per_expert = lambda *tail: pl.BlockSpec((1,) + tail, lambda q, *_: (q, 0, 0))
    whole = lambda a: pl.BlockSpec(a.shape, lambda q, *_: (0, 0))
    weight = pl.BlockSpec((1, width, units), lambda q, *_: (q, k, 0))
    in_specs = [whole(x), weight, weight]
    args = [x, gate_proj, up_proj]
    scratch = [
        pltpu.VMEM((tokens * width // LANES, LANES), F32),
        pltpu.VMEM((slots * width // LANES, LANES), F32),
    ]
    if not first:
        in_specs += [per_expert(slots, units)] * 2
        args += list(sums)
    if last:
        in_specs += [whole(a) for a in extras]
        args += list(extras)
        out_shape = (
            jax.ShapeDtypeStruct((held, slots, units), BF),
            jax.ShapeDtypeStruct((tokens, held * slots), BF),
        )
        out_specs = (per_expert(slots, units), pl.BlockSpec((tokens, slots), lambda q, *_: (0, q)))
        scratch.append(pltpu.VMEM((slots, extras[0].shape[1]), F32))
    else:
        out_shape = (jax.ShapeDtypeStruct((held, slots, units), F32),) * 2
        out_specs = (per_expert(slots, units),) * 2
    return pl.pallas_call(
        functools.partial(up_body, first, last),
        grid_spec=pltpu.PrefetchScalarGridSpec(
            num_scalar_prefetch=1,
            grid=(held,),
            in_specs=in_specs,
            out_specs=out_specs,
            scratch_shapes=scratch,
        ),
        out_shape=out_shape,
        compiler_params=pltpu.CompilerParams(vmem_limit_bytes=40 << 20),
        cost_estimate=pl.CostEstimate(
            flops=4 * held * slots * width * units,
            transcendentals=0,
            bytes_accessed=4 * held * width * units,
        ),
        name=f"expert_up_{k}",
    )(token_at, *args)


def down_body(act, comb, wd, keep, send, halves):
    held, slots, _ = act.shape
    for q in range(held):
        halves[q * slots : (q + 1) * slots] = jnp.dot(
            act[q], wd[q], preferred_element_type=F32
        ).astype(BF)
    kept = keep.shape[0]
    total = jnp.dot(comb[...], halves[...], preferred_element_type=F32)
    keep[...] = total[:kept]
    send[...] = total[kept:].astype(BF)


def expert_down(k, chunks, act, comb, down_proj, kept):
    held, slots, units = act.shape
    tokens = comb.shape[0]
    width = down_proj.shape[2] // chunks
    block = min(width, DOWN_BLOCK)
    steps = width // block
    return pl.pallas_call(
        down_body,
        grid=(steps,),
        in_specs=[
            pl.BlockSpec(act.shape, lambda j: (0, 0, 0)),
            pl.BlockSpec(comb.shape, lambda j: (0, 0)),
            pl.BlockSpec((held, units, block), lambda j: (0, 0, k * steps + j)),
        ],
        out_specs=(
            pl.BlockSpec((kept, block), lambda j: (0, j)),
            pl.BlockSpec((tokens - kept, block), lambda j: (0, j)),
        ),
        out_shape=(
            jax.ShapeDtypeStruct((kept, width), F32),
            jax.ShapeDtypeStruct((tokens - kept, width), BF),
        ),
        scratch_shapes=[pltpu.VMEM((held * slots, block), BF)],
        compiler_params=pltpu.CompilerParams(vmem_limit_bytes=40 << 20),
        cost_estimate=pl.CostEstimate(
            flops=2 * held * slots * width * (tokens + units),
            transcendentals=0,
            bytes_accessed=2 * held * width * units,
        ),
        name=f"expert_down_{k}",
    )(act, comb, down_proj)


def body(
    ssm_input,
    write_vec,
    read_vec,
    step_raw,
    step_bias,
    decay_rate,
    skip_gain,
    cache_state,
    parents,
    out_proj,
    residual,
    norm_gain,
    router,
    expert_ids,
    gate_proj,
    up_proj,
    down_proj,
):
    nodes, requests, columns = ssm_input.shape
    heads = step_raw.shape[2]
    head_size = columns // heads
    local_nodes, _, width = residual.shape
    tokens = local_nodes * requests
    topk = expert_ids.shape[2]
    experts = router.shape[1]
    held = gate_proj.shape[0]
    ring = Ring(lax.axis_size("head"), lax.axis_size("req"))
    cores, ys, reqs = ring.cores, ring.ys, ring.reqs
    head_at = lax.axis_index("head")
    y_at, c_at = head_at // cores, head_at % cores
    device = head_at * reqs + lax.axis_index("req")
    e0 = (device * held) % experts

    choices = expert_ids.reshape(tokens, topk)
    labels = jnp.arange(experts, dtype=jnp.int32)
    match = choices[:, :, None] == labels[None, None, :]
    named = jnp.any(match, axis=1).astype(BF)

    states = write_vec.shape[2]
    early = jnp.concatenate(
        [write_vec.reshape(tokens, states), read_vec.reshape(tokens, states), named], axis=1
    )
    early = ring.gather_y(ring.gather_core(early))
    named_all = ring.gather_z(early[..., 2 * states :])
    named_all = named_all.transpose(2, 1, 0, 3, 4).reshape(-1, experts)
    early = early.reshape(ys * cores, tokens, -1)
    absolute = jnp.arange(ys * cores, dtype=jnp.int32)
    slot_of = ((y_at - absolute // cores) % ys) * cores + (c_at - absolute % cores) % cores
    slots = jnp.arange(cores * ys, dtype=jnp.int32)
    goes_to = ((y_at - slots % ys) % ys) * cores + (c_at - slots // ys) % cores
    factor, grown = prepare(parents, step_raw, step_bias, decay_rate)
    near_rows = ys * tokens

    all_tokens = named_all.shape[0]
    capacity = 2 * tokens * topk // (experts + experts // 4)
    room = capacity * (all_tokens // tokens)
    mine = lax.dynamic_slice_in_dim(named_all, e0, held, axis=1)
    order = jnp.arange(all_tokens, dtype=jnp.int32)
    before = (order[:, None] > order[None, :]).astype(BF)
    rank = jnp.dot(before, mine, preferred_element_type=F32)
    place = jnp.where(mine > 0, rank, -1.0).astype(jnp.int32)
    spots = jnp.arange(room, dtype=jnp.int32)
    chosen = place.T[:, None, :] == spots[None, :, None]
    token_at = jnp.sum(jnp.where(chosen, order, 0), axis=2).reshape(-1)

    rows_left = residual.reshape(tokens, width)
    mixes = []
    part_span = width // MIX_CHUNKS
    for m in range(MIX_CHUNKS):
        cut = slice(m * part_span, (m + 1) * part_span)
        if m == 0:
            mixed, away, mixed_rows = front(
                early, ssm_input, cache_state, factor, grown, skip_gain, out_proj,
                slot_of, goes_to, near_rows, m, MIX_CHUNKS,
            )
        else:
            mixed, away = project(mixed_rows, out_proj, near_rows, m, MIX_CHUNKS)
        if cores > 1:
            mixed = ring.scatter([away], mixed, "dc")
        mixed = mixed.reshape(ys, tokens, part_span)
        mixed = ring.scatter([mixed[s].astype(BF) for s in range(1, ys)], mixed[0], "dy")
        mixes.append((rows_left[:, cut].astype(F32) + mixed).astype(BF))
    span = width // AG_CHUNKS
    after_mixer = jnp.concatenate(mixes, axis=1)
    sums = None
    for k in range(AG_CHUNKS):
        cut = slice(k * span, (k + 1) * span)
        m = k * MIX_CHUNKS // AG_CHUNKS
        local = slice(k * span - m * part_span, (k + 1) * span - m * part_span)
        payload = (mixes[m][:, local].astype(F32) * norm_gain[cut]).astype(BF)
        extras = None
        if k == AG_CHUNKS - 1:
            widened = after_mixer.astype(F32)
            scale = lax.rsqrt(jnp.mean(widened * widened, axis=-1, keepdims=True) + 1e-05)
            normed = (widened * scale * norm_gain).astype(BF)
            logits = jnp.dot(normed, router, preferred_element_type=F32)
            picked_logits = jnp.sum(jnp.where(match, logits[:, None, :], 0.0), axis=2)
            powered = jnp.exp(picked_logits)
            gate = (powered / jnp.sum(powered, axis=1, keepdims=True)).astype(BF)
            dense = jnp.sum(jnp.where(match, gate.astype(F32)[:, :, None], 0.0), axis=1)
            top = scale.astype(BF)
            middle = (scale - top.astype(F32)).astype(BF)
            low = (scale - top.astype(F32) - middle.astype(F32)).astype(BF)
            extra = jnp.concatenate([top, middle, low, dense.astype(BF)], axis=1)
            tail = -(-extra.shape[1] // LANES) * LANES
            extra = jnp.pad(extra, ((0, 0), (0, tail - extra.shape[1])))
            payload = jnp.concatenate([payload, extra], axis=1)
        rows = ring.gather_core(ring.gather_y(ring.gather_z(payload)))
        rows = rows.reshape(all_tokens, -1)
        if k == AG_CHUNKS - 1:
            extra = rows[:, span:].astype(F32)
            rows = rows[:, :span]
            share = lax.dynamic_slice_in_dim(extra, e0 + 3, held, axis=1)
            extras = (extra, place, share)
        sums = expert_up(k, AG_CHUNKS, token_at, rows, gate_proj, up_proj, sums, extras)
    act, comb = sums

    pieces = []
    span = width // RS_CHUNKS
    for k in range(RS_CHUNKS):
        keep, send = expert_down(k, RS_CHUNKS, act, comb, down_proj, ys * reqs * tokens)
        total = ring.scatter([send], keep, "dc") if cores > 1 else keep
        total = total.reshape(ys, reqs * tokens, span)
        total = ring.scatter([total[s].astype(BF) for s in range(1, ys)], total[0], "dy")
        total = total.reshape(reqs, tokens, span)
        total = ring.scatter([total[s].astype(BF) for s in range(1, reqs)], total[0], "dz")
        cut = slice(k * span, (k + 1) * span)
        pieces.append((after_mixer[:, cut].astype(F32) + total).astype(BF))
    return jnp.concatenate(pieces, axis=1).reshape(local_nodes, requests, width)


def solution(mesh):
    in_specs = (
        P(None, ("groups", "req"), "head"),
        P("head", ("groups", "req"), None),
        P("head", ("groups", "req"), None),
        P(None, ("groups", "req"), "head"),
        P("head"),
        P("head"),
        P("head"),
        P(("groups", "req"), "head", None, None),
        P(("groups", "req"), None),
        P("head", None),
        P("head", ("groups", "req"), None),
        P(),
        P(),
        P("head", ("groups", "req"), None),
        P(("head", "req"), None, None),
        P(("head", "req"), None, None),
        P(("head", "req"), None, None),
    )
    out_specs = P("head", ("groups", "req"), None)
    return jax.shard_map(body, mesh=mesh, in_specs=in_specs, out_specs=out_specs, check_vma=False)
```

```python
import functools
import jax
import jax.numpy as jnp
from jax import lax
from jax.experimental import pallas as pl
from jax.experimental.pallas import tpu as pltpu
from jax.sharding import PartitionSpec as P


BF = jnp.bfloat16
F32 = jnp.float32
AXES = ("head", "req")
LANES = 128
MIX_CHUNKS = 2
AG_CHUNKS = 4
RS_CHUNKS = 4
DOWN_BLOCK = 512
BATCH = 16


def in_hbm(*arrays):
    return [pltpu.with_memory_space_constraint(a, pltpu.HBM) for a in arrays]


class Ring:
    def __init__(self, heads, reqs):
        self.heads, self.reqs = heads, reqs
        self.cores = 2 if heads % 2 == 0 else 1
        self.ys = heads // self.cores

    def pairs(self, dy, dc, dz):
        found = []
        for y in range(self.ys):
            for c in range(self.cores):
                for z in range(self.reqs):
                    there = ((y + dy) % self.ys) * self.cores + (c + dc) % self.cores
                    found.append(
                        (
                            (y * self.cores + c) * self.reqs + z,
                            there * self.reqs + (z + dz) % self.reqs,
                        )
                    )
        return found

    def shift(self, x, dy=0, dc=0, dz=0):
        return lax.ppermute(x, AXES, self.pairs(dy, dc, dz))

    def gather(self, x, axis):
        count = {"dc": self.cores, "dy": self.ys, "dz": self.reqs}[axis]
        moved = [self.shift(x, **{axis: s}) for s in range(1, count)]
        return jnp.stack([x] + moved)

    def scatter(self, parts, keep, axis):
        total = keep
        for s, part in enumerate(parts, 1):
            total = total + self.shift(part, **{axis: -s}).astype(F32)
        return total


def prep_body(heads, parents, step_raw, bias, decay, factor, grown):
    rows = parents.shape[0]
    reqs = step_raw.shape[1]
    lane = lax.broadcasted_iota(jnp.int32, (rows, rows), 1)
    row = lax.broadcasted_iota(jnp.int32, (rows, rows), 0)
    hop = parents[...]
    at = jnp.where(hop >= 0, hop * reqs + lax.broadcasted_iota(jnp.int32, hop.shape, 0) % reqs, -1)
    power = jnp.where(at == lane, 1.0, 0.0)
    reach = jnp.where(row == lane, 1.0, 0.0) + power
    power = power.astype(BF)
    span = 2
    while span * reqs < rows:
        power = jnp.dot(power, power, preferred_element_type=F32).astype(BF)
        reach = reach + jnp.dot(reach.astype(BF), power, preferred_element_type=F32)
        span *= 2
    raw = step_raw[...].reshape(rows, heads) + bias[...]
    step = jnp.maximum(raw, 0.0) + jnp.log1p(jnp.exp(-jnp.abs(raw)))
    rate = -step * decay[...]
    blank = jnp.zeros((rows, rows - heads), F32)
    wide_step = jnp.concatenate([step, blank], axis=1)
    wide_rate = jnp.concatenate([rate, blank], axis=1)
    depth = jnp.dot(
        reach, wide_rate, preferred_element_type=F32, precision=lax.Precision.HIGHEST
    )
    grown[...] = jnp.exp(depth[:, :heads])
    depth_t = depth.T
    step_t = wide_step.T
    linked = reach > 0
    for h in range(heads):
        spread = jnp.where(linked, depth[:, h : h + 1] - depth_t[h : h + 1, :], 0.0)
        factor[h] = jnp.where(linked, jnp.exp(spread) * step_t[h : h + 1, :], 0.0)


def prepare(parents, step_raw, step_bias, decay_rate):
    nodes, reqs, heads = step_raw.shape
    rows = nodes * reqs
    return pl.pallas_call(
        functools.partial(prep_body, heads),
        out_shape=(
            jax.ShapeDtypeStruct((heads, rows, rows), F32),
            jax.ShapeDtypeStruct((rows, heads), F32),
        ),
        compiler_params=pltpu.CompilerParams(vmem_limit_bytes=16 << 20),
        name="prepare",
    )(
        parents.T.reshape(rows, 1),
        *in_hbm(step_raw, step_bias.reshape(1, heads), decay_rate.reshape(1, heads)),
    )


def front_body(
    heads, near_rows, slot_of, goes_to, early, x, state, factor, grown, skip, weight,
    near, far, mixed_rows, read_rows, write_rows, cache, result,
):
    blocks, tokens = early.shape[0], early.shape[1]
    nodes, reqs, columns = x.shape
    rows = nodes * reqs
    size = columns // heads
    states = state.shape[2]

    @pl.when(pl.program_id(0) == 0)
    def _():
        for a in range(blocks):
            block = early[slot_of[a]].astype(F32)
            write_rows[a * tokens : (a + 1) * tokens] = block[:, :states]
            read_rows[a * tokens : (a + 1) * tokens] = block[:, states : 2 * states]
        writes = write_rows[...].astype(BF)
        reads = read_rows[...].astype(BF)
        affinity = lax.dot_general(
            reads, writes, (((1,), (1,)), ((), ())), preferred_element_type=F32
        )
        for r in range(reqs):
            mine = read_rows[pl.ds(r, nodes, stride=reqs), :].astype(BF)
            got = lax.dot_general(
                mine, state[r], (((1,), (1,)), ((), ())), preferred_element_type=F32
            )
            for i in range(columns // LANES):
                cache.at[i][pl.ds(r, nodes, stride=reqs), :] = got[:, i * LANES : (i + 1) * LANES]
        values = x[...].reshape(rows, columns)
        pair = 2 * size
        left = lax.broadcasted_iota(jnp.int32, (rows, pair), 1) < size
        for h in range(0, heads, 2):
            cut = slice(h * size, h * size + pair)
            own = values[:, cut]
            first = (factor[h] * affinity).astype(BF)
            second = (factor[h + 1] * affinity).astype(BF)
            zero = jnp.zeros_like(own)
            both = jnp.dot(
                jnp.concatenate([first, second], axis=1),
                jnp.concatenate([jnp.where(left, own, zero), jnp.where(left, zero, own)], axis=0),
                preferred_element_type=F32,
            )
            grow = jnp.where(left, grown[:, h : h + 1], grown[:, h + 1 : h + 2])
            gain = jnp.where(left, skip[:, h : h + 1], skip[:, h + 1 : h + 2])
            both = both + cache[h * size // LANES] * grow + gain * own.astype(F32)
            result[:, cut] = both.astype(BF).astype(F32)
        for s in range(blocks):
            start = pl.multiple_of(goes_to[s] * tokens, tokens)
            mixed_rows[s * tokens : (s + 1) * tokens] = result[pl.ds(start, tokens)].astype(BF)

    total = jnp.dot(mixed_rows[...], weight[...], preferred_element_type=F32)
    near[...] = total[:near_rows]
    far[...] = total[near_rows:].astype(BF)


def front(early, x, state, factor, grown, skip_gain, out_proj, slot_of, goes_to, near_rows, part, parts):
    nodes, reqs, columns = x.shape
    heads = skip_gain.shape[0]
    rows = nodes * reqs
    states = state.shape[3]
    span = out_proj.shape[1] // parts
    block = min(span, 512)
    steps = span // block
    whole = lambda a: pl.BlockSpec(a.shape, lambda j, *_: (0,) * len(a.shape))
    state = state.reshape(state.shape[0], columns, states)
    skip = skip_gain.reshape(1, heads)
    x, state, skip, out_proj = in_hbm(x, state, skip, out_proj)
    return pl.pallas_call(
        functools.partial(front_body, heads, near_rows),
        grid_spec=pltpu.PrefetchScalarGridSpec(
            num_scalar_prefetch=2,
            grid=(steps,),
            in_specs=[
                whole(early), whole(x), whole(state), whole(factor), whole(grown), whole(skip),
                pl.BlockSpec((columns, block), lambda j, *_: (0, part * steps + j)),
            ],
            out_specs=(
                pl.BlockSpec((near_rows, block), lambda j, *_: (0, j)),
                pl.BlockSpec((rows - near_rows, block), lambda j, *_: (0, j)),
                pl.BlockSpec((rows, columns), lambda j, *_: (0, 0)),
            ),
            scratch_shapes=[
                pltpu.VMEM((rows, states), F32),
                pltpu.VMEM((rows, states), F32),
                pltpu.VMEM((columns // LANES, rows, LANES), F32),
                pltpu.VMEM((rows, columns), F32),
            ],
        ),
        out_shape=(
            jax.ShapeDtypeStruct((near_rows, span), F32),
            jax.ShapeDtypeStruct((rows - near_rows, span), BF),
            jax.ShapeDtypeStruct((rows, columns), BF),
        ),
        compiler_params=pltpu.CompilerParams(vmem_limit_bytes=32 << 20),
        cost_estimate=pl.CostEstimate(
            flops=2 * rows * columns * span, transcendentals=0, bytes_accessed=2 * columns * span
        ),
        name="front",
    )(slot_of, goes_to, early, x, state, factor, grown, skip, out_proj)


def project_body(near_rows, rows, weight, near, far):
    total = jnp.dot(rows[...], weight[...], preferred_element_type=F32)
    near[...] = total[:near_rows]
    far[...] = total[near_rows:].astype(BF)


def project(rows, out_proj, near_rows, part, parts):
    count, columns = rows.shape
    span = out_proj.shape[1] // parts
    block = min(span, 512)
    steps = span // block
    return pl.pallas_call(
        functools.partial(project_body, near_rows),
        grid=(steps,),
        in_specs=[
            pl.BlockSpec((count, columns), lambda j: (0, 0)),
            pl.BlockSpec((columns, block), lambda j: (0, part * steps + j)),
        ],
        out_specs=(
            pl.BlockSpec((near_rows, block), lambda j: (0, j)),
            pl.BlockSpec((count - near_rows, block), lambda j: (0, j)),
        ),
        out_shape=(
            jax.ShapeDtypeStruct((near_rows, span), F32),
            jax.ShapeDtypeStruct((count - near_rows, span), BF),
        ),
        compiler_params=pltpu.CompilerParams(vmem_limit_bytes=16 << 20),
        cost_estimate=pl.CostEstimate(
            flops=2 * count * columns * span, transcendentals=0, bytes_accessed=2 * columns * span
        ),
        name="project",
    )(rows, *in_hbm(out_proj))


def up_body(first, last, token_at, x, wg, wu, *rest):
    rest = list(rest)
    if not first:
        gin, uin = rest.pop(0), rest.pop(0)
    if last:
        extra, spot, share = rest.pop(0), rest.pop(0), rest.pop(0)
    if last:
        act_out, comb_out, spread, picked, scales = rest
    else:
        gout, uout, spread, picked = rest
    q = pl.program_id(0)
    tokens, width = x.shape
    tall = width // LANES
    slots = picked.shape[0] // tall

    @pl.when(q == 0)
    def _():
        for i in range(tall):
            spread[pl.ds(i, tokens, stride=tall), :] = x[:, i * LANES : (i + 1) * LANES].astype(F32)

    for c in range(0, slots, BATCH):
        at = [token_at[q * slots + c + i] for i in range(BATCH)]
        got = [spread[pl.ds(pl.multiple_of(t * tall, tall), tall)] for t in at]
        picked[c * tall : (c + BATCH) * tall] = jnp.concatenate(got, axis=0)
        if last:
            got = [extra[pl.ds(t, 1)] for t in at]
            for i in range(BATCH):
                scales[c + i : c + i + 1] = got[i]
    rows = jnp.concatenate(
        [picked[pl.ds(i, slots, stride=tall), :].astype(BF) for i in range(tall)], axis=1
    )
    gated = jnp.dot(rows, wg[0], preferred_element_type=F32)
    lifted = jnp.dot(rows, wu[0], preferred_element_type=F32)
    if not first:
        gated = gated + gin[0]
        lifted = lifted + uin[0]
    if not last:
        gout[0] = gated
        uout[0] = lifted
        return
    scale = scales[:, 0:1] + scales[:, 1:2] + scales[:, 2:3]
    gated = gated * scale
    lifted = lifted * scale
    act_out[0] = (gated / (1.0 + jnp.exp(-gated)) * lifted).astype(BF)
    lane = lax.broadcasted_iota(jnp.int32, (tokens, slots), 1)
    column = lax.broadcasted_iota(jnp.int32, spot.shape, 1)
    own_spot = jnp.sum(jnp.where(column == q, spot[...], 0), axis=1, keepdims=True)
    own_share = jnp.sum(jnp.where(column == q, share[...], 0.0), axis=1, keepdims=True)
    comb_out[...] = jnp.where(lane == own_spot, own_share, 0.0).astype(BF)


def expert_up(k, chunks, token_at, x, gate_proj, up_proj, sums, extras):
    held = gate_proj.shape[0]
    tokens, width = x.shape
    slots = token_at.shape[0] // held
    units = gate_proj.shape[2]
    first, last = k == 0, k == chunks - 1
    per_expert = lambda *tail: pl.BlockSpec((1,) + tail, lambda q, *_: (q, 0, 0))
    whole = lambda a: pl.BlockSpec(a.shape, lambda q, *_: (0, 0))
    weight = pl.BlockSpec((1, width, units), lambda q, *_: (q, k, 0))
    in_specs = [whole(x), weight, weight]
    args = [x, *in_hbm(gate_proj, up_proj)]
    scratch = [
        pltpu.VMEM((tokens * width // LANES, LANES), F32),
        pltpu.VMEM((slots * width // LANES, LANES), F32),
    ]
    if not first:
        in_specs += [per_expert(slots, units)] * 2
        args += list(sums)
    if last:
        in_specs += [whole(a) for a in extras]
        args += list(extras)
        out_shape = (
            jax.ShapeDtypeStruct((held, slots, units), BF),
            jax.ShapeDtypeStruct((tokens, held * slots), BF),
        )
        out_specs = (per_expert(slots, units), pl.BlockSpec((tokens, slots), lambda q, *_: (0, q)))
        scratch.append(pltpu.VMEM((slots, extras[0].shape[1]), F32))
    else:
        out_shape = (jax.ShapeDtypeStruct((held, slots, units), F32),) * 2
        out_specs = (per_expert(slots, units),) * 2
    return pl.pallas_call(
        functools.partial(up_body, first, last),
        grid_spec=pltpu.PrefetchScalarGridSpec(
            num_scalar_prefetch=1,
            grid=(held,),
            in_specs=in_specs,
            out_specs=out_specs,
            scratch_shapes=scratch,
        ),
        out_shape=out_shape,
        compiler_params=pltpu.CompilerParams(vmem_limit_bytes=40 << 20),
        cost_estimate=pl.CostEstimate(
            flops=4 * held * slots * width * units,
            transcendentals=0,
            bytes_accessed=4 * held * width * units,
        ),
    )(token_at, *args)


def down_body(act, comb, wd, keep, send, halves):
    held, slots, _ = act.shape
    for q in range(held):
        halves[q * slots : (q + 1) * slots] = jnp.dot(
            act[q], wd[q], preferred_element_type=F32
        ).astype(BF)
    kept = keep.shape[0]
    total = jnp.dot(comb[...], halves[...], preferred_element_type=F32)
    keep[...] = total[:kept]
    send[...] = total[kept:].astype(BF)


def expert_down(k, chunks, act, comb, down_proj, kept):
    held, slots, units = act.shape
    tokens = comb.shape[0]
    width = down_proj.shape[2] // chunks
    block = min(width, DOWN_BLOCK)
    steps = width // block
    return pl.pallas_call(
        down_body,
        grid=(steps,),
        in_specs=[
            pl.BlockSpec(act.shape, lambda j: (0, 0, 0)),
            pl.BlockSpec(comb.shape, lambda j: (0, 0)),
            pl.BlockSpec((held, units, block), lambda j: (0, 0, k * steps + j)),
        ],
        out_specs=(
            pl.BlockSpec((kept, block), lambda j: (0, j)),
            pl.BlockSpec((tokens - kept, block), lambda j: (0, j)),
        ),
        out_shape=(
            jax.ShapeDtypeStruct((kept, width), F32),
            jax.ShapeDtypeStruct((tokens - kept, width), BF),
        ),
        scratch_shapes=[pltpu.VMEM((held * slots, block), BF)],
        compiler_params=pltpu.CompilerParams(vmem_limit_bytes=40 << 20),
        cost_estimate=pl.CostEstimate(
            flops=2 * held * slots * width * (tokens + units),
            transcendentals=0,
            bytes_accessed=2 * held * width * units,
        ),
    )(act, comb, *in_hbm(down_proj))


def layer(
    ssm_input,
    write_vec,
    read_vec,
    step_raw,
    step_bias,
    decay_rate,
    skip_gain,
    cache_state,
    parents,
    out_proj,
    residual,
    norm_gain,
    router,
    expert_ids,
    gate_proj,
    up_proj,
    down_proj,
):
    _, requests, _ = ssm_input.shape
    local_nodes, _, width = residual.shape
    tokens = local_nodes * requests
    topk = expert_ids.shape[2]
    experts = router.shape[1]
    held = gate_proj.shape[0]
    ring = Ring(lax.axis_size("head"), lax.axis_size("req"))
    cores, ys, reqs = ring.cores, ring.ys, ring.reqs
    head_at = lax.axis_index("head")
    y_at, c_at = head_at // cores, head_at % cores
    device = head_at * reqs + lax.axis_index("req")
    e0 = (device * held) % experts

    choices = expert_ids.reshape(tokens, topk)
    labels = jnp.arange(experts, dtype=jnp.int32)
    match = choices[:, :, None] == labels[None, None, :]
    named = jnp.any(match, axis=1).astype(BF)

    states = write_vec.shape[2]
    early = jnp.concatenate(
        [write_vec.reshape(tokens, states), read_vec.reshape(tokens, states)], axis=1
    )
    early = ring.gather(ring.gather(early, "dc"), "dy")
    early = early.reshape(ys * cores, tokens, -1)
    absolute = jnp.arange(ys * cores, dtype=jnp.int32)
    slot_of = ((y_at - absolute // cores) % ys) * cores + (c_at - absolute % cores) % cores
    slots = jnp.arange(cores * ys, dtype=jnp.int32)
    goes_to = ((y_at - slots % ys) % ys) * cores + (c_at - slots // ys) % cores
    factor, grown = prepare(parents, step_raw, step_bias, decay_rate)
    near_rows = ys * tokens

    all_tokens = cores * ys * reqs * tokens
    capacity = 2 * tokens * topk // (experts + experts // 4)
    room = capacity * cores * ys * reqs

    rows_left = residual.reshape(tokens, width)
    mixes = []
    part_span = width // MIX_CHUNKS
    for m in range(MIX_CHUNKS):
        cut = slice(m * part_span, (m + 1) * part_span)
        if m == 0:
            mixed, away, mixed_rows = front(
                early, ssm_input, cache_state, factor, grown, skip_gain, out_proj,
                slot_of, goes_to, near_rows, m, MIX_CHUNKS,
            )
        else:
            mixed, away = project(mixed_rows, out_proj, near_rows, m, MIX_CHUNKS)
        if cores > 1:
            mixed = ring.scatter([away], mixed, "dc")
        mixed = mixed.reshape(ys, tokens, part_span)
        mixed = ring.scatter([mixed[s].astype(BF) for s in range(1, ys)], mixed[0], "dy")
        mixes.append((rows_left[:, cut].astype(F32) + mixed).astype(BF))
    span = width // AG_CHUNKS
    after_mixer = jnp.concatenate(mixes, axis=1)
    sums = None
    for k in range(AG_CHUNKS):
        cut = slice(k * span, (k + 1) * span)
        m = k * MIX_CHUNKS // AG_CHUNKS
        local = slice(k * span - m * part_span, (k + 1) * span - m * part_span)
        payload = (mixes[m][:, local].astype(F32) * norm_gain[cut]).astype(BF)
        extras = None
        if k == AG_CHUNKS - 1:
            widened = after_mixer.astype(F32)
            scale = lax.rsqrt(jnp.mean(widened * widened, axis=-1, keepdims=True) + 1e-05)
            normed = (widened * scale * norm_gain).astype(BF)
            logits = jnp.dot(normed, router, preferred_element_type=F32)
            picked_logits = jnp.sum(jnp.where(match, logits[:, None, :], 0.0), axis=2)
            powered = jnp.exp(picked_logits)
            gate = (powered / jnp.sum(powered, axis=1, keepdims=True)).astype(BF)
            dense = jnp.sum(jnp.where(match, gate.astype(F32)[:, :, None], 0.0), axis=1)
            top = scale.astype(BF)
            middle = (scale - top.astype(F32)).astype(BF)
            low = (scale - top.astype(F32) - middle.astype(F32)).astype(BF)
            extra = jnp.concatenate([top, middle, low, dense.astype(BF)], axis=1)
            tail = -(-extra.shape[1] // LANES) * LANES
            extra = jnp.pad(extra, ((0, 0), (0, tail - extra.shape[1])))
            payload = jnp.concatenate([payload, extra], axis=1)
        if k == 0:
            tail = -(-experts // LANES) * LANES
            extra = jnp.pad(named, ((0, 0), (0, tail - experts)))
            payload = jnp.concatenate([payload, extra], axis=1)
        rows = ring.gather(payload, "dz")
        rows = ring.gather(rows, "dy")
        rows = ring.gather(rows, "dc")
        rows = rows.reshape(all_tokens, -1)
        if k == 0:
            named_all = rows[:, span : span + experts]
            mine = lax.dynamic_slice_in_dim(named_all, e0, held, axis=1)
            order = jnp.arange(all_tokens, dtype=jnp.int32)
            before = (order[:, None] > order[None, :]).astype(BF)
            rank = jnp.dot(before, mine, preferred_element_type=F32)
            place = jnp.where(mine > 0, rank, -1.0).astype(jnp.int32)
            spots = jnp.arange(room, dtype=jnp.int32)
            chosen = place.T[:, None, :] == spots[None, :, None]
            token_at = jnp.sum(jnp.where(chosen, order, 0), axis=2).reshape(-1)
        if k == AG_CHUNKS - 1:
            extra = rows[:, -tail:].astype(F32)
            share = lax.dynamic_slice_in_dim(extra, e0 + 3, held, axis=1)
            extras = (extra, place, share)
        rows = rows[:, :span]
        sums = expert_up(k, AG_CHUNKS, token_at, rows, gate_proj, up_proj, sums, extras)
    act, comb = sums

    pieces = []
    span = width // RS_CHUNKS
    for k in range(RS_CHUNKS):
        keep, send = expert_down(k, RS_CHUNKS, act, comb, down_proj, ys * reqs * tokens)
        total = ring.scatter([send], keep, "dc") if cores > 1 else keep
        total = total.reshape(ys, reqs * tokens, span)
        total = ring.scatter([total[s].astype(BF) for s in range(1, ys)], total[0], "dy")
        total = total.reshape(reqs, tokens, span)
        total = ring.scatter([total[s].astype(BF) for s in range(1, reqs)], total[0], "dz")
        cut = slice(k * span, (k + 1) * span)
        pieces.append((after_mixer[:, cut].astype(F32) + total).astype(BF))
    return jnp.concatenate(pieces, axis=1).reshape(local_nodes, requests, width)


def solution(mesh):
    in_specs = (
        P(None, ("groups", "req"), "head"),
        P("head", ("groups", "req"), None),
        P("head", ("groups", "req"), None),
        P(None, ("groups", "req"), "head"),
        P("head"),
        P("head"),
        P("head"),
        P(("groups", "req"), "head", None, None),
        P(("groups", "req"), None),
        P("head", None),
        P("head", ("groups", "req"), None),
        P(),
        P(),
        P("head", ("groups", "req"), None),
        P(("head", "req"), None, None),
        P(("head", "req"), None, None),
        P(("head", "req"), None, None),
    )
    out_specs = P("head", ("groups", "req"), None)
    return jax.shard_map(layer, mesh=mesh, in_specs=in_specs, out_specs=out_specs, check_vma=False)
```

```python
import functools
import jax
import jax.numpy as jnp
from jax import lax
from jax.experimental import pallas as pl
from jax.experimental.pallas import tpu as pltpu
from jax.sharding import PartitionSpec as P


BF = jnp.bfloat16
F32 = jnp.float32
AXES = ("head", "req")
LANES = 128
MIX_CHUNKS = 2
AG_CHUNKS = 4
RS_CHUNKS = 4
BATCH = 16


def in_hbm(*arrays):
    return [pltpu.with_memory_space_constraint(a, pltpu.HBM) for a in arrays]


class Ring:
    def __init__(self, heads, reqs):
        self.heads, self.reqs = heads, reqs
        self.cores = 2 if heads % 2 == 0 else 1
        self.ys = heads // self.cores

    def pairs(self, dy=0, dc=0, dz=0, flip=0):
        found = []
        for y in range(self.ys):
            for c in range(self.cores):
                for z in range(self.reqs):
                    there = ((y + dy) % self.ys) * self.cores + (c + dc) % self.cores
                    to = (z ^ flip) if flip else (z + dz) % self.reqs
                    found.append(((y * self.cores + c) * self.reqs + z, there * self.reqs + to))
        return found

    def shift(self, x, **how):
        return lax.ppermute(x, AXES, self.pairs(**how))

    def flips(self):
        if self.reqs & (self.reqs - 1):
            return None
        return [1 << b for b in range(self.reqs.bit_length() - 1)]

    def gather_z(self, x):
        flips = self.flips()
        if flips is None:
            return self.gather(x, "dz")
        for flip in reversed(flips):
            x = jnp.stack([x, self.shift(x, flip=flip)])
        return x

    def scatter_z(self, total):
        flips = self.flips()
        if flips is None:
            parts = [total[s].astype(BF) for s in range(1, self.reqs)]
            return self.scatter(parts, total[0], "dz")
        for flip in flips:
            half = total.shape[0] // 2
            sent = self.shift(total[half:].astype(BF), flip=flip)
            total = total[:half] + sent.astype(F32)
        return total[0]

    def gather(self, x, axis):
        count = {"dc": self.cores, "dy": self.ys, "dz": self.reqs}[axis]
        moved = [self.shift(x, **{axis: s}) for s in range(1, count)]
        return jnp.stack([x] + moved)

    def scatter(self, parts, keep, axis):
        total = keep
        for s, part in enumerate(parts, 1):
            total = total + self.shift(part, **{axis: -s}).astype(F32)
        return total


def prep_body(heads, parents, ids, step_raw, bias, decay, factor, grown, named):
    reqs, nodes = parents.shape
    rows = nodes * reqs
    lane = lax.broadcasted_iota(jnp.int32, (rows, rows), 1)
    row = lax.broadcasted_iota(jnp.int32, (rows, rows), 0)
    hop = jnp.concatenate([parents[:, j : j + 1] for j in range(nodes)], axis=0)
    at = jnp.where(hop >= 0, hop * reqs + lax.broadcasted_iota(jnp.int32, hop.shape, 0) % reqs, -1)
    power = jnp.where(at == lane, 1.0, 0.0)
    reach = jnp.where(row == lane, 1.0, 0.0) + power
    power = power.astype(BF)
    span = 2
    while span * reqs < rows:
        power = jnp.dot(power, power, preferred_element_type=F32).astype(BF)
        reach = reach + jnp.dot(reach.astype(BF), power, preferred_element_type=F32)
        span *= 2
    raw = step_raw[...].reshape(rows, heads) + bias[...]
    step = jnp.maximum(raw, 0.0) + jnp.log1p(jnp.exp(-jnp.abs(raw)))
    rate = -step * decay[...]
    blank = jnp.zeros((rows, rows - heads), F32)
    wide_step = jnp.concatenate([step, blank], axis=1)
    wide_rate = jnp.concatenate([rate, blank], axis=1)
    depth = jnp.dot(
        reach, wide_rate, preferred_element_type=F32, precision=lax.Precision.HIGHEST
    )
    grown[...] = jnp.exp(depth[:, :heads])
    depth_t = depth.T
    step_t = wide_step.T
    linked = reach > 0
    for h in range(heads):
        spread = jnp.where(linked, depth[:, h : h + 1] - depth_t[h : h + 1, :], 0.0)
        factor[h] = jnp.where(linked, jnp.exp(spread) * step_t[h : h + 1, :], 0.0)
    chosen = ids[...].reshape(named.shape[0], ids.shape[2])
    label = lax.broadcasted_iota(jnp.int32, named.shape, 1)
    mask = jnp.zeros(named.shape, F32)
    for k in range(ids.shape[2]):
        mask = jnp.where(chosen[:, k : k + 1] == label, 1.0, mask)
    named[...] = mask.astype(BF)


def prepare(parents, expert_ids, step_raw, step_bias, decay_rate, experts):
    nodes, reqs, heads = step_raw.shape
    rows = nodes * reqs
    tokens = expert_ids.shape[0] * expert_ids.shape[1]
    lanes = -(-experts // LANES) * LANES
    return pl.pallas_call(
        functools.partial(prep_body, heads),
        out_shape=(
            jax.ShapeDtypeStruct((heads, rows, rows), F32),
            jax.ShapeDtypeStruct((rows, heads), F32),
            jax.ShapeDtypeStruct((tokens, lanes), BF),
        ),
        compiler_params=pltpu.CompilerParams(vmem_limit_bytes=16 << 20),
        name="prepare",
    )(
        *in_hbm(
            parents, expert_ids, step_raw, step_bias.reshape(1, heads), decay_rate.reshape(1, heads)
        ),
    )


def gate_body(experts, after, gain, router_t, named, out):
    tokens, width = after.shape
    lanes = out.shape[1]
    wide = after[...].astype(F32)
    scale = lax.rsqrt(jnp.sum(wide * wide, axis=1, keepdims=True) / width + 1e-05)
    normed = (wide * scale * gain[...]).astype(BF)
    logits = lax.dot_general(
        normed, router_t[...], (((1,), (1,)), ((), ())), preferred_element_type=F32
    )
    powered = jnp.where(named[:, :experts] > 0, jnp.exp(logits), 0.0)
    gate = powered / jnp.sum(powered, axis=1, keepdims=True)
    top = scale.astype(BF).astype(F32)
    middle = (scale - top).astype(BF).astype(F32)
    low = scale - top - middle
    lane = lax.broadcasted_iota(jnp.int32, (tokens, lanes - experts), 1)
    head = jnp.where(lane == 0, top, jnp.where(lane == 1, middle, jnp.where(lane == 2, low, 0.0)))
    out[...] = jnp.concatenate([head, gate], axis=1).astype(BF)


def gate_lanes(experts):
    return -(-(experts + 3) // LANES) * LANES


def gates(after_mixer, norm_gain, router, named):
    tokens, width = after_mixer.shape
    experts = router.shape[1]
    return pl.pallas_call(
        functools.partial(gate_body, experts),
        out_shape=jax.ShapeDtypeStruct((tokens, gate_lanes(experts)), BF),
        compiler_params=pltpu.CompilerParams(vmem_limit_bytes=16 << 20),
        name="gates",
    )(after_mixer, norm_gain.reshape(1, width), router.T, named.astype(F32))


def project_blocks(rows, weight, held, arrived, first, near, far):
    near_rows = near.shape[0]
    block = held.shape[2]
    for b in range(held.shape[0]):
        weight_copy(weight, held, arrived, first, b).wait()
        total = jnp.dot(rows, held[b], preferred_element_type=F32)
        near[:, b * block : (b + 1) * block] = total[:near_rows]
        far[:, b * block : (b + 1) * block] = total[near_rows:].astype(BF)


def weight_copy(weight, held, arrived, first, b):
    block = held.shape[2]
    return pltpu.make_async_copy(
        weight.at[:, pl.ds(first + b * block, block)], held.at[b], arrived.at[b]
    )


def front_body(
    heads, first, slot_of, goes_to, early, x, state, factor, grown, skip, weight,
    near, far, mixed_rows, read_rows, write_rows, cache, result, states_held, states_in, held, arrived,
):
    blocks, tokens = early.shape[0], early.shape[1]
    nodes, reqs, columns = x.shape
    rows = nodes * reqs
    size = columns // heads
    states = state.shape[2]
    for r in range(reqs):
        pltpu.make_async_copy(state.at[r], states_held.at[r], states_in.at[r]).start()
    for b in range(held.shape[0]):
        weight_copy(weight, held, arrived, first, b).start()
    for a in range(blocks):
        block = early[slot_of[a]].astype(F32)
        write_rows[a * tokens : (a + 1) * tokens] = block[:, :states]
        read_rows[a * tokens : (a + 1) * tokens] = block[:, states : 2 * states]
    writes = write_rows[...].astype(BF)
    reads = read_rows[...].astype(BF)
    affinity = lax.dot_general(
        reads, writes, (((1,), (1,)), ((), ())), preferred_element_type=F32
    )
    for r in range(reqs):
        pltpu.make_async_copy(state.at[r], states_held.at[r], states_in.at[r]).wait()
        mine = read_rows[pl.ds(r, nodes, stride=reqs), :].astype(BF)
        got = lax.dot_general(
            mine, states_held[r], (((1,), (1,)), ((), ())), preferred_element_type=F32
        )
        for i in range(columns // LANES):
            cache.at[i][pl.ds(r, nodes, stride=reqs), :] = got[:, i * LANES : (i + 1) * LANES]
    values = x[...].reshape(rows, columns)
    pair = 2 * size
    left = lax.broadcasted_iota(jnp.int32, (rows, pair), 1) < size
    for h in range(0, heads, 2):
        cut = slice(h * size, h * size + pair)
        own = values[:, cut]
        one = (factor[h] * affinity).astype(BF)
        two = (factor[h + 1] * affinity).astype(BF)
        zero = jnp.zeros_like(own)
        both = jnp.dot(
            jnp.concatenate([one, two], axis=1),
            jnp.concatenate([jnp.where(left, own, zero), jnp.where(left, zero, own)], axis=0),
            preferred_element_type=F32,
        )
        grow = jnp.where(left, grown[:, h : h + 1], grown[:, h + 1 : h + 2])
        gain = jnp.where(left, skip[:, h : h + 1], skip[:, h + 1 : h + 2])
        both = both + cache[h * size // LANES] * grow + gain * own.astype(F32)
        result[:, cut] = both.astype(BF).astype(F32)
    for s in range(blocks):
        start = pl.multiple_of(goes_to[s] * tokens, tokens)
        mixed_rows[s * tokens : (s + 1) * tokens] = result[pl.ds(start, tokens)].astype(BF)
    project_blocks(mixed_rows[...], weight, held, arrived, first, near, far)


def weight_scratch(columns, span):
    block = min(span, 512)
    return [
        pltpu.VMEM((span // block, columns, block), BF),
        pltpu.SemaphoreType.DMA((span // block,)),
    ]


def front(early, x, state, factor, grown, skip_gain, out_proj, slot_of, goes_to, near_rows, part, parts):
    nodes, reqs, columns = x.shape
    heads = skip_gain.shape[0]
    rows = nodes * reqs
    states = state.shape[3]
    span = out_proj.shape[1] // parts
    state = state.reshape(state.shape[0], columns, states)
    skip = skip_gain.reshape(1, heads)
    x, state, skip, out_proj = in_hbm(x, state, skip, out_proj)
    vmem = pl.BlockSpec(memory_space=pltpu.VMEM)
    hbm = pl.BlockSpec(memory_space=pltpu.HBM)
    return pl.pallas_call(
        functools.partial(front_body, heads, part * span),
        grid_spec=pltpu.PrefetchScalarGridSpec(
            num_scalar_prefetch=2,
            in_specs=[vmem, vmem, hbm, vmem, vmem, vmem, hbm],
            out_specs=(vmem, vmem, vmem),
            scratch_shapes=[
                pltpu.VMEM((rows, states), F32),
                pltpu.VMEM((rows, states), F32),
                pltpu.VMEM((columns // LANES, rows, LANES), F32),
                pltpu.VMEM((rows, columns), F32),
                pltpu.VMEM(state.shape, BF),
                pltpu.SemaphoreType.DMA((reqs,)),
                *weight_scratch(columns, span),
            ],
        ),
        out_shape=(
            jax.ShapeDtypeStruct((near_rows, span), F32),
            jax.ShapeDtypeStruct((rows - near_rows, span), BF),
            jax.ShapeDtypeStruct((rows, columns), BF),
        ),
        compiler_params=pltpu.CompilerParams(vmem_limit_bytes=32 << 20),
        cost_estimate=pl.CostEstimate(
            flops=2 * rows * columns * span, transcendentals=0, bytes_accessed=2 * columns * span
        ),
        name="front",
    )(slot_of, goes_to, early, x, state, factor, grown, skip, out_proj)


def project_body(first, rows, weight, near, far, held, arrived):
    for b in range(held.shape[0]):
        weight_copy(weight, held, arrived, first, b).start()
    project_blocks(rows[...], weight, held, arrived, first, near, far)


def project(rows, out_proj, near_rows, part, parts):
    count, columns = rows.shape
    span = out_proj.shape[1] // parts
    vmem = pl.BlockSpec(memory_space=pltpu.VMEM)
    return pl.pallas_call(
        functools.partial(project_body, part * span),
        in_specs=[vmem, pl.BlockSpec(memory_space=pltpu.HBM)],
        out_specs=(vmem, vmem),
        out_shape=(
            jax.ShapeDtypeStruct((near_rows, span), F32),
            jax.ShapeDtypeStruct((count - near_rows, span), BF),
        ),
        scratch_shapes=weight_scratch(columns, span),
        compiler_params=pltpu.CompilerParams(vmem_limit_bytes=16 << 20),
        cost_estimate=pl.CostEstimate(
            flops=2 * count * columns * span, transcendentals=0, bytes_accessed=2 * columns * span
        ),
        name="project",
    )(rows, *in_hbm(out_proj))


def up_body(first, last, begin, token_at, x, wg, wu, *rest):
    rest = list(rest)
    if not first:
        gin, uin = rest.pop(0), rest.pop(0)
    if last:
        extra, spot, share = rest.pop(0), rest.pop(0), rest.pop(0)
    if last:
        act_out, comb_out, spread, picked, gates_held, ups_held, arrived, scales = rest
    else:
        gout, uout, spread, picked, gates_held, ups_held, arrived = rest
    q = pl.program_id(0)
    tokens, width = x.shape
    tall = width // LANES
    slots = picked.shape[0] // tall

    def copies(e):
        cut = pl.ds(begin, width)
        return (
            pltpu.make_async_copy(wg.at[e, cut], gates_held.at[e], arrived.at[0, e]),
            pltpu.make_async_copy(wu.at[e, cut], ups_held.at[e], arrived.at[1, e]),
        )

    @pl.when(q == 0)
    def _():
        for e in range(gates_held.shape[0]):
            for copy in copies(e):
                copy.start()
        for i in range(tall):
            spread[pl.ds(i, tokens, stride=tall), :] = x[:, i * LANES : (i + 1) * LANES].astype(F32)

    for c in range(0, slots, BATCH):
        at = [token_at[q * slots + c + i] for i in range(BATCH)]
        got = [spread[pl.ds(pl.multiple_of(t * tall, tall), tall)] for t in at]
        picked[c * tall : (c + BATCH) * tall] = jnp.concatenate(got, axis=0)
        if last:
            got = [extra[pl.ds(t, 1)] for t in at]
            for i in range(BATCH):
                scales[c + i : c + i + 1] = got[i]
    rows = jnp.concatenate(
        [picked[pl.ds(i, slots, stride=tall), :].astype(BF) for i in range(tall)], axis=1
    )
    for copy in copies(q):
        copy.wait()
    gated = jnp.dot(rows, gates_held[q], preferred_element_type=F32)
    lifted = jnp.dot(rows, ups_held[q], preferred_element_type=F32)
    if not first:
        gated = gated + gin[0]
        lifted = lifted + uin[0]
    if not last:
        gout[0] = gated
        uout[0] = lifted
        return
    scale = scales[:, 0:1] + scales[:, 1:2] + scales[:, 2:3]
    gated = gated * scale
    lifted = lifted * scale
    act_out[0] = (gated / (1.0 + jnp.exp(-gated)) * lifted).astype(BF)
    lane = lax.broadcasted_iota(jnp.int32, (tokens, slots), 1)
    column = lax.broadcasted_iota(jnp.int32, spot.shape, 1)
    own_spot = jnp.sum(jnp.where(column == q, spot[...], 0), axis=1, keepdims=True)
    own_share = jnp.sum(jnp.where(column == q, share[...], 0.0), axis=1, keepdims=True)
    comb_out[...] = jnp.where(lane == own_spot, own_share, 0.0).astype(BF)


def expert_up(k, chunks, token_at, x, gate_proj, up_proj, sums, extras):
    held = gate_proj.shape[0]
    tokens, width = x.shape
    slots = token_at.shape[0] // held
    units = gate_proj.shape[2]
    first, last = k == 0, k == chunks - 1
    per_expert = lambda *tail: pl.BlockSpec((1,) + tail, lambda q, *_: (q, 0, 0))
    whole = lambda a: pl.BlockSpec(a.shape, lambda q, *_: (0, 0))
    weight = pl.BlockSpec(memory_space=pltpu.HBM)
    in_specs = [whole(x), weight, weight]
    args = [x, *in_hbm(gate_proj, up_proj)]
    scratch = [
        pltpu.VMEM((tokens * width // LANES, LANES), F32),
        pltpu.VMEM((slots * width // LANES, LANES), F32),
        pltpu.VMEM((held, width, units), BF),
        pltpu.VMEM((held, width, units), BF),
        pltpu.SemaphoreType.DMA((2, held)),
    ]
    if not first:
        in_specs += [per_expert(slots, units)] * 2
        args += list(sums)
    if last:
        in_specs += [whole(a) for a in extras]
        args += list(extras)
        out_shape = (
            jax.ShapeDtypeStruct((held, slots, units), BF),
            jax.ShapeDtypeStruct((tokens, held * slots), BF),
        )
        out_specs = (per_expert(slots, units), pl.BlockSpec((tokens, slots), lambda q, *_: (0, q)))
        scratch.append(pltpu.VMEM((slots, extras[0].shape[1]), F32))
    else:
        out_shape = (jax.ShapeDtypeStruct((held, slots, units), F32),) * 2
        out_specs = (per_expert(slots, units),) * 2
    return pl.pallas_call(
        functools.partial(up_body, first, last, k * width),
        grid_spec=pltpu.PrefetchScalarGridSpec(
            num_scalar_prefetch=1,
            grid=(held,),
            in_specs=in_specs,
            out_specs=out_specs,
            scratch_shapes=scratch,
        ),
        out_shape=out_shape,
        compiler_params=pltpu.CompilerParams(vmem_limit_bytes=48 << 20),
        cost_estimate=pl.CostEstimate(
            flops=4 * held * slots * width * units,
            transcendentals=0,
            bytes_accessed=4 * held * width * units,
        ),
    )(token_at, *args)


def down_body(begin, act, comb, wd, keep, send, halves, held_rows, arrived):
    held, slots, _ = act.shape
    width = keep.shape[1]

    def copy(q):
        return pltpu.make_async_copy(
            wd.at[q, :, pl.ds(begin, width)], held_rows.at[q], arrived.at[q]
        )

    for q in range(held):
        copy(q).start()
    for q in range(held):
        copy(q).wait()
        halves[q * slots : (q + 1) * slots] = jnp.dot(
            act[q], held_rows[q], preferred_element_type=F32
        ).astype(BF)
    kept = keep.shape[0]
    block = min(width, 256)
    for j in range(0, width, block):
        cut = slice(j, j + block)
        total = jnp.dot(comb[...], halves[:, cut], preferred_element_type=F32)
        keep[:, cut] = total[:kept]
        send[:, cut] = total[kept:].astype(BF)


def expert_down(k, chunks, act, comb, down_proj, kept):
    held, slots, units = act.shape
    tokens = comb.shape[0]
    width = down_proj.shape[2] // chunks
    vmem = pl.BlockSpec(memory_space=pltpu.VMEM)
    return pl.pallas_call(
        functools.partial(down_body, k * width),
        in_specs=[vmem, vmem, pl.BlockSpec(memory_space=pltpu.HBM)],
        out_specs=(vmem, vmem),
        out_shape=(
            jax.ShapeDtypeStruct((kept, width), F32),
            jax.ShapeDtypeStruct((tokens - kept, width), BF),
        ),
        scratch_shapes=[
            pltpu.VMEM((held * slots, width), BF),
            pltpu.VMEM((held, units, width), BF),
            pltpu.SemaphoreType.DMA((held,)),
        ],
        compiler_params=pltpu.CompilerParams(vmem_limit_bytes=48 << 20),
        cost_estimate=pl.CostEstimate(
            flops=2 * held * slots * width * (tokens + units),
            transcendentals=0,
            bytes_accessed=2 * held * width * units,
        ),
    )(act, comb, *in_hbm(down_proj))


def layer(
    ssm_input,
    write_vec,
    read_vec,
    step_raw,
    step_bias,
    decay_rate,
    skip_gain,
    cache_state,
    parents,
    out_proj,
    residual,
    norm_gain,
    router,
    expert_ids,
    gate_proj,
    up_proj,
    down_proj,
):
    _, requests, _ = ssm_input.shape
    local_nodes, _, width = residual.shape
    tokens = local_nodes * requests
    topk = expert_ids.shape[2]
    experts = router.shape[1]
    held = gate_proj.shape[0]
    ring = Ring(lax.axis_size("head"), lax.axis_size("req"))
    cores, ys, reqs = ring.cores, ring.ys, ring.reqs
    head_at = lax.axis_index("head")
    y_at, c_at = head_at // cores, head_at % cores
    device = head_at * reqs + lax.axis_index("req")
    e0 = (device * held) % experts

    states = write_vec.shape[2]
    early = jnp.concatenate(
        [write_vec.reshape(tokens, states), read_vec.reshape(tokens, states)], axis=1
    )
    early = ring.gather(ring.gather(early, "dc"), "dy")
    early = early.reshape(ys * cores, tokens, -1)
    absolute = jnp.arange(ys * cores, dtype=jnp.int32)
    slot_of = ((y_at - absolute // cores) % ys) * cores + (c_at - absolute % cores) % cores
    slots = jnp.arange(cores * ys, dtype=jnp.int32)
    goes_to = ((y_at - slots % ys) % ys) * cores + (c_at - slots // ys) % cores
    factor, grown, named = prepare(parents, expert_ids, step_raw, step_bias, decay_rate, experts)
    near_rows = ys * tokens

    all_tokens = cores * ys * reqs * tokens
    capacity = 2 * tokens * topk // (experts + experts // 4)
    room = capacity * cores * ys * reqs

    rows_left = residual.reshape(tokens, width)
    mixes = []
    part_span = width // MIX_CHUNKS
    for m in range(MIX_CHUNKS):
        cut = slice(m * part_span, (m + 1) * part_span)
        if m == 0:
            mixed, away, mixed_rows = front(
                early, ssm_input, cache_state, factor, grown, skip_gain, out_proj,
                slot_of, goes_to, near_rows, m, MIX_CHUNKS,
            )
        else:
            mixed, away = project(mixed_rows, out_proj, near_rows, m, MIX_CHUNKS)
        if cores > 1:
            mixed = ring.scatter([away], mixed, "dc")
        mixed = mixed.reshape(ys, tokens, part_span)
        mixed = ring.scatter([mixed[s].astype(BF) for s in range(1, ys)], mixed[0], "dy")
        mixes.append((rows_left[:, cut].astype(F32) + mixed).astype(BF))
    span = width // AG_CHUNKS
    after_mixer = jnp.concatenate(mixes, axis=1)
    sums = None
    for k in range(AG_CHUNKS):
        cut = slice(k * span, (k + 1) * span)
        m = k * MIX_CHUNKS // AG_CHUNKS
        local = slice(k * span - m * part_span, (k + 1) * span - m * part_span)
        payload = (mixes[m][:, local].astype(F32) * norm_gain[cut]).astype(BF)
        extras = None
        if k == AG_CHUNKS - 1:
            extra = gates(after_mixer, norm_gain, router, named)
            payload = jnp.concatenate([payload, extra], axis=1)
        if k == 0:
            payload = jnp.concatenate([payload, named], axis=1)
        rows = ring.gather_z(payload)
        rows = ring.gather(rows, "dy")
        rows = ring.gather(rows, "dc")
        rows = rows.reshape(all_tokens, -1)
        if k == 0:
            named_all = rows[:, span : span + experts]
            mine = lax.dynamic_slice_in_dim(named_all, e0, held, axis=1)
            order = jnp.arange(all_tokens, dtype=jnp.int32)
            before = (order[:, None] > order[None, :]).astype(BF)
            rank = jnp.dot(before, mine, preferred_element_type=F32)
            place = jnp.where(mine > 0, rank, -1.0).astype(jnp.int32)
            spots = jnp.arange(room, dtype=jnp.int32)
            chosen = place.T[:, None, :] == spots[None, :, None]
            token_at = jnp.sum(jnp.where(chosen, order, 0), axis=2).reshape(-1)
        if k == AG_CHUNKS - 1:
            extra = rows[:, rows.shape[1] - gate_lanes(experts) :].astype(F32)
            share = lax.dynamic_slice_in_dim(
                extra, e0 + extra.shape[1] - experts, held, axis=1
            )
            extras = (extra, place, share)
        rows = rows[:, :span]
        sums = expert_up(k, AG_CHUNKS, token_at, rows, gate_proj, up_proj, sums, extras)
    act, comb = sums

    pieces = []
    span = width // RS_CHUNKS
    for k in range(RS_CHUNKS):
        keep, send = expert_down(k, RS_CHUNKS, act, comb, down_proj, ys * reqs * tokens)
        total = ring.scatter([send], keep, "dc") if cores > 1 else keep
        total = total.reshape(ys, reqs * tokens, span)
        total = ring.scatter([total[s].astype(BF) for s in range(1, ys)], total[0], "dy")
        total = ring.scatter_z(total.reshape(reqs, tokens, span))
        cut = slice(k * span, (k + 1) * span)
        pieces.append((after_mixer[:, cut].astype(F32) + total).astype(BF))
    return jnp.concatenate(pieces, axis=1).reshape(local_nodes, requests, width)


def solution(mesh):
    in_specs = (
        P(None, ("groups", "req"), "head"),
        P("head", ("groups", "req"), None),
        P("head", ("groups", "req"), None),
        P(None, ("groups", "req"), "head"),
        P("head"),
        P("head"),
        P("head"),
        P(("groups", "req"), "head", None, None),
        P(("groups", "req"), None),
        P("head", None),
        P("head", ("groups", "req"), None),
        P(),
        P(),
        P("head", ("groups", "req"), None),
        P(("head", "req"), None, None),
        P(("head", "req"), None, None),
        P(("head", "req"), None, None),
    )
    out_specs = P("head", ("groups", "req"), None)
    return jax.shard_map(layer, mesh=mesh, in_specs=in_specs, out_specs=out_specs, check_vma=False)
```

```python
import functools
import jax
import jax.numpy as jnp
from jax import lax
from jax.experimental import pallas as pl
from jax.experimental.pallas import tpu as pltpu
from jax.sharding import PartitionSpec as P


BF = jnp.bfloat16
F32 = jnp.float32
AXES = ("head", "req")
LANES = 128
MIX_CHUNKS = 2
AG_CHUNKS = 4
RS_CHUNKS = 4
BATCH = 16


def in_hbm(*arrays):
    return [pltpu.with_memory_space_constraint(a, pltpu.HBM) for a in arrays]


class Ring:
    def __init__(self, heads, reqs):
        self.heads, self.reqs = heads, reqs
        self.cores = 2 if heads % 2 == 0 else 1
        self.ys = heads // self.cores

    def pairs(self, dy=0, dc=0, dz=0, flip=0):
        found = []
        for y in range(self.ys):
            for c in range(self.cores):
                for z in range(self.reqs):
                    there = ((y + dy) % self.ys) * self.cores + (c + dc) % self.cores
                    to = (z ^ flip) if flip else (z + dz) % self.reqs
                    found.append(((y * self.cores + c) * self.reqs + z, there * self.reqs + to))
        return found

    def shift(self, x, **how):
        return lax.ppermute(x, AXES, self.pairs(**how))

    def flips(self):
        if self.reqs & (self.reqs - 1):
            return None
        return [1 << b for b in range(self.reqs.bit_length() - 1)]

    def gather_z(self, x):
        flips = self.flips()
        if flips is None:
            return self.gather(x, "dz")
        for flip in reversed(flips):
            x = jnp.stack([x, self.shift(x, flip=flip)])
        return x

    def scatter_z(self, total):
        flips = self.flips()
        if flips is None:
            parts = [total[s].astype(BF) for s in range(1, self.reqs)]
            return self.scatter(parts, total[0], "dz")
        for flip in flips:
            half = total.shape[0] // 2
            sent = self.shift(total[half:].astype(BF), flip=flip)
            total = total[:half] + sent.astype(F32)
        return total[0]

    def gather(self, x, axis):
        count = {"dc": self.cores, "dy": self.ys, "dz": self.reqs}[axis]
        moved = [self.shift(x, **{axis: s}) for s in range(1, count)]
        return jnp.stack([x] + moved)

    def scatter(self, parts, keep, axis):
        total = keep
        for s, part in enumerate(parts, 1):
            total = total + self.shift(part, **{axis: -s}).astype(F32)
        return total


def prep_body(heads, parents, ids, step_raw, bias, decay, factor, grown, named):
    reqs, nodes = parents.shape
    rows = nodes * reqs
    lane = lax.broadcasted_iota(jnp.int32, (rows, rows), 1)
    row = lax.broadcasted_iota(jnp.int32, (rows, rows), 0)
    hop = jnp.concatenate([parents[:, j : j + 1] for j in range(nodes)], axis=0)
    at = jnp.where(hop >= 0, hop * reqs + lax.broadcasted_iota(jnp.int32, hop.shape, 0) % reqs, -1)
    power = jnp.where(at == lane, 1.0, 0.0)
    reach = jnp.where(row == lane, 1.0, 0.0) + power
    power = power.astype(BF)
    span = 2
    while span * reqs < rows:
        power = jnp.dot(power, power, preferred_element_type=F32).astype(BF)
        reach = reach + jnp.dot(reach.astype(BF), power, preferred_element_type=F32)
        span *= 2
    raw = step_raw[...].reshape(rows, heads) + bias[...]
    step = jnp.maximum(raw, 0.0) + jnp.log1p(jnp.exp(-jnp.abs(raw)))
    rate = -step * decay[...]
    blank = jnp.zeros((rows, rows - heads), F32)
    wide_step = jnp.concatenate([step, blank], axis=1)
    wide_rate = jnp.concatenate([rate, blank], axis=1)
    depth = jnp.dot(
        reach, wide_rate, preferred_element_type=F32, precision=lax.Precision.HIGHEST
    )
    grown[...] = jnp.exp(depth[:, :heads])
    depth_t = depth.T
    step_t = wide_step.T
    linked = reach > 0
    for h in range(heads):
        spread = jnp.where(linked, depth[:, h : h + 1] - depth_t[h : h + 1, :], 0.0)
        factor[h] = jnp.where(linked, jnp.exp(spread) * step_t[h : h + 1, :], 0.0)
    chosen = ids[...].reshape(named.shape[0], ids.shape[2])
    label = lax.broadcasted_iota(jnp.int32, named.shape, 1)
    mask = jnp.zeros(named.shape, F32)
    for k in range(ids.shape[2]):
        mask = jnp.where(chosen[:, k : k + 1] == label, 1.0, mask)
    named[...] = mask.astype(BF)


def prepare(parents, expert_ids, step_raw, step_bias, decay_rate, experts):
    nodes, reqs, heads = step_raw.shape
    rows = nodes * reqs
    tokens = expert_ids.shape[0] * expert_ids.shape[1]
    lanes = -(-experts // LANES) * LANES
    return pl.pallas_call(
        functools.partial(prep_body, heads),
        out_shape=(
            jax.ShapeDtypeStruct((heads, rows, rows), F32),
            jax.ShapeDtypeStruct((rows, heads), F32),
            jax.ShapeDtypeStruct((tokens, lanes), BF),
        ),
        compiler_params=pltpu.CompilerParams(vmem_limit_bytes=16 << 20),
        name="prepare",
    )(
        *in_hbm(
            parents, expert_ids, step_raw, step_bias.reshape(1, heads), decay_rate.reshape(1, heads)
        ),
    )


def gate_body(experts, after, gain, router_t, named, out):
    tokens, width = after.shape
    lanes = out.shape[1]
    wide = after[...].astype(F32)
    scale = lax.rsqrt(jnp.sum(wide * wide, axis=1, keepdims=True) / width + 1e-05)
    normed = (wide * scale * gain[...]).astype(BF)
    logits = lax.dot_general(
        normed, router_t[...], (((1,), (1,)), ((), ())), preferred_element_type=F32
    )
    powered = jnp.where(named[:, :experts] > 0, jnp.exp(logits), 0.0)
    gate = powered / jnp.sum(powered, axis=1, keepdims=True)
    top = scale.astype(BF).astype(F32)
    middle = (scale - top).astype(BF).astype(F32)
    low = scale - top - middle
    lane = lax.broadcasted_iota(jnp.int32, (tokens, lanes - experts), 1)
    head = jnp.where(lane == 0, top, jnp.where(lane == 1, middle, jnp.where(lane == 2, low, 0.0)))
    out[...] = jnp.concatenate([head, gate], axis=1).astype(BF)


def gate_lanes(experts):
    return -(-(experts + 3) // LANES) * LANES


def gates(after_mixer, norm_gain, router, named):
    tokens, width = after_mixer.shape
    experts = router.shape[1]
    return pl.pallas_call(
        functools.partial(gate_body, experts),
        out_shape=jax.ShapeDtypeStruct((tokens, gate_lanes(experts)), BF),
        compiler_params=pltpu.CompilerParams(vmem_limit_bytes=16 << 20),
        name="gates",
    )(after_mixer, norm_gain.reshape(1, width), router.T, named.astype(F32))


def project_blocks(rows, weight, held, arrived, first, near, far):
    near_rows = near.shape[0]
    block = held.shape[2]
    for b in range(held.shape[0]):
        weight_copy(weight, held, arrived, first, b).wait()
        total = jnp.dot(rows, held[b], preferred_element_type=F32)
        near[:, b * block : (b + 1) * block] = total[:near_rows]
        far[:, b * block : (b + 1) * block] = total[near_rows:].astype(BF)


def weight_copy(weight, held, arrived, first, b):
    block = held.shape[2]
    return pltpu.make_async_copy(
        weight.at[:, pl.ds(first + b * block, block)], held.at[b], arrived.at[b]
    )


def front_body(
    heads, first, slot_of, goes_to, early, x, state, factor, grown, skip, weight,
    near, far, mixed_rows, read_rows, write_rows, cache, result, states_held, states_in, held, arrived,
):
    blocks, tokens = early.shape[0], early.shape[1]
    nodes, reqs, columns = x.shape
    rows = nodes * reqs
    size = columns // heads
    states = state.shape[2]
    for r in range(reqs):
        pltpu.make_async_copy(state.at[r], states_held.at[r], states_in.at[r]).start()
    for b in range(held.shape[0]):
        weight_copy(weight, held, arrived, first, b).start()
    for a in range(blocks):
        block = early[slot_of[a]].astype(F32)
        write_rows[a * tokens : (a + 1) * tokens] = block[:, :states]
        read_rows[a * tokens : (a + 1) * tokens] = block[:, states : 2 * states]
    writes = write_rows[...].astype(BF)
    reads = read_rows[...].astype(BF)
    affinity = lax.dot_general(
        reads, writes, (((1,), (1,)), ((), ())), preferred_element_type=F32
    )
    for r in range(reqs):
        pltpu.make_async_copy(state.at[r], states_held.at[r], states_in.at[r]).wait()
        mine = read_rows[pl.ds(r, nodes, stride=reqs), :].astype(BF)
        got = lax.dot_general(
            mine, states_held[r], (((1,), (1,)), ((), ())), preferred_element_type=F32
        )
        for i in range(columns // LANES):
            cache.at[i][pl.ds(r, nodes, stride=reqs), :] = got[:, i * LANES : (i + 1) * LANES]
    values = x[...].reshape(rows, columns)
    pair = 2 * size
    left = lax.broadcasted_iota(jnp.int32, (rows, pair), 1) < size
    for h in range(0, heads, 2):
        cut = slice(h * size, h * size + pair)
        own = values[:, cut]
        one = (factor[h] * affinity).astype(BF)
        two = (factor[h + 1] * affinity).astype(BF)
        zero = jnp.zeros_like(own)
        both = jnp.dot(
            jnp.concatenate([one, two], axis=1),
            jnp.concatenate([jnp.where(left, own, zero), jnp.where(left, zero, own)], axis=0),
            preferred_element_type=F32,
        )
        grow = jnp.where(left, grown[:, h : h + 1], grown[:, h + 1 : h + 2])
        gain = jnp.where(left, skip[:, h : h + 1], skip[:, h + 1 : h + 2])
        both = both + cache[h * size // LANES] * grow + gain * own.astype(F32)
        result[:, cut] = both.astype(BF).astype(F32)
    for s in range(blocks):
        start = pl.multiple_of(goes_to[s] * tokens, tokens)
        mixed_rows[s * tokens : (s + 1) * tokens] = result[pl.ds(start, tokens)].astype(BF)
    project_blocks(mixed_rows[...], weight, held, arrived, first, near, far)


def weight_scratch(columns, span):
    block = min(span, 512)
    return [
        pltpu.VMEM((span // block, columns, block), BF),
        pltpu.SemaphoreType.DMA((span // block,)),
    ]


def front(early, x, state, factor, grown, skip_gain, out_proj, slot_of, goes_to, near_rows, part, parts):
    nodes, reqs, columns = x.shape
    heads = skip_gain.shape[0]
    rows = nodes * reqs
    states = state.shape[3]
    span = out_proj.shape[1] // parts
    state = state.reshape(state.shape[0], columns, states)
    skip = skip_gain.reshape(1, heads)
    x, state, skip, out_proj = in_hbm(x, state, skip, out_proj)
    vmem = pl.BlockSpec(memory_space=pltpu.VMEM)
    hbm = pl.BlockSpec(memory_space=pltpu.HBM)
    return pl.pallas_call(
        functools.partial(front_body, heads, part * span),
        grid_spec=pltpu.PrefetchScalarGridSpec(
            num_scalar_prefetch=2,
            in_specs=[vmem, vmem, hbm, vmem, vmem, vmem, hbm],
            out_specs=(vmem, vmem, vmem),
            scratch_shapes=[
                pltpu.VMEM((rows, states), F32),
                pltpu.VMEM((rows, states), F32),
                pltpu.VMEM((columns // LANES, rows, LANES), F32),
                pltpu.VMEM((rows, columns), F32),
                pltpu.VMEM(state.shape, BF),
                pltpu.SemaphoreType.DMA((reqs,)),
                *weight_scratch(columns, span),
            ],
        ),
        out_shape=(
            jax.ShapeDtypeStruct((near_rows, span), F32),
            jax.ShapeDtypeStruct((rows - near_rows, span), BF),
            jax.ShapeDtypeStruct((rows, columns), BF),
        ),
        compiler_params=pltpu.CompilerParams(vmem_limit_bytes=16 << 20),
        cost_estimate=pl.CostEstimate(
            flops=2 * rows * columns * span, transcendentals=0, bytes_accessed=2 * columns * span
        ),
        name="front",
    )(slot_of, goes_to, early, x, state, factor, grown, skip, out_proj)


def project_body(first, rows, weight, near, far, held, arrived):
    for b in range(held.shape[0]):
        weight_copy(weight, held, arrived, first, b).start()
    project_blocks(rows[...], weight, held, arrived, first, near, far)


def project(rows, out_proj, near_rows, part, parts):
    count, columns = rows.shape
    span = out_proj.shape[1] // parts
    vmem = pl.BlockSpec(memory_space=pltpu.VMEM)
    return pl.pallas_call(
        functools.partial(project_body, part * span),
        in_specs=[vmem, pl.BlockSpec(memory_space=pltpu.HBM)],
        out_specs=(vmem, vmem),
        out_shape=(
            jax.ShapeDtypeStruct((near_rows, span), F32),
            jax.ShapeDtypeStruct((count - near_rows, span), BF),
        ),
        scratch_shapes=weight_scratch(columns, span),
        compiler_params=pltpu.CompilerParams(vmem_limit_bytes=10 << 20),
        cost_estimate=pl.CostEstimate(
            flops=2 * count * columns * span, transcendentals=0, bytes_accessed=2 * columns * span
        ),
        name="project",
    )(rows, *in_hbm(out_proj))


def up_body(first, last, begin, pieces, width, token_at, *rest):
    rest = list(rest)
    xs = [rest.pop(0) for _ in range(pieces)]
    wg, wu = rest.pop(0), rest.pop(0)
    if not first:
        gin, uin = rest.pop(0), rest.pop(0)
    if last:
        extra, spot, share = rest.pop(0), rest.pop(0), rest.pop(0)
        act_out, comb_out, spread, picked, gates_held, ups_held, arrived, scales = rest
    else:
        gout, uout, spread, picked, gates_held, ups_held, arrived = rest
    held = gates_held.shape[0]
    tall = width // LANES
    slots = picked.shape[0] // tall

    def copies(e):
        cut = pl.ds(begin, width)
        return (
            pltpu.make_async_copy(wg.at[e, cut], gates_held.at[e], arrived.at[0, e]),
            pltpu.make_async_copy(wu.at[e, cut], ups_held.at[e], arrived.at[1, e]),
        )

    for e in range(held):
        for copy in copies(e):
            copy.start()
    done = 0
    for x in xs:
        tokens = x.shape[0]
        for i in range(tall):
            spread[pl.ds(done * tall + i, tokens, stride=tall), :] = x[
                :, i * LANES : (i + 1) * LANES
            ].astype(F32)
        done += tokens

    def visit(q, carry):
        for c in range(0, slots, BATCH):
            at = [token_at[q * slots + c + i] for i in range(BATCH)]
            got = [spread[pl.ds(pl.multiple_of(t * tall, tall), tall)] for t in at]
            picked[c * tall : (c + BATCH) * tall] = jnp.concatenate(got, axis=0)
            if last:
                got = [extra[pl.ds(t, 1)] for t in at]
                for i in range(BATCH):
                    scales[c + i : c + i + 1] = got[i]
        rows = jnp.concatenate(
            [picked[pl.ds(i, slots, stride=tall), :].astype(BF) for i in range(tall)], axis=1
        )
        for copy in copies(q):
            copy.wait()
        gated = jnp.dot(rows, gates_held[q], preferred_element_type=F32)
        lifted = jnp.dot(rows, ups_held[q], preferred_element_type=F32)
        if not first:
            gated = gated + gin[q]
            lifted = lifted + uin[q]
        if not last:
            gout[q] = gated
            uout[q] = lifted
            return carry
        scale = scales[:, 0:1] + scales[:, 1:2] + scales[:, 2:3]
        gated = gated * scale
        lifted = lifted * scale
        act_out[q] = (gated / (1.0 + jnp.exp(-gated)) * lifted).astype(BF)
        lane = lax.broadcasted_iota(jnp.int32, (done, slots), 1)
        column = lax.broadcasted_iota(jnp.int32, spot.shape, 1)
        own_spot = jnp.sum(jnp.where(column == q, spot[...], 0), axis=1, keepdims=True)
        own_share = jnp.sum(jnp.where(column == q, share[...], 0.0), axis=1, keepdims=True)
        comb_out[q] = jnp.where(lane == own_spot, own_share, 0.0).astype(BF)
        return carry

    lax.fori_loop(0, held, visit, 0)


def expert_up(k, chunks, token_at, xs, gate_proj, up_proj, sums, extras):
    held = gate_proj.shape[0]
    width = gate_proj.shape[1] // chunks
    tokens = sum(x.shape[0] for x in xs)
    slots = token_at.shape[0] // held
    units = gate_proj.shape[2]
    first, last = k == 0, k == chunks - 1
    vmem = pl.BlockSpec(memory_space=pltpu.VMEM)
    hbm = pl.BlockSpec(memory_space=pltpu.HBM)
    in_specs = [pl.BlockSpec(memory_space=pltpu.SMEM)] + [vmem] * len(xs) + [hbm, hbm]
    args = [token_at, *xs, *in_hbm(gate_proj, up_proj)]
    scratch = [
        pltpu.VMEM((tokens * width // LANES, LANES), F32),
        pltpu.VMEM((slots * width // LANES, LANES), F32),
        pltpu.VMEM((held, width, units), BF),
        pltpu.VMEM((held, width, units), BF),
        pltpu.SemaphoreType.DMA((2, held)),
    ]
    aliases = {}
    if not first:
        if not last:
            aliases = {len(args): 0, len(args) + 1: 1}
        in_specs += [vmem] * 2
        args += list(sums)
    if last:
        in_specs += [vmem] * 3
        args += list(extras)
        out_shape = (
            jax.ShapeDtypeStruct((held, slots, units), BF),
            jax.ShapeDtypeStruct((held, tokens, slots), BF),
        )
        scratch.append(pltpu.VMEM((slots, extras[0].shape[1]), F32))
    else:
        out_shape = (jax.ShapeDtypeStruct((held, slots, units), F32),) * 2
    return pl.pallas_call(
        functools.partial(up_body, first, last, k * width, len(xs), width),
        in_specs=in_specs,
        out_specs=(vmem, vmem),
        out_shape=out_shape,
        scratch_shapes=scratch,
        input_output_aliases=aliases,
        compiler_params=pltpu.CompilerParams(vmem_limit_bytes=4 * held * width * units + 4 * tokens * width + (6 << 20)),
        cost_estimate=pl.CostEstimate(
            flops=4 * held * slots * width * units,
            transcendentals=0,
            bytes_accessed=4 * held * width * units,
        ),
    )(*args)


def down_body(begin, act, comb, wd, keep, send, halves, held_rows, arrived):
    held, slots, _ = act.shape
    width = keep.shape[1]

    def copy(q):
        return pltpu.make_async_copy(
            wd.at[q, :, pl.ds(begin, width)], held_rows.at[q], arrived.at[q]
        )

    for q in range(held):
        copy(q).start()
    for q in range(held):
        copy(q).wait()
        halves[q * slots : (q + 1) * slots] = jnp.dot(
            act[q], held_rows[q], preferred_element_type=F32
        ).astype(BF)
    kept = keep.shape[0]
    comb_rows = jnp.concatenate([comb[q] for q in range(held)], axis=1)
    block = min(width, 256)
    for j in range(0, width, block):
        cut = slice(j, j + block)
        total = jnp.dot(comb_rows, halves[:, cut], preferred_element_type=F32)
        keep[:, cut] = total[:kept]
        send[:, cut] = total[kept:].astype(BF)


def expert_down(k, chunks, act, comb, down_proj, kept):
    held, slots, units = act.shape
    tokens = comb.shape[1]
    width = down_proj.shape[2] // chunks
    vmem = pl.BlockSpec(memory_space=pltpu.VMEM)
    return pl.pallas_call(
        functools.partial(down_body, k * width),
        in_specs=[vmem, vmem, pl.BlockSpec(memory_space=pltpu.HBM)],
        out_specs=(vmem, vmem),
        out_shape=(
            jax.ShapeDtypeStruct((kept, width), F32),
            jax.ShapeDtypeStruct((tokens - kept, width), BF),
        ),
        scratch_shapes=[
            pltpu.VMEM((held * slots, width), BF),
            pltpu.VMEM((held, units, width), BF),
            pltpu.SemaphoreType.DMA((held,)),
        ],
        compiler_params=pltpu.CompilerParams(vmem_limit_bytes=2 * held * width * (units + slots) + (8 << 20)),
        cost_estimate=pl.CostEstimate(
            flops=2 * held * slots * width * (tokens + units),
            transcendentals=0,
            bytes_accessed=2 * held * width * units,
        ),
    )(act, comb, *in_hbm(down_proj))


def layer(
    ssm_input,
    write_vec,
    read_vec,
    step_raw,
    step_bias,
    decay_rate,
    skip_gain,
    cache_state,
    parents,
    out_proj,
    residual,
    norm_gain,
    router,
    expert_ids,
    gate_proj,
    up_proj,
    down_proj,
):
    _, requests, _ = ssm_input.shape
    local_nodes, _, width = residual.shape
    tokens = local_nodes * requests
    topk = expert_ids.shape[2]
    experts = router.shape[1]
    held = gate_proj.shape[0]
    ring = Ring(lax.axis_size("head"), lax.axis_size("req"))
    cores, ys, reqs = ring.cores, ring.ys, ring.reqs
    head_at = lax.axis_index("head")
    y_at, c_at = head_at // cores, head_at % cores
    device = head_at * reqs + lax.axis_index("req")
    e0 = (device * held) % experts

    states = write_vec.shape[2]
    early = jnp.concatenate(
        [write_vec.reshape(tokens, states), read_vec.reshape(tokens, states)], axis=1
    )
    early = ring.gather(ring.gather(early, "dc"), "dy")
    early = early.reshape(ys * cores, tokens, -1)
    absolute = jnp.arange(ys * cores, dtype=jnp.int32)
    slot_of = ((y_at - absolute // cores) % ys) * cores + (c_at - absolute % cores) % cores
    slots = jnp.arange(cores * ys, dtype=jnp.int32)
    goes_to = ((y_at - slots % ys) % ys) * cores + (c_at - slots // ys) % cores
    factor, grown, named = prepare(parents, expert_ids, step_raw, step_bias, decay_rate, experts)
    near_rows = ys * tokens

    all_tokens = cores * ys * reqs * tokens
    capacity = 2 * tokens * topk // (experts + experts // 4)
    room = capacity * cores * ys * reqs

    rows_left = residual.reshape(tokens, width)
    mixes = []
    part_span = width // MIX_CHUNKS
    for m in range(MIX_CHUNKS):
        cut = slice(m * part_span, (m + 1) * part_span)
        if m == 0:
            mixed, away, mixed_rows = front(
                early, ssm_input, cache_state, factor, grown, skip_gain, out_proj,
                slot_of, goes_to, near_rows, m, MIX_CHUNKS,
            )
        else:
            mixed, away = project(mixed_rows, out_proj, near_rows, m, MIX_CHUNKS)
        if cores > 1:
            mixed = ring.scatter([away], mixed, "dc")
        mixed = mixed.reshape(ys, tokens, part_span)
        mixed = ring.scatter([mixed[s].astype(BF) for s in range(1, ys)], mixed[0], "dy")
        mixes.append((rows_left[:, cut].astype(F32) + mixed).astype(BF))
    span = width // AG_CHUNKS
    after_mixer = jnp.concatenate(mixes, axis=1)
    sums = None
    for k in range(AG_CHUNKS):
        cut = slice(k * span, (k + 1) * span)
        m = k * MIX_CHUNKS // AG_CHUNKS
        local = slice(k * span - m * part_span, (k + 1) * span - m * part_span)
        payload = (mixes[m][:, local].astype(F32) * norm_gain[cut]).astype(BF)
        extras = None
        if k == AG_CHUNKS - 1:
            extra = gates(after_mixer, norm_gain, router, named)
            payload = jnp.concatenate([payload, extra], axis=1)
        if k == 0:
            payload = jnp.concatenate([payload, named], axis=1)
        rows = ring.gather_z(payload)
        rows = ring.gather(rows, "dy")
        rows = rows.reshape(all_tokens // cores, -1)
        xs = [rows]
        if cores > 1:
            xs.append(ring.shift(rows, dc=1))
        if k == 0:
            named_all = jnp.concatenate([x[:, span : span + experts] for x in xs], axis=0)
            mine = lax.dynamic_slice_in_dim(named_all, e0, held, axis=1)
            order = jnp.arange(all_tokens, dtype=jnp.int32)
            before = (order[:, None] > order[None, :]).astype(BF)
            rank = jnp.dot(before, mine, preferred_element_type=F32)
            place = jnp.where(mine > 0, rank, -1.0).astype(jnp.int32)
            spots = jnp.arange(room, dtype=jnp.int32)
            chosen = place.T[:, None, :] == spots[None, :, None]
            token_at = jnp.sum(jnp.where(chosen, order, 0), axis=2).reshape(-1)
        if k == AG_CHUNKS - 1:
            tail = rows.shape[1] - gate_lanes(experts)
            extra = jnp.concatenate([x[:, tail:] for x in xs], axis=0).astype(F32)
            share = lax.dynamic_slice_in_dim(
                extra, e0 + extra.shape[1] - experts, held, axis=1
            )
            extras = (extra, place, share)
        sums = expert_up(k, AG_CHUNKS, token_at, xs, gate_proj, up_proj, sums, extras)
    act, comb = sums

    pieces = []
    span = width // RS_CHUNKS
    for k in range(RS_CHUNKS):
        keep, send = expert_down(k, RS_CHUNKS, act, comb, down_proj, ys * reqs * tokens)
        total = ring.scatter([send], keep, "dc") if cores > 1 else keep
        total = total.reshape(ys, reqs * tokens, span)
        total = ring.scatter([total[s].astype(BF) for s in range(1, ys)], total[0], "dy")
        total = ring.scatter_z(total.reshape(reqs, tokens, span))
        cut = slice(k * span, (k + 1) * span)
        pieces.append((after_mixer[:, cut].astype(F32) + total).astype(BF))
    return jnp.concatenate(pieces, axis=1).reshape(local_nodes, requests, width)


def solution(mesh):
    in_specs = (
        P(None, ("groups", "req"), "head"),
        P("head", ("groups", "req"), None),
        P("head", ("groups", "req"), None),
        P(None, ("groups", "req"), "head"),
        P("head"),
        P("head"),
        P("head"),
        P(("groups", "req"), "head", None, None),
        P(("groups", "req"), None),
        P("head", None),
        P("head", ("groups", "req"), None),
        P(),
        P(),
        P("head", ("groups", "req"), None),
        P(("head", "req"), None, None),
        P(("head", "req"), None, None),
        P(("head", "req"), None, None),
    )
    out_specs = P("head", ("groups", "req"), None)
    return jax.shard_map(layer, mesh=mesh, in_specs=in_specs, out_specs=out_specs, check_vma=False)
```

```python
import functools
import jax
import jax.numpy as jnp
from jax import lax
from jax.experimental import pallas as pl
from jax.experimental.pallas import tpu as pltpu
from jax.sharding import PartitionSpec as P


BF = jnp.bfloat16
F32 = jnp.float32
AXES = ("head", "req")
LANES = 128
MIX_CHUNKS = 2
AG_CHUNKS = 4
RS_CHUNKS = 4
BATCH = 16


def in_hbm(*arrays):
    return [pltpu.with_memory_space_constraint(a, pltpu.HBM) for a in arrays]


class Ring:
    def __init__(self, heads, reqs):
        self.heads, self.reqs = heads, reqs
        self.cores = 2 if heads % 2 == 0 else 1
        self.ys = heads // self.cores

    def pairs(self, dy=0, dc=0, dz=0, flip=0):
        found = []
        for y in range(self.ys):
            for c in range(self.cores):
                for z in range(self.reqs):
                    there = ((y + dy) % self.ys) * self.cores + (c + dc) % self.cores
                    to = (z ^ flip) if flip else (z + dz) % self.reqs
                    found.append(((y * self.cores + c) * self.reqs + z, there * self.reqs + to))
        return found

    def shift(self, x, **how):
        return lax.ppermute(x, AXES, self.pairs(**how))

    def flips(self):
        if self.reqs & (self.reqs - 1):
            return None
        return [1 << b for b in range(self.reqs.bit_length() - 1)]

    def gather_z(self, x):
        flips = self.flips()
        if flips is None:
            return self.gather(x, "dz")
        for flip in reversed(flips):
            x = jnp.stack([x, self.shift(x, flip=flip)])
        return x

    def scatter_z(self, total):
        flips = self.flips()
        if flips is None:
            parts = [total[s].astype(BF) for s in range(1, self.reqs)]
            return self.scatter(parts, total[0], "dz")
        for flip in flips:
            half = total.shape[0] // 2
            sent = self.shift(total[half:].astype(BF), flip=flip)
            total = total[:half] + sent.astype(F32)
        return total[0]

    def gather(self, x, axis):
        count = {"dc": self.cores, "dy": self.ys, "dz": self.reqs}[axis]
        moved = [self.shift(x, **{axis: s}) for s in range(1, count)]
        return jnp.stack([x] + moved)

    def scatter(self, parts, keep, axis):
        total = keep
        for s, part in enumerate(parts, 1):
            total = total + self.shift(part, **{axis: -s}).astype(F32)
        return total


def prep_body(heads, parents, ids, step_raw, bias, decay, factor, grown, named):
    reqs, nodes = parents.shape
    rows = nodes * reqs
    lane = lax.broadcasted_iota(jnp.int32, (rows, rows), 1)
    row = lax.broadcasted_iota(jnp.int32, (rows, rows), 0)
    hop = jnp.concatenate([parents[:, j : j + 1] for j in range(nodes)], axis=0)
    at = jnp.where(hop >= 0, hop * reqs + lax.broadcasted_iota(jnp.int32, hop.shape, 0) % reqs, -1)
    power = jnp.where(at == lane, 1.0, 0.0)
    reach = jnp.where(row == lane, 1.0, 0.0) + power
    power = power.astype(BF)
    span = 2
    while span * reqs < rows:
        power = jnp.dot(power, power, preferred_element_type=F32).astype(BF)
        reach = reach + jnp.dot(reach.astype(BF), power, preferred_element_type=F32)
        span *= 2
    raw = step_raw[...].reshape(rows, heads) + bias[...]
    step = jnp.maximum(raw, 0.0) + jnp.log1p(jnp.exp(-jnp.abs(raw)))
    rate = -step * decay[...]
    blank = jnp.zeros((rows, rows - heads), F32)
    wide_step = jnp.concatenate([step, blank], axis=1)
    wide_rate = jnp.concatenate([rate, blank], axis=1)
    depth = jnp.dot(
        reach, wide_rate, preferred_element_type=F32, precision=lax.Precision.HIGHEST
    )
    grown[...] = jnp.exp(depth[:, :heads])
    depth_t = depth.T
    step_t = wide_step.T
    linked = reach > 0
    for h in range(heads):
        spread = jnp.where(linked, depth[:, h : h + 1] - depth_t[h : h + 1, :], 0.0)
        factor[h] = jnp.where(linked, jnp.exp(spread) * step_t[h : h + 1, :], 0.0)
    chosen = ids[...].reshape(named.shape[0], ids.shape[2])
    label = lax.broadcasted_iota(jnp.int32, named.shape, 1)
    mask = jnp.zeros(named.shape, F32)
    for k in range(ids.shape[2]):
        mask = jnp.where(chosen[:, k : k + 1] == label, 1.0, mask)
    named[...] = mask.astype(BF)


def prepare(parents, expert_ids, step_raw, step_bias, decay_rate, experts):
    nodes, reqs, heads = step_raw.shape
    rows = nodes * reqs
    tokens = expert_ids.shape[0] * expert_ids.shape[1]
    lanes = -(-experts // LANES) * LANES
    return pl.pallas_call(
        functools.partial(prep_body, heads),
        out_shape=(
            jax.ShapeDtypeStruct((heads, rows, rows), F32),
            jax.ShapeDtypeStruct((rows, heads), F32),
            jax.ShapeDtypeStruct((tokens, lanes), BF),
        ),
        compiler_params=pltpu.CompilerParams(vmem_limit_bytes=16 << 20),
        name="prepare",
    )(
        *in_hbm(
            parents, expert_ids, step_raw, step_bias.reshape(1, heads), decay_rate.reshape(1, heads)
        ),
    )


def gate_body(experts, after, gain, router_t, named, out):
    tokens, width = after.shape
    lanes = out.shape[1]
    wide = after[...].astype(F32)
    scale = lax.rsqrt(jnp.sum(wide * wide, axis=1, keepdims=True) / width + 1e-05)
    normed = (wide * scale * gain[...]).astype(BF)
    logits = lax.dot_general(
        normed, router_t[...], (((1,), (1,)), ((), ())), preferred_element_type=F32
    )
    powered = jnp.where(named[:, :experts] > 0, jnp.exp(logits), 0.0)
    gate = powered / jnp.sum(powered, axis=1, keepdims=True)
    top = scale.astype(BF).astype(F32)
    middle = (scale - top).astype(BF).astype(F32)
    low = scale - top - middle
    lane = lax.broadcasted_iota(jnp.int32, (tokens, lanes - experts), 1)
    head = jnp.where(lane == 0, top, jnp.where(lane == 1, middle, jnp.where(lane == 2, low, 0.0)))
    out[...] = jnp.concatenate([head, gate], axis=1).astype(BF)


def gate_lanes(experts):
    return -(-(experts + 3) // LANES) * LANES


def gates(after_mixer, norm_gain, router, named):
    tokens, width = after_mixer.shape
    experts = router.shape[1]
    return pl.pallas_call(
        functools.partial(gate_body, experts),
        out_shape=jax.ShapeDtypeStruct((tokens, gate_lanes(experts)), BF),
        compiler_params=pltpu.CompilerParams(vmem_limit_bytes=16 << 20),
        name="gates",
    )(after_mixer, norm_gain.reshape(1, width), router.T, named.astype(F32))


def project_blocks(rows, weight, held, arrived, first, near, far):
    near_rows = near.shape[0]
    block = held.shape[2]
    for b in range(held.shape[0]):
        weight_copy(weight, held, arrived, first, b).wait()
        total = jnp.dot(rows, held[b], preferred_element_type=F32)
        near[:, b * block : (b + 1) * block] = total[:near_rows]
        far[:, b * block : (b + 1) * block] = total[near_rows:].astype(BF)


def weight_copy(weight, held, arrived, first, b):
    block = held.shape[2]
    return pltpu.make_async_copy(
        weight.at[:, pl.ds(first + b * block, block)], held.at[b], arrived.at[b]
    )


def front_body(
    heads, first, slot_of, goes_to, early, x, state, factor, grown, skip, weight,
    near, far, mixed_rows, read_rows, write_rows, cache, result, states_held, states_in, held, arrived,
):
    blocks, tokens = early.shape[0], early.shape[1]
    nodes, reqs, columns = x.shape
    rows = nodes * reqs
    size = columns // heads
    states = state.shape[2]
    for r in range(reqs):
        pltpu.make_async_copy(state.at[r], states_held.at[r], states_in.at[r]).start()
    for b in range(held.shape[0]):
        weight_copy(weight, held, arrived, first, b).start()
    for a in range(blocks):
        block = early[slot_of[a]].astype(F32)
        write_rows[a * tokens : (a + 1) * tokens] = block[:, :states]
        read_rows[a * tokens : (a + 1) * tokens] = block[:, states : 2 * states]
    writes = write_rows[...].astype(BF)
    reads = read_rows[...].astype(BF)
    affinity = lax.dot_general(
        reads, writes, (((1,), (1,)), ((), ())), preferred_element_type=F32
    )
    for r in range(reqs):
        pltpu.make_async_copy(state.at[r], states_held.at[r], states_in.at[r]).wait()
        mine = read_rows[pl.ds(r, nodes, stride=reqs), :].astype(BF)
        got = lax.dot_general(
            mine, states_held[r], (((1,), (1,)), ((), ())), preferred_element_type=F32
        )
        for i in range(columns // LANES):
            cache.at[i][pl.ds(r, nodes, stride=reqs), :] = got[:, i * LANES : (i + 1) * LANES]
    values = x[...].reshape(rows, columns)
    pair = 2 * size
    left = lax.broadcasted_iota(jnp.int32, (rows, pair), 1) < size
    for h in range(0, heads, 2):
        cut = slice(h * size, h * size + pair)
        own = values[:, cut]
        one = (factor[h] * affinity).astype(BF)
        two = (factor[h + 1] * affinity).astype(BF)
        zero = jnp.zeros_like(own)
        both = jnp.dot(
            jnp.concatenate([one, two], axis=1),
            jnp.concatenate([jnp.where(left, own, zero), jnp.where(left, zero, own)], axis=0),
            preferred_element_type=F32,
        )
        grow = jnp.where(left, grown[:, h : h + 1], grown[:, h + 1 : h + 2])
        gain = jnp.where(left, skip[:, h : h + 1], skip[:, h + 1 : h + 2])
        both = both + cache[h * size // LANES] * grow + gain * own.astype(F32)
        result[:, cut] = both.astype(BF).astype(F32)
    for s in range(blocks):
        start = pl.multiple_of(goes_to[s] * tokens, tokens)
        mixed_rows[s * tokens : (s + 1) * tokens] = result[pl.ds(start, tokens)].astype(BF)
    project_blocks(mixed_rows[...], weight, held, arrived, first, near, far)


def weight_scratch(columns, span):
    block = min(span, 512)
    return [
        pltpu.VMEM((span // block, columns, block), BF),
        pltpu.SemaphoreType.DMA((span // block,)),
    ]


def front(early, x, state, factor, grown, skip_gain, out_proj, slot_of, goes_to, near_rows, part, parts):
    nodes, reqs, columns = x.shape
    heads = skip_gain.shape[0]
    rows = nodes * reqs
    states = state.shape[3]
    span = out_proj.shape[1] // parts
    state = state.reshape(state.shape[0], columns, states)
    skip = skip_gain.reshape(1, heads)
    x, state, skip, out_proj = in_hbm(x, state, skip, out_proj)
    vmem = pl.BlockSpec(memory_space=pltpu.VMEM)
    hbm = pl.BlockSpec(memory_space=pltpu.HBM)
    return pl.pallas_call(
        functools.partial(front_body, heads, part * span),
        grid_spec=pltpu.PrefetchScalarGridSpec(
            num_scalar_prefetch=2,
            in_specs=[vmem, vmem, hbm, vmem, vmem, vmem, hbm],
            out_specs=(vmem, vmem, vmem),
            scratch_shapes=[
                pltpu.VMEM((rows, states), F32),
                pltpu.VMEM((rows, states), F32),
                pltpu.VMEM((columns // LANES, rows, LANES), F32),
                pltpu.VMEM((rows, columns), F32),
                pltpu.VMEM(state.shape, BF),
                pltpu.SemaphoreType.DMA((reqs,)),
                *weight_scratch(columns, span),
            ],
        ),
        out_shape=(
            jax.ShapeDtypeStruct((near_rows, span), F32),
            jax.ShapeDtypeStruct((rows - near_rows, span), BF),
            jax.ShapeDtypeStruct((rows, columns), BF),
        ),
        compiler_params=pltpu.CompilerParams(vmem_limit_bytes=16 << 20),
        cost_estimate=pl.CostEstimate(
            flops=2 * rows * columns * span, transcendentals=0, bytes_accessed=2 * columns * span
        ),
        name="front",
    )(slot_of, goes_to, early, x, state, factor, grown, skip, out_proj)


def project_body(first, rows, weight, near, far, held, arrived):
    for b in range(held.shape[0]):
        weight_copy(weight, held, arrived, first, b).start()
    project_blocks(rows[...], weight, held, arrived, first, near, far)


def project(rows, out_proj, near_rows, part, parts):
    count, columns = rows.shape
    span = out_proj.shape[1] // parts
    vmem = pl.BlockSpec(memory_space=pltpu.VMEM)
    return pl.pallas_call(
        functools.partial(project_body, part * span),
        in_specs=[vmem, pl.BlockSpec(memory_space=pltpu.HBM)],
        out_specs=(vmem, vmem),
        out_shape=(
            jax.ShapeDtypeStruct((near_rows, span), F32),
            jax.ShapeDtypeStruct((count - near_rows, span), BF),
        ),
        scratch_shapes=weight_scratch(columns, span),
        compiler_params=pltpu.CompilerParams(vmem_limit_bytes=10 << 20),
        cost_estimate=pl.CostEstimate(
            flops=2 * count * columns * span, transcendentals=0, bytes_accessed=2 * columns * span
        ),
        name="project",
    )(rows, *in_hbm(out_proj))


def own_columns(lanes, first, held):
    at = lax.broadcasted_iota(jnp.int32, (lanes, held), 0)
    to = lax.broadcasted_iota(jnp.int32, (lanes, held), 1)
    return jnp.where(at == to + first, 1.0, 0.0).astype(BF)


def place_body(begin, e0, *rest):
    xs, (tokens_out, place_out) = rest[:-2], rest[-2:]
    held, slots = tokens_out.shape
    named = jnp.concatenate([x[:, begin:] for x in xs], axis=0)
    count, lanes = named.shape
    mine = jnp.dot(
        named, own_columns(lanes, e0[0], held), preferred_element_type=F32
    )
    row = lax.broadcasted_iota(jnp.int32, (count, count), 0)
    column = lax.broadcasted_iota(jnp.int32, (count, count), 1)
    before = jnp.where(row > column, 1.0, 0.0).astype(BF)
    rank = jnp.dot(before, mine.astype(BF), preferred_element_type=F32)
    place = jnp.where(mine > 0, rank, -1.0)
    place_out[...] = place
    spot = lax.broadcasted_iota(jnp.int32, (count, slots), 1).astype(F32)
    token = lax.broadcasted_iota(jnp.int32, (count, slots), 0).astype(F32)
    for q in range(held):
        here = jnp.where(spot == place[:, q : q + 1], token, 0.0)
        tokens_out[q : q + 1] = jnp.sum(here, axis=0, keepdims=True).astype(jnp.int32)


def places(e0, xs, begin, held, slots):
    tokens = sum(x.shape[0] for x in xs)
    return pl.pallas_call(
        functools.partial(place_body, begin),
        in_specs=[pl.BlockSpec(memory_space=pltpu.SMEM)]
        + [pl.BlockSpec(memory_space=pltpu.VMEM)] * len(xs),
        out_shape=(
            jax.ShapeDtypeStruct((held, slots), jnp.int32),
            jax.ShapeDtypeStruct((tokens, held), F32),
        ),
        compiler_params=pltpu.CompilerParams(vmem_limit_bytes=10 << 20),
        name="places",
    )(e0, *xs)


def up_body(first, last, begin, pieces, width, experts, token_at, *rest):
    rest = list(rest)
    xs = [rest.pop(0) for _ in range(pieces)]
    wg, wu = rest.pop(0), rest.pop(0)
    if not first:
        gin, uin = rest.pop(0), rest.pop(0)
    if last:
        spot, e0 = rest.pop(0), rest.pop(0)
        act_out, comb_out, spread, picked, gates_held, ups_held, arrived, scales, extra = rest
    else:
        gout, uout, spread, picked, gates_held, ups_held, arrived = rest
    held = gates_held.shape[0]
    tall = width // LANES
    slots = picked.shape[0] // tall

    def copies(e):
        cut = pl.ds(begin, width)
        return (
            pltpu.make_async_copy(wg.at[e, cut], gates_held.at[e], arrived.at[0, e]),
            pltpu.make_async_copy(wu.at[e, cut], ups_held.at[e], arrived.at[1, e]),
        )

    for e in range(held):
        for copy in copies(e):
            copy.start()
    done = 0
    for x in xs:
        tokens = x.shape[0]
        for i in range(tall):
            spread[pl.ds(done * tall + i, tokens, stride=tall), :] = x[
                :, i * LANES : (i + 1) * LANES
            ].astype(F32)
        if last:
            extra[done : done + tokens] = x[:, width:].astype(F32)
        done += tokens
    if last:
        lanes = extra.shape[1]
        share = jnp.dot(
            extra[...].astype(BF),
            own_columns(lanes, e0[0] + lanes - experts, held),
            preferred_element_type=F32,
        )

    def visit(q, carry):
        for c in range(0, slots, BATCH):
            at = [token_at[q, c + i] for i in range(BATCH)]
            got = [spread[pl.ds(pl.multiple_of(t * tall, tall), tall)] for t in at]
            picked[c * tall : (c + BATCH) * tall] = jnp.concatenate(got, axis=0)
            if last:
                got = [extra[pl.ds(t, 1)] for t in at]
                for i in range(BATCH):
                    scales[c + i : c + i + 1] = got[i]
        rows = jnp.concatenate(
            [picked[pl.ds(i, slots, stride=tall), :].astype(BF) for i in range(tall)], axis=1
        )
        for copy in copies(q):
            copy.wait()
        gated = jnp.dot(rows, gates_held[q], preferred_element_type=F32)
        lifted = jnp.dot(rows, ups_held[q], preferred_element_type=F32)
        if not first:
            gated = gated + gin[q]
            lifted = lifted + uin[q]
        if not last:
            gout[q] = gated
            uout[q] = lifted
            return carry
        scale = scales[:, 0:1] + scales[:, 1:2] + scales[:, 2:3]
        gated = gated * scale
        lifted = lifted * scale
        act_out[q] = (gated / (1.0 + jnp.exp(-gated)) * lifted).astype(BF)
        lane = lax.broadcasted_iota(jnp.int32, (done, slots), 1).astype(F32)
        column = lax.broadcasted_iota(jnp.int32, spot.shape, 1)
        own_spot = jnp.sum(jnp.where(column == q, spot[...], 0.0), axis=1, keepdims=True)
        own_share = jnp.sum(jnp.where(column == q, share, 0.0), axis=1, keepdims=True)
        comb_out[q] = jnp.where(lane == own_spot, own_share, 0.0).astype(BF)
        return carry

    lax.fori_loop(0, held, visit, 0)


def expert_up(k, chunks, experts, token_at, xs, gate_proj, up_proj, sums, place, e0):
    held = gate_proj.shape[0]
    width = gate_proj.shape[1] // chunks
    tokens = sum(x.shape[0] for x in xs)
    slots = token_at.shape[1]
    units = gate_proj.shape[2]
    first, last = k == 0, k == chunks - 1
    vmem = pl.BlockSpec(memory_space=pltpu.VMEM)
    hbm = pl.BlockSpec(memory_space=pltpu.HBM)
    in_specs = [pl.BlockSpec(memory_space=pltpu.SMEM)] + [vmem] * len(xs) + [hbm, hbm]
    args = [token_at, *xs, *in_hbm(gate_proj, up_proj)]
    scratch = [
        pltpu.VMEM((tokens * width // LANES, LANES), F32),
        pltpu.VMEM((slots * width // LANES, LANES), F32),
        pltpu.VMEM((held, width, units), BF),
        pltpu.VMEM((held, width, units), BF),
        pltpu.SemaphoreType.DMA((2, held)),
    ]
    aliases = {}
    if not first:
        if not last:
            aliases = {len(args): 0, len(args) + 1: 1}
        in_specs += [vmem] * 2
        args += list(sums)
    if last:
        in_specs += [vmem, pl.BlockSpec(memory_space=pltpu.SMEM)]
        args += [place, e0]
        out_shape = (
            jax.ShapeDtypeStruct((held, slots, units), BF),
            jax.ShapeDtypeStruct((held, tokens, slots), BF),
        )
        lanes = gate_lanes(experts)
        scratch += [pltpu.VMEM((slots, lanes), F32), pltpu.VMEM((tokens, lanes), F32)]
    else:
        out_shape = (jax.ShapeDtypeStruct((held, slots, units), F32),) * 2
    return pl.pallas_call(
        functools.partial(up_body, first, last, k * width, len(xs), width, experts),
        in_specs=in_specs,
        out_specs=(vmem, vmem),
        out_shape=out_shape,
        scratch_shapes=scratch,
        input_output_aliases=aliases,
        compiler_params=pltpu.CompilerParams(vmem_limit_bytes=4 * held * width * units + 4 * tokens * width + (6 << 20)),
        cost_estimate=pl.CostEstimate(
            flops=4 * held * slots * width * units,
            transcendentals=0,
            bytes_accessed=4 * held * width * units,
        ),
    )(*args)


def down_body(begin, act, comb, wd, keep, send, halves, held_rows, arrived):
    held, slots, _ = act.shape
    width = keep.shape[1]

    def copy(q):
        return pltpu.make_async_copy(
            wd.at[q, :, pl.ds(begin, width)], held_rows.at[q], arrived.at[q]
        )

    for q in range(held):
        copy(q).start()
    for q in range(held):
        copy(q).wait()
        halves[q * slots : (q + 1) * slots] = jnp.dot(
            act[q], held_rows[q], preferred_element_type=F32
        ).astype(BF)
    kept = keep.shape[0]
    comb_rows = jnp.concatenate([comb[q] for q in range(held)], axis=1)
    block = min(width, 256)
    for j in range(0, width, block):
        cut = slice(j, j + block)
        total = jnp.dot(comb_rows, halves[:, cut], preferred_element_type=F32)
        keep[:, cut] = total[:kept]
        send[:, cut] = total[kept:].astype(BF)


def expert_down(k, chunks, act, comb, down_proj, kept):
    held, slots, units = act.shape
    tokens = comb.shape[1]
    width = down_proj.shape[2] // chunks
    vmem = pl.BlockSpec(memory_space=pltpu.VMEM)
    return pl.pallas_call(
        functools.partial(down_body, k * width),
        in_specs=[vmem, vmem, pl.BlockSpec(memory_space=pltpu.HBM)],
        out_specs=(vmem, vmem),
        out_shape=(
            jax.ShapeDtypeStruct((kept, width), F32),
            jax.ShapeDtypeStruct((tokens - kept, width), BF),
        ),
        scratch_shapes=[
            pltpu.VMEM((held * slots, width), BF),
            pltpu.VMEM((held, units, width), BF),
            pltpu.SemaphoreType.DMA((held,)),
        ],
        compiler_params=pltpu.CompilerParams(vmem_limit_bytes=2 * held * width * (units + slots) + (8 << 20)),
        cost_estimate=pl.CostEstimate(
            flops=2 * held * slots * width * (tokens + units),
            transcendentals=0,
            bytes_accessed=2 * held * width * units,
        ),
    )(act, comb, *in_hbm(down_proj))


def layer(
    ssm_input,
    write_vec,
    read_vec,
    step_raw,
    step_bias,
    decay_rate,
    skip_gain,
    cache_state,
    parents,
    out_proj,
    residual,
    norm_gain,
    router,
    expert_ids,
    gate_proj,
    up_proj,
    down_proj,
):
    _, requests, _ = ssm_input.shape
    local_nodes, _, width = residual.shape
    tokens = local_nodes * requests
    topk = expert_ids.shape[2]
    experts = router.shape[1]
    held = gate_proj.shape[0]
    ring = Ring(lax.axis_size("head"), lax.axis_size("req"))
    cores, ys, reqs = ring.cores, ring.ys, ring.reqs
    head_at = lax.axis_index("head")
    y_at, c_at = head_at // cores, head_at % cores
    device = head_at * reqs + lax.axis_index("req")
    e0 = ((device * held) % experts).reshape(1).astype(jnp.int32)

    states = write_vec.shape[2]
    early = jnp.concatenate(
        [write_vec.reshape(tokens, states), read_vec.reshape(tokens, states)], axis=1
    )
    early = ring.gather(ring.gather(early, "dc"), "dy")
    early = early.reshape(ys * cores, tokens, -1)
    absolute = jnp.arange(ys * cores, dtype=jnp.int32)
    slot_of = ((y_at - absolute // cores) % ys) * cores + (c_at - absolute % cores) % cores
    slots = jnp.arange(cores * ys, dtype=jnp.int32)
    goes_to = ((y_at - slots % ys) % ys) * cores + (c_at - slots // ys) % cores
    factor, grown, named = prepare(parents, expert_ids, step_raw, step_bias, decay_rate, experts)
    near_rows = ys * tokens

    all_tokens = cores * ys * reqs * tokens
    capacity = 2 * tokens * topk // (experts + experts // 4)
    room = capacity * cores * ys * reqs

    rows_left = residual.reshape(tokens, width)
    mixes = []
    part_span = width // MIX_CHUNKS
    for m in range(MIX_CHUNKS):
        cut = slice(m * part_span, (m + 1) * part_span)
        if m == 0:
            mixed, away, mixed_rows = front(
                early, ssm_input, cache_state, factor, grown, skip_gain, out_proj,
                slot_of, goes_to, near_rows, m, MIX_CHUNKS,
            )
        else:
            mixed, away = project(mixed_rows, out_proj, near_rows, m, MIX_CHUNKS)
        if cores > 1:
            mixed = ring.scatter([away], mixed, "dc")
        mixed = mixed.reshape(ys, tokens, part_span)
        mixed = ring.scatter([mixed[s].astype(BF) for s in range(1, ys)], mixed[0], "dy")
        mixes.append((rows_left[:, cut].astype(F32) + mixed).astype(BF))
    span = width // AG_CHUNKS
    after_mixer = jnp.concatenate(mixes, axis=1)
    sums = None
    for k in range(AG_CHUNKS):
        cut = slice(k * span, (k + 1) * span)
        m = k * MIX_CHUNKS // AG_CHUNKS
        local = slice(k * span - m * part_span, (k + 1) * span - m * part_span)
        payload = (mixes[m][:, local].astype(F32) * norm_gain[cut]).astype(BF)
        if k == AG_CHUNKS - 1:
            extra = gates(after_mixer, norm_gain, router, named)
            payload = jnp.concatenate([payload, extra], axis=1)
        if k == 0:
            payload = jnp.concatenate([payload, named], axis=1)
        rows = ring.gather_z(payload)
        rows = ring.gather(rows, "dy")
        rows = rows.reshape(all_tokens // cores, -1)
        xs = [rows]
        if cores > 1:
            xs.append(ring.shift(rows, dc=1))
        if k == 0:
            token_at, place = places(e0, xs, span, held, room)
        sums = expert_up(k, AG_CHUNKS, experts, token_at, xs, gate_proj, up_proj, sums, place, e0)
    act, comb = sums

    pieces = []
    span = width // RS_CHUNKS
    for k in range(RS_CHUNKS):
        keep, send = expert_down(k, RS_CHUNKS, act, comb, down_proj, ys * reqs * tokens)
        total = ring.scatter([send], keep, "dc") if cores > 1 else keep
        total = total.reshape(ys, reqs * tokens, span)
        total = ring.scatter([total[s].astype(BF) for s in range(1, ys)], total[0], "dy")
        total = ring.scatter_z(total.reshape(reqs, tokens, span))
        cut = slice(k * span, (k + 1) * span)
        pieces.append((after_mixer[:, cut].astype(F32) + total).astype(BF))
    return jnp.concatenate(pieces, axis=1).reshape(local_nodes, requests, width)


def solution(mesh):
    in_specs = (
        P(None, ("groups", "req"), "head"),
        P("head", ("groups", "req"), None),
        P("head", ("groups", "req"), None),
        P(None, ("groups", "req"), "head"),
        P("head"),
        P("head"),
        P("head"),
        P(("groups", "req"), "head", None, None),
        P(("groups", "req"), None),
        P("head", None),
        P("head", ("groups", "req"), None),
        P(),
        P(),
        P("head", ("groups", "req"), None),
        P(("head", "req"), None, None),
        P(("head", "req"), None, None),
        P(("head", "req"), None, None),
    )
    out_specs = P("head", ("groups", "req"), None)
    return jax.shard_map(layer, mesh=mesh, in_specs=in_specs, out_specs=out_specs, check_vma=False)
```

```python
import functools
import jax
import jax.numpy as jnp
from jax import lax
from jax.experimental import pallas as pl
from jax.experimental.pallas import tpu as pltpu
from jax.sharding import PartitionSpec as P


BF = jnp.bfloat16
F32 = jnp.float32
AXES = ("head", "req")
LANES = 128
MIX_PARTS = ((0, 1), (1, 4))
AG_CHUNKS = 4
RS_CHUNKS = 4
BATCH = 16
Z_GROUPS = ((0,), (1,), (2, 3))


def in_hbm(*arrays):
    return [pltpu.with_memory_space_constraint(a, pltpu.HBM) for a in arrays]


class Ring:
    def __init__(self, heads, reqs):
        self.heads, self.reqs = heads, reqs
        self.cores = 2 if heads % 2 == 0 else 1
        self.ys = heads // self.cores

    def pairs(self, dy=0, dc=0, dz=0, flip=0):
        found = []
        for y in range(self.ys):
            for c in range(self.cores):
                for z in range(self.reqs):
                    there = ((y + dy) % self.ys) * self.cores + (c + dc) % self.cores
                    to = (z ^ flip) if flip else (z + dz) % self.reqs
                    found.append(((y * self.cores + c) * self.reqs + z, there * self.reqs + to))
        return found

    def shift(self, x, **how):
        return lax.ppermute(x, AXES, self.pairs(**how))

    def flips(self):
        if self.reqs & (self.reqs - 1):
            return None
        return [1 << b for b in range(self.reqs.bit_length() - 1)]

    def gather_z(self, x):
        flips = self.flips()
        if flips is None:
            return self.gather(x, "dz")
        for flip in reversed(flips):
            x = jnp.stack([x, self.shift(x, flip=flip)])
        return x

    def scatter_z(self, total):
        flips = self.flips()
        if flips is None:
            parts = [total[s].astype(BF) for s in range(1, self.reqs)]
            return self.scatter(parts, total[0], "dz")
        for flip in flips:
            half = total.shape[0] // 2
            sent = self.shift(total[half:].astype(BF), flip=flip)
            total = total[:half] + sent.astype(F32)
        return total[0]

    def gather(self, x, axis):
        count = {"dc": self.cores, "dy": self.ys, "dz": self.reqs}[axis]
        moved = [self.shift(x, **{axis: s}) for s in range(1, count)]
        return jnp.stack([x] + moved)

    def scatter(self, parts, keep, axis):
        total = keep
        for s, part in enumerate(parts, 1):
            total = total + self.shift(part, **{axis: -s}).astype(F32)
        return total


def prep_body(heads, parents, ids, step_raw, bias, decay, factor, grown, named):
    reqs, nodes = parents.shape
    rows = nodes * reqs
    lane = lax.broadcasted_iota(jnp.int32, (rows, rows), 1)
    row = lax.broadcasted_iota(jnp.int32, (rows, rows), 0)
    hop = jnp.concatenate([parents[:, j : j + 1] for j in range(nodes)], axis=0)
    at = jnp.where(hop >= 0, hop * reqs + lax.broadcasted_iota(jnp.int32, hop.shape, 0) % reqs, -1)
    power = jnp.where(at == lane, 1.0, 0.0)
    reach = jnp.where(row == lane, 1.0, 0.0) + power
    power = power.astype(BF)
    span = 2
    while span * reqs < rows:
        power = jnp.dot(power, power, preferred_element_type=F32).astype(BF)
        reach = reach + jnp.dot(reach.astype(BF), power, preferred_element_type=F32)
        span *= 2
    raw = step_raw[...].reshape(rows, heads) + bias[...]
    step = jnp.maximum(raw, 0.0) + jnp.log1p(jnp.exp(-jnp.abs(raw)))
    rate = -step * decay[...]
    blank = jnp.zeros((rows, rows - heads), F32)
    wide_step = jnp.concatenate([step, blank], axis=1)
    wide_rate = jnp.concatenate([rate, blank], axis=1)
    depth = jnp.dot(
        reach, wide_rate, preferred_element_type=F32, precision=lax.Precision.HIGHEST
    )
    grown[...] = jnp.exp(depth[:, :heads])
    depth_t = depth.T
    step_t = wide_step.T
    linked = reach > 0
    for h in range(heads):
        spread = jnp.where(linked, depth[:, h : h + 1] - depth_t[h : h + 1, :], 0.0)
        factor[h] = jnp.where(linked, jnp.exp(spread) * step_t[h : h + 1, :], 0.0)
    chosen = ids[...].reshape(named.shape[0], ids.shape[2])
    label = lax.broadcasted_iota(jnp.int32, named.shape, 1)
    mask = jnp.zeros(named.shape, F32)
    for k in range(ids.shape[2]):
        mask = jnp.where(chosen[:, k : k + 1] == label, 1.0, mask)
    named[...] = mask.astype(BF)


def prepare(parents, expert_ids, step_raw, step_bias, decay_rate, experts):
    nodes, reqs, heads = step_raw.shape
    rows = nodes * reqs
    tokens = expert_ids.shape[0] * expert_ids.shape[1]
    lanes = -(-experts // LANES) * LANES
    return pl.pallas_call(
        functools.partial(prep_body, heads),
        out_shape=(
            jax.ShapeDtypeStruct((heads, rows, rows), F32),
            jax.ShapeDtypeStruct((rows, heads), F32),
            jax.ShapeDtypeStruct((tokens, lanes), BF),
        ),
        compiler_params=pltpu.CompilerParams(vmem_limit_bytes=16 << 20),
        name="prepare",
    )(
        *in_hbm(
            parents, expert_ids, step_raw, step_bias.reshape(1, heads), decay_rate.reshape(1, heads)
        ),
    )


def gate_body(experts, after, gain, router_t, named, out):
    tokens, width = after.shape
    lanes = out.shape[1]
    wide = after[...].astype(F32)
    scale = lax.rsqrt(jnp.sum(wide * wide, axis=1, keepdims=True) / width + 1e-05)
    normed = (wide * scale * gain[...]).astype(BF)
    logits = lax.dot_general(
        normed, router_t[...], (((1,), (1,)), ((), ())), preferred_element_type=F32
    )
    powered = jnp.where(named[:, :experts] > 0, jnp.exp(logits), 0.0)
    gate = powered / jnp.sum(powered, axis=1, keepdims=True)
    top = scale.astype(BF).astype(F32)
    middle = (scale - top).astype(BF).astype(F32)
    low = scale - top - middle
    lane = lax.broadcasted_iota(jnp.int32, (tokens, lanes - experts), 1)
    head = jnp.where(lane == 0, top, jnp.where(lane == 1, middle, jnp.where(lane == 2, low, 0.0)))
    out[...] = jnp.concatenate([head, gate], axis=1).astype(BF)


def gate_lanes(experts):
    return -(-(experts + 3) // LANES) * LANES


def gates(after_mixer, norm_gain, router, named):
    tokens, width = after_mixer.shape
    experts = router.shape[1]
    return pl.pallas_call(
        functools.partial(gate_body, experts),
        out_shape=jax.ShapeDtypeStruct((tokens, gate_lanes(experts)), BF),
        compiler_params=pltpu.CompilerParams(vmem_limit_bytes=16 << 20),
        name="gates",
    )(after_mixer, norm_gain.reshape(1, width), router.T, named.astype(F32))


def project_blocks(rows, weight, held, arrived, first, near, far):
    near_rows = near.shape[0]
    block = held.shape[2]
    for b in range(held.shape[0]):
        weight_copy(weight, held, arrived, first, b).wait()
        total = jnp.dot(rows, held[b], preferred_element_type=F32)
        near[:, b * block : (b + 1) * block] = total[:near_rows]
        far[:, b * block : (b + 1) * block] = total[near_rows:].astype(BF)


def weight_copy(weight, held, arrived, first, b):
    block = held.shape[2]
    return pltpu.make_async_copy(
        weight.at[:, pl.ds(first + b * block, block)], held.at[b], arrived.at[b]
    )


def front_body(
    heads, first, slot_of, goes_to, early, x, state, factor, grown, skip, weight,
    near, far, mixed_rows, read_rows, write_rows, cache, result, states_held, states_in, held, arrived,
):
    blocks, tokens = early.shape[0], early.shape[1]
    nodes, reqs, columns = x.shape
    rows = nodes * reqs
    size = columns // heads
    states = state.shape[2]
    for r in range(reqs):
        pltpu.make_async_copy(state.at[r], states_held.at[r], states_in.at[r]).start()
    for b in range(held.shape[0]):
        weight_copy(weight, held, arrived, first, b).start()
    for a in range(blocks):
        block = early[slot_of[a]].astype(F32)
        write_rows[a * tokens : (a + 1) * tokens] = block[:, :states]
        read_rows[a * tokens : (a + 1) * tokens] = block[:, states : 2 * states]
    writes = write_rows[...].astype(BF)
    reads = read_rows[...].astype(BF)
    affinity = lax.dot_general(
        reads, writes, (((1,), (1,)), ((), ())), preferred_element_type=F32
    )
    for r in range(reqs):
        pltpu.make_async_copy(state.at[r], states_held.at[r], states_in.at[r]).wait()
        mine = read_rows[pl.ds(r, nodes, stride=reqs), :].astype(BF)
        got = lax.dot_general(
            mine, states_held[r], (((1,), (1,)), ((), ())), preferred_element_type=F32
        )
        for i in range(columns // LANES):
            cache.at[i][pl.ds(r, nodes, stride=reqs), :] = got[:, i * LANES : (i + 1) * LANES]
    values = x[...].reshape(rows, columns)
    pair = 2 * size
    left = lax.broadcasted_iota(jnp.int32, (rows, pair), 1) < size
    for h in range(0, heads, 2):
        cut = slice(h * size, h * size + pair)
        own = values[:, cut]
        one = (factor[h] * affinity).astype(BF)
        two = (factor[h + 1] * affinity).astype(BF)
        zero = jnp.zeros_like(own)
        both = jnp.dot(
            jnp.concatenate([one, two], axis=1),
            jnp.concatenate([jnp.where(left, own, zero), jnp.where(left, zero, own)], axis=0),
            preferred_element_type=F32,
        )
        grow = jnp.where(left, grown[:, h : h + 1], grown[:, h + 1 : h + 2])
        gain = jnp.where(left, skip[:, h : h + 1], skip[:, h + 1 : h + 2])
        both = both + cache[h * size // LANES] * grow + gain * own.astype(F32)
        result[:, cut] = both.astype(BF).astype(F32)
    for s in range(blocks):
        start = pl.multiple_of(goes_to[s] * tokens, tokens)
        mixed_rows[s * tokens : (s + 1) * tokens] = result[pl.ds(start, tokens)].astype(BF)
    project_blocks(mixed_rows[...], weight, held, arrived, first, near, far)


def weight_scratch(columns, span):
    block = min(span, 512)
    return [
        pltpu.VMEM((span // block, columns, block), BF),
        pltpu.SemaphoreType.DMA((span // block,)),
    ]


def front(early, x, state, factor, grown, skip_gain, out_proj, slot_of, goes_to, near_rows, begin, span):
    nodes, reqs, columns = x.shape
    heads = skip_gain.shape[0]
    rows = nodes * reqs
    states = state.shape[3]
    state = state.reshape(state.shape[0], columns, states)
    skip = skip_gain.reshape(1, heads)
    x, state, skip, out_proj = in_hbm(x, state, skip, out_proj)
    vmem = pl.BlockSpec(memory_space=pltpu.VMEM)
    hbm = pl.BlockSpec(memory_space=pltpu.HBM)
    return pl.pallas_call(
        functools.partial(front_body, heads, begin),
        grid_spec=pltpu.PrefetchScalarGridSpec(
            num_scalar_prefetch=2,
            in_specs=[vmem, vmem, hbm, vmem, vmem, vmem, hbm],
            out_specs=(vmem, vmem, vmem),
            scratch_shapes=[
                pltpu.VMEM((rows, states), F32),
                pltpu.VMEM((rows, states), F32),
                pltpu.VMEM((columns // LANES, rows, LANES), F32),
                pltpu.VMEM((rows, columns), F32),
                pltpu.VMEM(state.shape, BF),
                pltpu.SemaphoreType.DMA((reqs,)),
                *weight_scratch(columns, span),
            ],
        ),
        out_shape=(
            jax.ShapeDtypeStruct((near_rows, span), F32),
            jax.ShapeDtypeStruct((rows - near_rows, span), BF),
            jax.ShapeDtypeStruct((rows, columns), BF),
        ),
        compiler_params=pltpu.CompilerParams(vmem_limit_bytes=16 << 20),
        cost_estimate=pl.CostEstimate(
            flops=2 * rows * columns * span, transcendentals=0, bytes_accessed=2 * columns * span
        ),
        name="front",
    )(slot_of, goes_to, early, x, state, factor, grown, skip, out_proj)


def project_body(first, rows, weight, near, far, held, arrived):
    for b in range(held.shape[0]):
        weight_copy(weight, held, arrived, first, b).start()
    project_blocks(rows[...], weight, held, arrived, first, near, far)


def project(rows, out_proj, near_rows, begin, span):
    count, columns = rows.shape
    vmem = pl.BlockSpec(memory_space=pltpu.VMEM)
    return pl.pallas_call(
        functools.partial(project_body, begin),
        in_specs=[vmem, pl.BlockSpec(memory_space=pltpu.HBM)],
        out_specs=(vmem, vmem),
        out_shape=(
            jax.ShapeDtypeStruct((near_rows, span), F32),
            jax.ShapeDtypeStruct((count - near_rows, span), BF),
        ),
        scratch_shapes=weight_scratch(columns, span),
        compiler_params=pltpu.CompilerParams(vmem_limit_bytes=10 << 20),
        cost_estimate=pl.CostEstimate(
            flops=2 * count * columns * span, transcendentals=0, bytes_accessed=2 * columns * span
        ),
        name="project",
    )(rows, *in_hbm(out_proj))


def own_columns(lanes, first, held):
    at = lax.broadcasted_iota(jnp.int32, (lanes, held), 0)
    to = lax.broadcasted_iota(jnp.int32, (lanes, held), 1)
    return jnp.where(at == to + first, 1.0, 0.0).astype(BF)


def place_body(begin, e0, *rest):
    xs, (tokens_out, place_out) = rest[:-2], rest[-2:]
    held, slots = tokens_out.shape
    named = jnp.concatenate([x[:, begin:] for x in xs], axis=0)
    count, lanes = named.shape
    mine = jnp.dot(
        named, own_columns(lanes, e0[0], held), preferred_element_type=F32
    )
    row = lax.broadcasted_iota(jnp.int32, (count, count), 0)
    column = lax.broadcasted_iota(jnp.int32, (count, count), 1)
    before = jnp.where(row > column, 1.0, 0.0).astype(BF)
    rank = jnp.dot(before, mine.astype(BF), preferred_element_type=F32)
    place = jnp.where(mine > 0, rank, -1.0)
    place_out[...] = place
    spot = lax.broadcasted_iota(jnp.int32, (count, slots), 1).astype(F32)
    token = lax.broadcasted_iota(jnp.int32, (count, slots), 0).astype(F32)
    for q in range(held):
        here = jnp.where(spot == place[:, q : q + 1], token, 0.0)
        tokens_out[q : q + 1] = jnp.sum(here, axis=0, keepdims=True).astype(jnp.int32)


def places(e0, xs, begin, held, slots):
    tokens = sum(x.shape[0] for x in xs)
    return pl.pallas_call(
        functools.partial(place_body, begin),
        in_specs=[pl.BlockSpec(memory_space=pltpu.SMEM)]
        + [pl.BlockSpec(memory_space=pltpu.VMEM)] * len(xs),
        out_shape=(
            jax.ShapeDtypeStruct((held, slots), jnp.int32),
            jax.ShapeDtypeStruct((tokens, held), F32),
        ),
        compiler_params=pltpu.CompilerParams(vmem_limit_bytes=10 << 20),
        name="places",
    )(e0, *xs)


def up_body(first, last, begin, pieces, width, experts, token_at, *rest):
    rest = list(rest)
    xs = [rest.pop(0) for _ in range(pieces)]
    wg, wu = rest.pop(0), rest.pop(0)
    if not first:
        gin, uin = rest.pop(0), rest.pop(0)
    if last:
        spot, e0 = rest.pop(0), rest.pop(0)
        act_out, comb_out, spread, picked, gates_held, ups_held, arrived, scales, extra = rest
    else:
        gout, uout, spread, picked, gates_held, ups_held, arrived = rest
    held = gates_held.shape[0]
    tall = width // LANES
    slots = picked.shape[1] // tall

    def copies(e):
        cut = pl.ds(begin, width)
        return (
            pltpu.make_async_copy(wg.at[e, cut], gates_held.at[e], arrived.at[0, e]),
            pltpu.make_async_copy(wu.at[e, cut], ups_held.at[e], arrived.at[1, e]),
        )

    for e in range(held):
        for copy in copies(e):
            copy.start()
    done = 0
    for x in xs:
        tokens = x.shape[0]
        for i in range(tall):
            spread[pl.ds(done * tall + i, tokens, stride=tall), :] = x[
                :, i * LANES : (i + 1) * LANES
            ].astype(F32)
        if last:
            extra[done : done + tokens] = x[:, width:].astype(F32)
        done += tokens
    if last:
        lanes = extra.shape[1]
        share = jnp.dot(
            extra[...].astype(BF),
            own_columns(lanes, e0[0] + lanes - experts, held),
            preferred_element_type=F32,
        )

    def pick(q, b):
        for c in range(0, slots, BATCH):
            at = [token_at[q, c + i] for i in range(BATCH)]
            got = [spread[pl.ds(pl.multiple_of(t * tall, tall), tall)] for t in at]
            picked[b, c * tall : (c + BATCH) * tall] = jnp.concatenate(got, axis=0)
            if last:
                got = [extra[pl.ds(t, 1)] for t in at]
                for i in range(BATCH):
                    scales[b, c + i : c + i + 1] = got[i]

    def multiply(q, b):
        half = picked.at[b]
        rows = jnp.concatenate(
            [half[pl.ds(i, slots, stride=tall), :].astype(BF) for i in range(tall)], axis=1
        )
        gated = jnp.dot(rows, gates_held[q], preferred_element_type=F32)
        lifted = jnp.dot(rows, ups_held[q], preferred_element_type=F32)
        if not first:
            gated = gated + gin[q]
            lifted = lifted + uin[q]
        if not last:
            gout[q] = gated
            uout[q] = lifted
            return
        scale = scales[b, :, 0:1] + scales[b, :, 1:2] + scales[b, :, 2:3]
        gated = gated * scale
        lifted = lifted * scale
        act_out[q] = (gated / (1.0 + jnp.exp(-gated)) * lifted).astype(BF)
        lane = lax.broadcasted_iota(jnp.int32, (done, slots), 1).astype(F32)
        column = lax.broadcasted_iota(jnp.int32, spot.shape, 1)
        own_spot = jnp.sum(jnp.where(column == q, spot[...], 0.0), axis=1, keepdims=True)
        own_share = jnp.sum(jnp.where(column == q, share, 0.0), axis=1, keepdims=True)
        at = pl.ds(pl.multiple_of(q * slots, LANES), slots)
        comb_out[:, at] = jnp.where(lane == own_spot, own_share, 0.0).astype(BF)

    count = picked.shape[0]

    def visit(p, carry):
        for b in range(count):
            for copy in copies(p * count + b):
                copy.wait()
        for b in range(count):
            pick(p * count + b, b)
        for b in range(count):
            multiply(p * count + b, b)
        return carry

    lax.fori_loop(0, held // count, visit, 0)


def expert_up(k, chunks, experts, token_at, xs, gate_proj, up_proj, sums, place, e0):
    held = gate_proj.shape[0]
    width = gate_proj.shape[1] // chunks
    tokens = sum(x.shape[0] for x in xs)
    slots = token_at.shape[1]
    units = gate_proj.shape[2]
    first, last = k == 0, k == chunks - 1
    vmem = pl.BlockSpec(memory_space=pltpu.VMEM)
    hbm = pl.BlockSpec(memory_space=pltpu.HBM)
    in_specs = [pl.BlockSpec(memory_space=pltpu.SMEM)] + [vmem] * len(xs) + [hbm, hbm]
    args = [token_at, *xs, *in_hbm(gate_proj, up_proj)]
    pair = 2 if held % 2 == 0 else 1
    scratch = [
        pltpu.VMEM((tokens * width // LANES, LANES), F32),
        pltpu.VMEM((pair, slots * width // LANES, LANES), F32),
        pltpu.VMEM((held, width, units), BF),
        pltpu.VMEM((held, width, units), BF),
        pltpu.SemaphoreType.DMA((2, held)),
    ]
    aliases = {}
    if not first:
        if not last:
            aliases = {len(args): 0, len(args) + 1: 1}
        in_specs += [vmem] * 2
        args += list(sums)
    if last:
        in_specs += [vmem, pl.BlockSpec(memory_space=pltpu.SMEM)]
        args += [place, e0]
        out_shape = (
            jax.ShapeDtypeStruct((held, slots, units), BF),
            jax.ShapeDtypeStruct((tokens, held * slots), BF),
        )
        lanes = gate_lanes(experts)
        scratch += [pltpu.VMEM((pair, slots, lanes), F32), pltpu.VMEM((tokens, lanes), F32)]
    else:
        out_shape = (jax.ShapeDtypeStruct((held, slots, units), F32),) * 2
    return pl.pallas_call(
        functools.partial(up_body, first, last, k * width, len(xs), width, experts),
        in_specs=in_specs,
        out_specs=(vmem, vmem),
        out_shape=out_shape,
        scratch_shapes=scratch,
        input_output_aliases=aliases,
        compiler_params=pltpu.CompilerParams(vmem_limit_bytes=4 * held * width * units + 4 * tokens * width + (6 << 20)),
        cost_estimate=pl.CostEstimate(
            flops=4 * held * slots * width * units,
            transcendentals=0,
            bytes_accessed=4 * held * width * units,
        ),
    )(*args)


def down_body(begin, act, comb, wd, keep, send, halves, held_rows, arrived):
    held, slots, _ = act.shape
    width = keep.shape[1]

    def copy(q):
        return pltpu.make_async_copy(
            wd.at[q, :, pl.ds(begin, width)], held_rows.at[q], arrived.at[q]
        )

    for q in range(held):
        copy(q).start()
    for q in range(held):
        copy(q).wait()
        halves[q * slots : (q + 1) * slots] = jnp.dot(
            act[q], held_rows[q], preferred_element_type=F32
        ).astype(BF)
    kept = keep.shape[0]
    block = min(width, 256)
    for j in range(0, width, block):
        cut = slice(j, j + block)
        total = jnp.dot(comb[...], halves[:, cut], preferred_element_type=F32)
        keep[:, cut] = total[:kept]
        send[:, cut] = total[kept:].astype(BF)


def expert_down(k, chunks, act, comb, down_proj, kept):
    held, slots, units = act.shape
    tokens = comb.shape[0]
    width = down_proj.shape[2] // chunks
    vmem = pl.BlockSpec(memory_space=pltpu.VMEM)
    return pl.pallas_call(
        functools.partial(down_body, k * width),
        in_specs=[vmem, vmem, pl.BlockSpec(memory_space=pltpu.HBM)],
        out_specs=(vmem, vmem),
        out_shape=(
            jax.ShapeDtypeStruct((kept, width), F32),
            jax.ShapeDtypeStruct((tokens - kept, width), BF),
        ),
        scratch_shapes=[
            pltpu.VMEM((held * slots, width), BF),
            pltpu.VMEM((held, units, width), BF),
            pltpu.SemaphoreType.DMA((held,)),
        ],
        compiler_params=pltpu.CompilerParams(vmem_limit_bytes=2 * held * width * (units + slots) + (8 << 20)),
        cost_estimate=pl.CostEstimate(
            flops=2 * held * slots * width * (tokens + units),
            transcendentals=0,
            bytes_accessed=2 * held * width * units,
        ),
    )(act, comb, *in_hbm(down_proj))


def layer(
    ssm_input,
    write_vec,
    read_vec,
    step_raw,
    step_bias,
    decay_rate,
    skip_gain,
    cache_state,
    parents,
    out_proj,
    residual,
    norm_gain,
    router,
    expert_ids,
    gate_proj,
    up_proj,
    down_proj,
):
    _, requests, _ = ssm_input.shape
    local_nodes, _, width = residual.shape
    tokens = local_nodes * requests
    topk = expert_ids.shape[2]
    experts = router.shape[1]
    held = gate_proj.shape[0]
    ring = Ring(lax.axis_size("head"), lax.axis_size("req"))
    cores, ys, reqs = ring.cores, ring.ys, ring.reqs
    head_at = lax.axis_index("head")
    y_at, c_at = head_at // cores, head_at % cores
    device = head_at * reqs + lax.axis_index("req")
    e0 = ((device * held) % experts).reshape(1).astype(jnp.int32)

    states = write_vec.shape[2]
    early = jnp.concatenate(
        [write_vec.reshape(tokens, states), read_vec.reshape(tokens, states)], axis=1
    )
    early = ring.gather(ring.gather(early, "dc"), "dy")
    early = early.reshape(ys * cores, tokens, -1)
    absolute = jnp.arange(ys * cores, dtype=jnp.int32)
    slot_of = ((y_at - absolute // cores) % ys) * cores + (c_at - absolute % cores) % cores
    slots = jnp.arange(cores * ys, dtype=jnp.int32)
    goes_to = ((y_at - slots % ys) % ys) * cores + (c_at - slots // ys) % cores
    factor, grown, named = prepare(parents, expert_ids, step_raw, step_bias, decay_rate, experts)
    near_rows = ys * tokens

    all_tokens = cores * ys * reqs * tokens
    capacity = 2 * tokens * topk // (experts + experts // 4)
    room = capacity * cores * ys * reqs

    rows_left = residual.reshape(tokens, width)
    mixes = []
    span = width // AG_CHUNKS
    for m, (low, high) in enumerate(MIX_PARTS):
        begin, part_span = low * span, (high - low) * span
        cut = slice(begin, begin + part_span)
        if m == 0:
            mixed, away, mixed_rows = front(
                early, ssm_input, cache_state, factor, grown, skip_gain, out_proj,
                slot_of, goes_to, near_rows, begin, part_span,
            )
        else:
            mixed, away = project(mixed_rows, out_proj, near_rows, begin, part_span)
        if cores > 1:
            mixed = ring.scatter([away], mixed, "dc")
        mixed = mixed.reshape(ys, tokens, part_span)
        mixed = ring.scatter([mixed[s].astype(BF) for s in range(1, ys)], mixed[0], "dy")
        mixes.append((rows_left[:, cut].astype(F32) + mixed).astype(BF))
    after_mixer = jnp.concatenate(mixes, axis=1)
    moved = {}
    for members in Z_GROUPS:
        parts = []
        for k in members:
            cut = slice(k * span, (k + 1) * span)
            m = [low <= k < high for low, high in MIX_PARTS].index(True)
            local = slice((k - MIX_PARTS[m][0]) * span, (k + 1 - MIX_PARTS[m][0]) * span)
            parts.append((mixes[m][:, local].astype(F32) * norm_gain[cut]).astype(BF))
            if k == AG_CHUNKS - 1:
                parts.append(gates(after_mixer, norm_gain, router, named))
            if k == 0:
                parts.append(named)
        payload = jnp.concatenate(parts, axis=1) if len(parts) > 1 else parts[0]
        rows = ring.gather_z(payload)
        done = 0
        for k in members:
            wide = span
            if k == 0:
                wide += named.shape[1]
            if k == AG_CHUNKS - 1:
                wide += gate_lanes(experts)
            moved[k] = rows[..., done : done + wide]
            done += wide
    sums = None
    for k in range(AG_CHUNKS):
        rows = moved[k]
        rows = ring.gather(rows, "dy")
        rows = rows.reshape(all_tokens // cores, -1)
        xs = [rows]
        if cores > 1:
            xs.append(ring.shift(rows, dc=1))
        if k == 0:
            token_at, place = places(e0, xs, span, held, room)
        sums = expert_up(k, AG_CHUNKS, experts, token_at, xs, gate_proj, up_proj, sums, place, e0)
    act, comb = sums

    pieces = []
    span = width // RS_CHUNKS
    for k in range(RS_CHUNKS):
        keep, send = expert_down(k, RS_CHUNKS, act, comb, down_proj, ys * reqs * tokens)
        total = ring.scatter([send], keep, "dc") if cores > 1 else keep
        total = total.reshape(ys, reqs * tokens, span)
        total = ring.scatter([total[s].astype(BF) for s in range(1, ys)], total[0], "dy")
        total = ring.scatter_z(total.reshape(reqs, tokens, span))
        cut = slice(k * span, (k + 1) * span)
        pieces.append((after_mixer[:, cut].astype(F32) + total).astype(BF))
    return jnp.concatenate(pieces, axis=1).reshape(local_nodes, requests, width)


def solution(mesh):
    in_specs = (
        P(None, ("groups", "req"), "head"),
        P("head", ("groups", "req"), None),
        P("head", ("groups", "req"), None),
        P(None, ("groups", "req"), "head"),
        P("head"),
        P("head"),
        P("head"),
        P(("groups", "req"), "head", None, None),
        P(("groups", "req"), None),
        P("head", None),
        P("head", ("groups", "req"), None),
        P(),
        P(),
        P("head", ("groups", "req"), None),
        P(("head", "req"), None, None),
        P(("head", "req"), None, None),
        P(("head", "req"), None, None),
    )
    out_specs = P("head", ("groups", "req"), None)
    return jax.shard_map(layer, mesh=mesh, in_specs=in_specs, out_specs=out_specs, check_vma=False)
```

```python
import functools
import jax
import jax.numpy as jnp
from jax import lax
from jax.experimental import pallas as pl
from jax.experimental.pallas import tpu as pltpu
from jax.sharding import PartitionSpec as P


BF = jnp.bfloat16
F32 = jnp.float32
AXES = ("head", "req")
LANES = 128
MIX_PARTS = ((0, 1), (1, 4))
AG_CHUNKS = 4
RS_PARTS = (1, 1, 1, 1)
BATCH = 16
Z_GROUPS = ((0,), (1,), (2, 3))


def in_hbm(*arrays):
    return [pltpu.with_memory_space_constraint(a, pltpu.HBM) for a in arrays]


class Ring:
    def __init__(self, heads, reqs):
        self.heads, self.reqs = heads, reqs
        self.cores = 2 if heads % 2 == 0 else 1
        self.ys = heads // self.cores

    def pairs(self, dy=0, dc=0, dz=0, flip=0):
        found = []
        for y in range(self.ys):
            for c in range(self.cores):
                for z in range(self.reqs):
                    there = ((y + dy) % self.ys) * self.cores + (c + dc) % self.cores
                    to = (z ^ flip) if flip else (z + dz) % self.reqs
                    found.append(((y * self.cores + c) * self.reqs + z, there * self.reqs + to))
        return found

    def shift(self, x, **how):
        return lax.ppermute(x, AXES, self.pairs(**how))

    def flips(self):
        if self.reqs & (self.reqs - 1):
            return None
        return [1 << b for b in range(self.reqs.bit_length() - 1)]

    def gather_z(self, x):
        flips = self.flips()
        if flips is None:
            return self.gather(x, "dz")
        for flip in reversed(flips):
            x = jnp.stack([x, self.shift(x, flip=flip)])
        return x

    def scatter_z(self, total):
        flips = self.flips()
        if flips is None:
            parts = [total[s].astype(BF) for s in range(1, self.reqs)]
            return self.scatter(parts, total[0], "dz")
        for flip in flips:
            half = total.shape[0] // 2
            sent = self.shift(total[half:].astype(BF), flip=flip)
            total = total[:half] + sent.astype(F32)
        return total[0]

    def gather(self, x, axis):
        count = {"dc": self.cores, "dy": self.ys, "dz": self.reqs}[axis]
        moved = [self.shift(x, **{axis: s}) for s in range(1, count)]
        return jnp.stack([x] + moved)

    def scatter(self, parts, keep, axis):
        total = keep
        for s, part in enumerate(parts, 1):
            total = total + self.shift(part, **{axis: -s}).astype(F32)
        return total


def prep_body(heads, parents, ids, step_raw, bias, decay, factor, grown, named):
    reqs, nodes = parents.shape
    rows = nodes * reqs
    lane = lax.broadcasted_iota(jnp.int32, (rows, rows), 1)
    row = lax.broadcasted_iota(jnp.int32, (rows, rows), 0)
    hop = jnp.concatenate([parents[:, j : j + 1] for j in range(nodes)], axis=0)
    at = jnp.where(hop >= 0, hop * reqs + lax.broadcasted_iota(jnp.int32, hop.shape, 0) % reqs, -1)
    power = jnp.where(at == lane, 1.0, 0.0)
    reach = jnp.where(row == lane, 1.0, 0.0) + power
    power = power.astype(BF)
    span = 2
    while span * reqs < rows:
        power = jnp.dot(power, power, preferred_element_type=F32).astype(BF)
        reach = reach + jnp.dot(reach.astype(BF), power, preferred_element_type=F32)
        span *= 2
    raw = step_raw[...].reshape(rows, heads) + bias[...]
    step = jnp.maximum(raw, 0.0) + jnp.log1p(jnp.exp(-jnp.abs(raw)))
    rate = -step * decay[...]
    blank = jnp.zeros((rows, rows - heads), F32)
    wide_step = jnp.concatenate([step, blank], axis=1)
    wide_rate = jnp.concatenate([rate, blank], axis=1)
    depth = jnp.dot(
        reach, wide_rate, preferred_element_type=F32, precision=lax.Precision.HIGHEST
    )
    grown[...] = jnp.exp(depth[:, :heads])
    depth_t = depth.T
    step_t = wide_step.T
    linked = reach > 0
    for h in range(heads):
        spread = jnp.where(linked, depth[:, h : h + 1] - depth_t[h : h + 1, :], 0.0)
        factor[h] = jnp.where(linked, jnp.exp(spread) * step_t[h : h + 1, :], 0.0)
    chosen = ids[...].reshape(named.shape[0], ids.shape[2])
    label = lax.broadcasted_iota(jnp.int32, named.shape, 1)
    mask = jnp.zeros(named.shape, F32)
    for k in range(ids.shape[2]):
        mask = jnp.where(chosen[:, k : k + 1] == label, 1.0, mask)
    named[...] = mask.astype(BF)


def prepare(parents, expert_ids, step_raw, step_bias, decay_rate, experts):
    nodes, reqs, heads = step_raw.shape
    rows = nodes * reqs
    tokens = expert_ids.shape[0] * expert_ids.shape[1]
    lanes = -(-experts // LANES) * LANES
    return pl.pallas_call(
        functools.partial(prep_body, heads),
        out_shape=(
            jax.ShapeDtypeStruct((heads, rows, rows), F32),
            jax.ShapeDtypeStruct((rows, heads), F32),
            jax.ShapeDtypeStruct((tokens, lanes), BF),
        ),
        compiler_params=pltpu.CompilerParams(vmem_limit_bytes=16 << 20),
        name="prepare",
    )(
        *in_hbm(
            parents, expert_ids, step_raw, step_bias.reshape(1, heads), decay_rate.reshape(1, heads)
        ),
    )


def gate_body(experts, after, gain, router_t, named, out):
    tokens, width = after.shape
    lanes = out.shape[1]
    wide = after[...].astype(F32)
    scale = lax.rsqrt(jnp.sum(wide * wide, axis=1, keepdims=True) / width + 1e-05)
    normed = (wide * scale * gain[...]).astype(BF)
    logits = lax.dot_general(
        normed, router_t[...], (((1,), (1,)), ((), ())), preferred_element_type=F32
    )
    powered = jnp.where(named[:, :experts] > 0, jnp.exp(logits), 0.0)
    gate = powered / jnp.sum(powered, axis=1, keepdims=True)
    top = scale.astype(BF).astype(F32)
    middle = (scale - top).astype(BF).astype(F32)
    low = scale - top - middle
    lane = lax.broadcasted_iota(jnp.int32, (tokens, lanes - experts), 1)
    head = jnp.where(lane == 0, top, jnp.where(lane == 1, middle, jnp.where(lane == 2, low, 0.0)))
    out[...] = jnp.concatenate([head, gate], axis=1).astype(BF)


def gate_lanes(experts):
    return -(-(experts + 3) // LANES) * LANES


def gates(after_mixer, norm_gain, router, named):
    tokens, width = after_mixer.shape
    experts = router.shape[1]
    return pl.pallas_call(
        functools.partial(gate_body, experts),
        out_shape=jax.ShapeDtypeStruct((tokens, gate_lanes(experts)), BF),
        compiler_params=pltpu.CompilerParams(vmem_limit_bytes=16 << 20),
        name="gates",
    )(after_mixer, norm_gain.reshape(1, width), router.T, named.astype(F32))


def project_blocks(rows, weight, held, arrived, first, near, far):
    near_rows = near.shape[0]
    block = held.shape[2]
    for b in range(held.shape[0]):
        weight_copy(weight, held, arrived, first, b).wait()
        total = jnp.dot(rows, held[b], preferred_element_type=F32)
        near[:, b * block : (b + 1) * block] = total[:near_rows]
        far[:, b * block : (b + 1) * block] = total[near_rows:].astype(BF)


def weight_copy(weight, held, arrived, first, b):
    block = held.shape[2]
    return pltpu.make_async_copy(
        weight.at[:, pl.ds(first + b * block, block)], held.at[b], arrived.at[b]
    )


def front_body(
    heads, first, slot_of, goes_to, early, x, state, factor, grown, skip, weight,
    near, far, mixed_rows, read_rows, write_rows, cache, result, states_held, states_in, held, arrived,
):
    blocks, tokens = early.shape[0], early.shape[1]
    nodes, reqs, columns = x.shape
    rows = nodes * reqs
    size = columns // heads
    states = state.shape[2]
    for r in range(reqs):
        pltpu.make_async_copy(state.at[r], states_held.at[r], states_in.at[r]).start()
    for b in range(held.shape[0]):
        weight_copy(weight, held, arrived, first, b).start()
    for a in range(blocks):
        block = early[slot_of[a]].astype(F32)
        write_rows[a * tokens : (a + 1) * tokens] = block[:, :states]
        read_rows[a * tokens : (a + 1) * tokens] = block[:, states : 2 * states]
    writes = write_rows[...].astype(BF)
    reads = read_rows[...].astype(BF)
    affinity = lax.dot_general(
        reads, writes, (((1,), (1,)), ((), ())), preferred_element_type=F32
    )
    for r in range(reqs):
        pltpu.make_async_copy(state.at[r], states_held.at[r], states_in.at[r]).wait()
        mine = read_rows[pl.ds(r, nodes, stride=reqs), :].astype(BF)
        got = lax.dot_general(
            mine, states_held[r], (((1,), (1,)), ((), ())), preferred_element_type=F32
        )
        for i in range(columns // LANES):
            cache.at[i][pl.ds(r, nodes, stride=reqs), :] = got[:, i * LANES : (i + 1) * LANES]
    values = x[...].reshape(rows, columns)
    pair = 2 * size
    left = lax.broadcasted_iota(jnp.int32, (rows, pair), 1) < size
    for h in range(0, heads, 2):
        cut = slice(h * size, h * size + pair)
        own = values[:, cut]
        one = (factor[h] * affinity).astype(BF)
        two = (factor[h + 1] * affinity).astype(BF)
        zero = jnp.zeros_like(own)
        both = jnp.dot(
            jnp.concatenate([one, two], axis=1),
            jnp.concatenate([jnp.where(left, own, zero), jnp.where(left, zero, own)], axis=0),
            preferred_element_type=F32,
        )
        grow = jnp.where(left, grown[:, h : h + 1], grown[:, h + 1 : h + 2])
        gain = jnp.where(left, skip[:, h : h + 1], skip[:, h + 1 : h + 2])
        both = both + cache[h * size // LANES] * grow + gain * own.astype(F32)
        result[:, cut] = both.astype(BF).astype(F32)
    for s in range(blocks):
        start = pl.multiple_of(goes_to[s] * tokens, tokens)
        mixed_rows[s * tokens : (s + 1) * tokens] = result[pl.ds(start, tokens)].astype(BF)
    project_blocks(mixed_rows[...], weight, held, arrived, first, near, far)


def weight_scratch(columns, span):
    block = min(span, 512)
    return [
        pltpu.VMEM((span // block, columns, block), BF),
        pltpu.SemaphoreType.DMA((span // block,)),
    ]


def front(early, x, state, factor, grown, skip_gain, out_proj, slot_of, goes_to, near_rows, begin, span):
    nodes, reqs, columns = x.shape
    heads = skip_gain.shape[0]
    rows = nodes * reqs
    states = state.shape[3]
    state = state.reshape(state.shape[0], columns, states)
    skip = skip_gain.reshape(1, heads)
    x, state, skip, out_proj = in_hbm(x, state, skip, out_proj)
    vmem = pl.BlockSpec(memory_space=pltpu.VMEM)
    hbm = pl.BlockSpec(memory_space=pltpu.HBM)
    return pl.pallas_call(
        functools.partial(front_body, heads, begin),
        grid_spec=pltpu.PrefetchScalarGridSpec(
            num_scalar_prefetch=2,
            in_specs=[vmem, vmem, hbm, vmem, vmem, vmem, hbm],
            out_specs=(vmem, vmem, vmem),
            scratch_shapes=[
                pltpu.VMEM((rows, states), F32),
                pltpu.VMEM((rows, states), F32),
                pltpu.VMEM((columns // LANES, rows, LANES), F32),
                pltpu.VMEM((rows, columns), F32),
                pltpu.VMEM(state.shape, BF),
                pltpu.SemaphoreType.DMA((reqs,)),
                *weight_scratch(columns, span),
            ],
        ),
        out_shape=(
            jax.ShapeDtypeStruct((near_rows, span), F32),
            jax.ShapeDtypeStruct((rows - near_rows, span), BF),
            jax.ShapeDtypeStruct((rows, columns), BF),
        ),
        compiler_params=pltpu.CompilerParams(vmem_limit_bytes=16 << 20),
        cost_estimate=pl.CostEstimate(
            flops=2 * rows * columns * span, transcendentals=0, bytes_accessed=2 * columns * span
        ),
        name="front",
    )(slot_of, goes_to, early, x, state, factor, grown, skip, out_proj)


def project_body(first, rows, weight, near, far, held, arrived):
    for b in range(held.shape[0]):
        weight_copy(weight, held, arrived, first, b).start()
    project_blocks(rows[...], weight, held, arrived, first, near, far)


def project(rows, out_proj, near_rows, begin, span):
    count, columns = rows.shape
    vmem = pl.BlockSpec(memory_space=pltpu.VMEM)
    return pl.pallas_call(
        functools.partial(project_body, begin),
        in_specs=[vmem, pl.BlockSpec(memory_space=pltpu.HBM)],
        out_specs=(vmem, vmem),
        out_shape=(
            jax.ShapeDtypeStruct((near_rows, span), F32),
            jax.ShapeDtypeStruct((count - near_rows, span), BF),
        ),
        scratch_shapes=weight_scratch(columns, span),
        compiler_params=pltpu.CompilerParams(vmem_limit_bytes=10 << 20),
        cost_estimate=pl.CostEstimate(
            flops=2 * count * columns * span, transcendentals=0, bytes_accessed=2 * columns * span
        ),
        name="project",
    )(rows, *in_hbm(out_proj))


def own_columns(lanes, first, held):
    at = lax.broadcasted_iota(jnp.int32, (lanes, held), 0)
    to = lax.broadcasted_iota(jnp.int32, (lanes, held), 1)
    return jnp.where(at == to + first, 1.0, 0.0).astype(BF)


def place_body(begin, e0, *rest):
    xs, (tokens_out, place_out) = rest[:-2], rest[-2:]
    held, slots = tokens_out.shape
    named = jnp.concatenate([x[:, begin:] for x in xs], axis=0)
    count, lanes = named.shape
    mine = jnp.dot(
        named, own_columns(lanes, e0[0], held), preferred_element_type=F32
    )
    row = lax.broadcasted_iota(jnp.int32, (count, count), 0)
    column = lax.broadcasted_iota(jnp.int32, (count, count), 1)
    before = jnp.where(row > column, 1.0, 0.0).astype(BF)
    rank = jnp.dot(before, mine.astype(BF), preferred_element_type=F32)
    place = jnp.where(mine > 0, rank, -1.0)
    place_out[...] = place
    spot = lax.broadcasted_iota(jnp.int32, (count, slots), 1).astype(F32)
    token = lax.broadcasted_iota(jnp.int32, (count, slots), 0).astype(F32)
    for q in range(held):
        here = jnp.where(spot == place[:, q : q + 1], token, 0.0)
        tokens_out[q : q + 1] = jnp.sum(here, axis=0, keepdims=True).astype(jnp.int32)


def places(e0, xs, begin, held, slots):
    tokens = sum(x.shape[0] for x in xs)
    return pl.pallas_call(
        functools.partial(place_body, begin),
        in_specs=[pl.BlockSpec(memory_space=pltpu.SMEM)]
        + [pl.BlockSpec(memory_space=pltpu.VMEM)] * len(xs),
        out_shape=(
            jax.ShapeDtypeStruct((held, slots), jnp.int32),
            jax.ShapeDtypeStruct((tokens, held), F32),
        ),
        compiler_params=pltpu.CompilerParams(vmem_limit_bytes=10 << 20),
        name="places",
    )(e0, *xs)


def up_body(first, last, begin, pieces, width, experts, token_at, *rest):
    rest = list(rest)
    xs = [rest.pop(0) for _ in range(pieces)]
    wg, wu = rest.pop(0), rest.pop(0)
    if not first:
        gin, uin = rest.pop(0), rest.pop(0)
    if last:
        spot, e0 = rest.pop(0), rest.pop(0)
        act_out, comb_out, spread, picked, gates_held, ups_held, arrived, scales, extra = rest
    else:
        gout, uout, spread, picked, gates_held, ups_held, arrived = rest
    held = gates_held.shape[0]
    tall = width // LANES
    slots = picked.shape[1] // tall

    def copies(e):
        cut = pl.ds(begin, width)
        return (
            pltpu.make_async_copy(wg.at[e, cut], gates_held.at[e], arrived.at[0, e]),
            pltpu.make_async_copy(wu.at[e, cut], ups_held.at[e], arrived.at[1, e]),
        )

    for e in range(held):
        for copy in copies(e):
            copy.start()
    done = 0
    for x in xs:
        tokens = x.shape[0]
        for i in range(tall):
            spread[pl.ds(done * tall + i, tokens, stride=tall), :] = x[
                :, i * LANES : (i + 1) * LANES
            ].astype(F32)
        if last:
            extra[done : done + tokens] = x[:, width:].astype(F32)
        done += tokens
    if last:
        lanes = extra.shape[1]
        share = jnp.dot(
            extra[...].astype(BF),
            own_columns(lanes, e0[0] + lanes - experts, held),
            preferred_element_type=F32,
        )

    def pick(q, b):
        for c in range(0, slots, BATCH):
            at = [token_at[q, c + i] for i in range(BATCH)]
            got = [spread[pl.ds(pl.multiple_of(t * tall, tall), tall)] for t in at]
            picked[b, c * tall : (c + BATCH) * tall] = jnp.concatenate(got, axis=0)
            if last:
                got = [extra[pl.ds(t, 1)] for t in at]
                for i in range(BATCH):
                    scales[b, c + i : c + i + 1] = got[i]

    def multiply(q, b):
        half = picked.at[b]
        rows = jnp.concatenate(
            [half[pl.ds(i, slots, stride=tall), :].astype(BF) for i in range(tall)], axis=1
        )
        gated = jnp.dot(rows, gates_held[q], preferred_element_type=F32)
        lifted = jnp.dot(rows, ups_held[q], preferred_element_type=F32)
        if not first:
            gated = gated + gin[q]
            lifted = lifted + uin[q]
        if not last:
            gout[q] = gated
            uout[q] = lifted
            return
        scale = scales[b, :, 0:1] + scales[b, :, 1:2] + scales[b, :, 2:3]
        gated = gated * scale
        lifted = lifted * scale
        act_out[q] = (gated / (1.0 + jnp.exp(-gated)) * lifted).astype(BF)
        lane = lax.broadcasted_iota(jnp.int32, (done, slots), 1).astype(F32)
        here = lane == spot[:, q : q + 1]
        comb_out[:, q * slots : (q + 1) * slots] = jnp.where(
            here, share[:, q : q + 1], 0.0
        ).astype(BF)

    count = picked.shape[0]

    def visit(p, carry):
        for b in range(count):
            for copy in copies(p * count + b):
                copy.wait()
        for b in range(count):
            pick(p * count + b, b)
        for b in range(count):
            multiply(p * count + b, b)
        return carry

    if last:
        for p in range(held // count):
            visit(p, 0)
    else:
        lax.fori_loop(0, held // count, visit, 0)


def expert_up(k, chunks, experts, token_at, xs, gate_proj, up_proj, sums, place, e0):
    held = gate_proj.shape[0]
    width = gate_proj.shape[1] // chunks
    tokens = sum(x.shape[0] for x in xs)
    slots = token_at.shape[1]
    units = gate_proj.shape[2]
    first, last = k == 0, k == chunks - 1
    vmem = pl.BlockSpec(memory_space=pltpu.VMEM)
    hbm = pl.BlockSpec(memory_space=pltpu.HBM)
    in_specs = [pl.BlockSpec(memory_space=pltpu.SMEM)] + [vmem] * len(xs) + [hbm, hbm]
    args = [token_at, *xs, *in_hbm(gate_proj, up_proj)]
    pair = 2 if held % 2 == 0 else 1
    scratch = [
        pltpu.VMEM((tokens * width // LANES, LANES), F32),
        pltpu.VMEM((pair, slots * width // LANES, LANES), F32),
        pltpu.VMEM((held, width, units), BF),
        pltpu.VMEM((held, width, units), BF),
        pltpu.SemaphoreType.DMA((2, held)),
    ]
    aliases = {}
    if not first:
        if not last:
            aliases = {len(args): 0, len(args) + 1: 1}
        in_specs += [vmem] * 2
        args += list(sums)
    if last:
        in_specs += [vmem, pl.BlockSpec(memory_space=pltpu.SMEM)]
        args += [place, e0]
        out_shape = (
            jax.ShapeDtypeStruct((held, slots, units), BF),
            jax.ShapeDtypeStruct((tokens, held * slots), BF),
        )
        lanes = gate_lanes(experts)
        scratch += [pltpu.VMEM((pair, slots, lanes), F32), pltpu.VMEM((tokens, lanes), F32)]
    else:
        out_shape = (jax.ShapeDtypeStruct((held, slots, units), F32),) * 2
    return pl.pallas_call(
        functools.partial(up_body, first, last, k * width, len(xs), width, experts),
        in_specs=in_specs,
        out_specs=(vmem, vmem),
        out_shape=out_shape,
        scratch_shapes=scratch,
        input_output_aliases=aliases,
        compiler_params=pltpu.CompilerParams(vmem_limit_bytes=4 * held * width * units + 4 * tokens * width + (6 << 20)),
        cost_estimate=pl.CostEstimate(
            flops=4 * held * slots * width * units,
            transcendentals=0,
            bytes_accessed=4 * held * width * units,
        ),
    )(*args)


def down_body(begin, act, comb, wd, keep, send, halves, held_rows, arrived):
    held, slots, _ = act.shape
    width = keep.shape[1]

    def copy(q):
        return pltpu.make_async_copy(
            wd.at[q, :, pl.ds(begin, width)], held_rows.at[q], arrived.at[q]
        )

    for q in range(held):
        copy(q).start()
    for q in range(held):
        copy(q).wait()
        halves[q * slots : (q + 1) * slots] = jnp.dot(
            act[q], held_rows[q], preferred_element_type=F32
        ).astype(BF)
    kept = keep.shape[0]
    block = min(width, 256)
    for j in range(0, width, block):
        cut = slice(j, j + block)
        total = jnp.dot(comb[...], halves[:, cut], preferred_element_type=F32)
        keep[:, cut] = total[:kept]
        send[:, cut] = total[kept:].astype(BF)


def expert_down(begin, width, act, comb, down_proj, kept):
    held, slots, units = act.shape
    tokens = comb.shape[0]
    vmem = pl.BlockSpec(memory_space=pltpu.VMEM)
    return pl.pallas_call(
        functools.partial(down_body, begin),
        in_specs=[vmem, vmem, pl.BlockSpec(memory_space=pltpu.HBM)],
        out_specs=(vmem, vmem),
        out_shape=(
            jax.ShapeDtypeStruct((kept, width), F32),
            jax.ShapeDtypeStruct((tokens - kept, width), BF),
        ),
        scratch_shapes=[
            pltpu.VMEM((held * slots, width), BF),
            pltpu.VMEM((held, units, width), BF),
            pltpu.SemaphoreType.DMA((held,)),
        ],
        compiler_params=pltpu.CompilerParams(vmem_limit_bytes=2 * held * width * (units + slots) + (8 << 20)),
        cost_estimate=pl.CostEstimate(
            flops=2 * held * slots * width * (tokens + units),
            transcendentals=0,
            bytes_accessed=2 * held * width * units,
        ),
    )(act, comb, *in_hbm(down_proj))


def layer(
    ssm_input,
    write_vec,
    read_vec,
    step_raw,
    step_bias,
    decay_rate,
    skip_gain,
    cache_state,
    parents,
    out_proj,
    residual,
    norm_gain,
    router,
    expert_ids,
    gate_proj,
    up_proj,
    down_proj,
):
    _, requests, _ = ssm_input.shape
    local_nodes, _, width = residual.shape
    tokens = local_nodes * requests
    topk = expert_ids.shape[2]
    experts = router.shape[1]
    held = gate_proj.shape[0]
    ring = Ring(lax.axis_size("head"), lax.axis_size("req"))
    cores, ys, reqs = ring.cores, ring.ys, ring.reqs
    head_at = lax.axis_index("head")
    y_at, c_at = head_at // cores, head_at % cores
    device = head_at * reqs + lax.axis_index("req")
    e0 = ((device * held) % experts).reshape(1).astype(jnp.int32)

    states = write_vec.shape[2]
    early = jnp.concatenate(
        [write_vec.reshape(tokens, states), read_vec.reshape(tokens, states)], axis=1
    )
    early = jnp.stack(
        [
            ring.shift(early, dy=sy, dc=sc) if sy + sc else early
            for sy in range(ys)
            for sc in range(cores)
        ]
    )
    absolute = jnp.arange(ys * cores, dtype=jnp.int32)
    slot_of = ((y_at - absolute // cores) % ys) * cores + (c_at - absolute % cores) % cores
    slots = jnp.arange(cores * ys, dtype=jnp.int32)
    goes_to = ((y_at - slots % ys) % ys) * cores + (c_at - slots // ys) % cores
    factor, grown, named = prepare(parents, expert_ids, step_raw, step_bias, decay_rate, experts)
    near_rows = ys * tokens

    all_tokens = cores * ys * reqs * tokens
    capacity = 2 * tokens * topk // (experts + experts // 4)
    room = capacity * cores * ys * reqs

    rows_left = residual.reshape(tokens, width)
    mixes = []
    span = width // AG_CHUNKS
    for m, (low, high) in enumerate(MIX_PARTS):
        begin, part_span = low * span, (high - low) * span
        cut = slice(begin, begin + part_span)
        if m == 0:
            mixed, away, mixed_rows = front(
                early, ssm_input, cache_state, factor, grown, skip_gain, out_proj,
                slot_of, goes_to, near_rows, begin, part_span,
            )
        else:
            mixed, away = project(mixed_rows, out_proj, near_rows, begin, part_span)
        if cores > 1:
            mixed = ring.scatter([away], mixed, "dc")
        mixed = mixed.reshape(ys, tokens, part_span)
        mixed = ring.scatter([mixed[s].astype(BF) for s in range(1, ys)], mixed[0], "dy")
        mixes.append((rows_left[:, cut].astype(F32) + mixed).astype(BF))
    after_mixer = jnp.concatenate(mixes, axis=1)
    moved = {}
    for members in Z_GROUPS:
        parts = []
        for k in members:
            cut = slice(k * span, (k + 1) * span)
            m = [low <= k < high for low, high in MIX_PARTS].index(True)
            local = slice((k - MIX_PARTS[m][0]) * span, (k + 1 - MIX_PARTS[m][0]) * span)
            parts.append((mixes[m][:, local].astype(F32) * norm_gain[cut]).astype(BF))
            if k == AG_CHUNKS - 1:
                parts.append(gates(after_mixer, norm_gain, router, named))
            if k == 0:
                parts.append(named)
        payload = jnp.concatenate(parts, axis=1) if len(parts) > 1 else parts[0]
        rows = ring.gather_z(payload)
        done = 0
        for k in members:
            wide = span
            if k == 0:
                wide += named.shape[1]
            if k == AG_CHUNKS - 1:
                wide += gate_lanes(experts)
            moved[k] = rows[..., done : done + wide]
            done += wide
    sums = None
    for k in range(AG_CHUNKS):
        rows = moved[k]
        rows = ring.gather(rows, "dy")
        rows = rows.reshape(all_tokens // cores, -1)
        xs = [rows]
        if cores > 1:
            xs.append(ring.shift(rows, dc=1))
        if k == 0:
            token_at, place = places(e0, xs, span, held, room)
        sums = expert_up(k, AG_CHUNKS, experts, token_at, xs, gate_proj, up_proj, sums, place, e0)
    act, comb = sums

    pieces = []
    begin = 0
    for part in RS_PARTS:
        span = width * part // sum(RS_PARTS)
        keep, send = expert_down(begin, span, act, comb, down_proj, ys * reqs * tokens)
        total = ring.scatter([send], keep, "dc") if cores > 1 else keep
        total = total.reshape(ys, reqs * tokens, span)
        total = ring.scatter([total[s].astype(BF) for s in range(1, ys)], total[0], "dy")
        total = ring.scatter_z(total.reshape(reqs, tokens, span))
        cut = slice(begin, begin + span)
        begin += span
        pieces.append((after_mixer[:, cut].astype(F32) + total).astype(BF))
    return jnp.concatenate(pieces, axis=1).reshape(local_nodes, requests, width)


def solution(mesh):
    in_specs = (
        P(None, ("groups", "req"), "head"),
        P("head", ("groups", "req"), None),
        P("head", ("groups", "req"), None),
        P(None, ("groups", "req"), "head"),
        P("head"),
        P("head"),
        P("head"),
        P(("groups", "req"), "head", None, None),
        P(("groups", "req"), None),
        P("head", None),
        P("head", ("groups", "req"), None),
        P(),
        P(),
        P("head", ("groups", "req"), None),
        P(("head", "req"), None, None),
        P(("head", "req"), None, None),
        P(("head", "req"), None, None),
    )
    out_specs = P("head", ("groups", "req"), None)
    return jax.shard_map(layer, mesh=mesh, in_specs=in_specs, out_specs=out_specs, check_vma=False)
```
